256 devices in a mesh: dp: 8 (over y, core), row: 16 (over x_hi, z), view: 2 (over x_lo).
Axes of the slice: x: 4 (x_hi: 2, x_lo: 2; x = x_hi * 2 + x_lo), y: 4, z: 8, core: 2. Of those that a mesh axis runs over, the one named last changes fastest.
Arguments:
- frames_in: float32 [2, 8, 64, 64, 480], P('view', 'dp', None, 'row'), may hold values from -13 to 13
- cotangent: float32 [2, 8, 64, 64, 480], P('view', 'dp', None, 'row'), may hold values from -36 to 36
- expand_in: float32 [128, 64], replicated, may hold values from -0.75 to 0.75
- conv_kernel: float32 [128, 3, 3], replicated, may hold values from -2 to 2
- pool_proj: float32 [64, 64], replicated, may hold values from -1.5 to 1.5
- pool_bias: float32 [64], replicated, may hold values from 0.5 to 1.5
- squeeze_out: float32 [64, 64], replicated, may hold values from -0.75 to 0.75
- branch_scale: float32 [64], replicated, may hold values from 0.3 to 1
- ffn_expand: float32 [128, 64], replicated, may hold values from -0.75 to 0.75
- ffn_shrink: float32 [64, 64], replicated, may hold values from -0.75 to 0.75
- ffn_scale: float32 [64], replicated, may hold values from 0.3 to 1
- query_proj: float32 [2, 64, 64], P('view'), may hold values from -1.5 to 1.5
- value_proj: float32 [2, 64, 64], P('view'), may hold values from -0.75 to 0.75
- cross_scale: float32 [2, 64], P('view'), may hold values from 0.3 to 1
Outputs:
- block_out: float32 [2, 8, 64, 64, 480], P('view', 'dp', None, 'row')
- grad_in: float32 [2, 8, 64, 64, 480], P('view', 'dp', None, 'row')
- grad_expand: float32 [128, 64], replicated
- grad_kernel: float32 [128, 3, 3], replicated
- grad_pool: float32 [64, 64], replicated
- grad_bias: float32 [64], replicated
- grad_squeeze: float32 [64, 64], replicated
- grad_branch: float32 [64], replicated
- grad_ffn_up: float32 [128, 64], replicated
- grad_ffn_down: float32 [64, 64], replicated
- grad_ffn_scale: float32 [64], replicated
- grad_query: float32 [2, 64, 64], P('view')
- grad_value: float32 [2, 64, 64], P('view')
- grad_cross: float32 [2, 64], P('view')
The draws below stay inside these ranges and needn't reach their ends.
All inputs are finite; a program needn't handle non-finite values.
Results may differ from the reference program's by a relative error of at most 0.0003.
Values sent between devices are 32-bit elements; how exact they have to be, the bound alone decides.
A program may use at most 64 MiB of HBM per device.

```python
import jax
import jax.numpy as jnp
from jax import lax

CH = 64
COLS = 480
FRAMES = 8
HEIGHT = 64


def draw_frames_in(key, part):
    noise_key, pattern_key = jax.random.split(jax.random.fold_in(key, 11))
    shape = (2, FRAMES, CH, HEIGHT, COLS)
    pattern = jnp.clip(jax.random.normal(pattern_key, (CH,), jnp.float32), -3.0, 3.0)
    ramp = jnp.arange(HEIGHT, dtype=jnp.float32) * (2.0 / max(HEIGHT - 1, 1))
    noise = jnp.clip(jax.random.normal(noise_key, shape, jnp.float32), -5.0, 5.0)
    return noise + pattern[None, None, :, None, None] * ramp[None, None, None, :, None]


def draw_cotangent(key, part):
    noise_key = jax.random.fold_in(key, 23)
    shape = (2, FRAMES, CH, HEIGHT, COLS)
    frame_rise = 1.0 + jnp.arange(FRAMES, dtype=jnp.float32) * (2.0 / max(FRAMES - 1, 1))
    row_rise = 1.0 + jnp.arange(HEIGHT, dtype=jnp.float32) * (2.0 / max(HEIGHT - 1, 1))
    noise = jnp.clip(jax.random.normal(noise_key, shape, jnp.float32), -4.0, 4.0)
    return noise * frame_rise[None, :, None, None, None] * row_rise[None, None, None, :, None]


def block_scale(stream_key, extent, shards, smallest, largest):
    def one(position, shards_of):
        steps = jax.random.uniform(jax.random.fold_in(jax.random.fold_in(stream_key, 6), position), (shards_of,), jnp.float32, smallest / len(shards), largest / len(shards))
        return jnp.repeat(jnp.exp(steps), extent[position] // shards_of).reshape((-1,) + (1,) * (len(extent) - position - 1))

    gain = one(*shards[0])
    for cut in shards[1:]:
        gain = gain * one(*cut)
    return gain


def gaussian(key, extent, scale, bound, pieces=(), kind=jnp.bfloat16):
    factor_of = block_scale(key, extent, pieces, -0.22, 0.18) if pieces else 1.0
    array = jax.random.normal(key, extent, jnp.float32) * scale * factor_of
    return jnp.minimum(jnp.maximum(array, -bound), bound).astype(kind)


def setup_inputs(seed: int = 0) -> dict:
    key_of = jax.random.split(jax.random.key(seed), 15)
    return {
        "frames_in": draw_frames_in(jax.random.fold_in(key_of[14], 71), 0),
        "cotangent": draw_cotangent(jax.random.fold_in(key_of[14], 71), 0),
        "expand_in": gaussian(key_of[2], (2 * CH, CH), CH ** -0.5, 0.75, (), jnp.float32),
        "conv_kernel": gaussian(key_of[3], (2 * CH, 3, 3), 9 ** -0.5, 2.0, (), jnp.float32),
        "pool_proj": gaussian(key_of[4], (CH, CH), (CH // 4) ** -0.5, 1.5, (), jnp.float32),
        "pool_bias": jnp.clip(1.0 + 0.1 * jax.random.normal(key_of[5], (CH,), jnp.float32), 0.5, 1.5),
        "squeeze_out": gaussian(key_of[6], (CH, CH), CH ** -0.5, 0.75, (), jnp.float32),
        "branch_scale": jnp.clip(jax.random.uniform(key_of[7], (CH,), jnp.float32, 0.3, 1.0), 0.3, 1.0),
        "ffn_expand": gaussian(key_of[8], (2 * CH, CH), CH ** -0.5, 0.75, (), jnp.float32),
        "ffn_shrink": gaussian(key_of[9], (CH, CH), CH ** -0.5, 0.75, (), jnp.float32),
        "ffn_scale": jnp.clip(jax.random.uniform(key_of[10], (CH,), jnp.float32, 0.3, 1.0), 0.3, 1.0),
        "query_proj": gaussian(key_of[11], (2, CH, CH), (CH // 4) ** -0.5, 1.5, ((0, 2),), jnp.float32),
        "value_proj": gaussian(key_of[12], (2, CH, CH), CH ** -0.5, 0.75, ((0, 2),), jnp.float32),
        "cross_scale": jnp.clip(0.3 + 0.7 * jax.random.uniform(key_of[13], (2, CH), jnp.float32) ** block_scale(key_of[13], (2, CH), ((0, 2),), -0.2, 0.2), 0.3, 1.0),
    }


epsilon = 1e-06
highest = lax.Precision.HIGHEST

def channel_norm(fields):
    center = fields - lax.optimization_barrier(jnp.mean(fields, axis=-3, keepdims=True))
    spread = lax.optimization_barrier(jnp.mean(center * center, axis=-3, keepdims=True))
    return center / jnp.sqrt(spread + epsilon)

def mixing(weight, fields):
    return jnp.einsum('oc,...chw->...ohw', weight, fields, precision=highest)

def depthwise(padded, kernel, height, breadth):
    summed = kernel[:, 0, 0][:, None, None] * padded[..., 0:height, 0:breadth]
    for offset in range(1, 9):
        row_off = offset // 3
        col_off = offset % 3
        summed = summed + kernel[:, row_off, col_off][:, None, None] * padded[..., row_off:row_off + height, col_off:col_off + breadth]
    return summed

def simple_gate(doubled):
    halves = doubled.shape[-3] // 2
    return doubled[..., :halves, :, :] * doubled[..., halves:, :, :]

def attend(hidden, queries, query_other, value_other, scales):
    scores = jnp.einsum('...chi,...chj->...hij', queries, query_other, precision=highest) * queries.shape[-3] ** (-0.5)
    weights = jnp.exp(scores)
    weights = weights / lax.optimization_barrier(jnp.sum(weights, axis=-1, keepdims=True))
    carried = jnp.einsum('...hij,...chj->...chi', weights, value_other, precision=highest)
    return hidden + scales[:, None, None] * carried

def block_tail(frames, gating, pooled, pool_proj, pool_bias, squeeze_out, branch_scale, ffn_expand, ffn_shrink, ffn_scale):
    attention = jnp.einsum('oc,...c->...o', pool_proj, pooled, precision=highest) + pool_bias
    scaled = gating * attention[..., :, None, None]
    residual_one = frames + branch_scale[:, None, None] * mixing(squeeze_out, scaled)
    expanded = mixing(ffn_expand, channel_norm(residual_one))
    return residual_one + ffn_scale[:, None, None] * mixing(ffn_shrink, simple_gate(expanded))

def one_view(frames, params):
    doubled = mixing(params[0], channel_norm(frames))
    padded = jnp.pad(doubled, ((0, 0), (1, 1), (1, 1)))
    gating = simple_gate(depthwise(padded, params[1], HEIGHT, COLS))
    pooled = lax.optimization_barrier(jnp.sum(gating, axis=(1, 2))) / (HEIGHT * COLS)
    return block_tail(frames, gating, pooled, params[2], params[3], params[4], params[5], params[6], params[7], params[8])

def frame_pair(paired, params):
    query_proj, value_proj, cross_scale = (params[9], params[10], params[11])
    hidden = [one_view(paired[view_idx], params) for view_idx in range(2)]
    queries = [mixing(query_proj[view_idx], channel_norm(hidden[view_idx])) for view_idx in range(2)]
    values = [mixing(value_proj[view_idx], hidden[view_idx]) for view_idx in range(2)]
    results = [attend(hidden[view_idx], queries[view_idx], queries[1 - view_idx], values[1 - view_idx], cross_scale[view_idx]) for view_idx in range(2)]
    return jnp.stack(results)

def reference(frames_in, cotangent, expand_in, conv_kernel, pool_proj, pool_bias, squeeze_out, branch_scale, ffn_expand, ffn_shrink, ffn_scale, query_proj, value_proj, cross_scale):
    params = (expand_in, conv_kernel, pool_proj, pool_bias, squeeze_out, branch_scale, ffn_expand, ffn_shrink, ffn_scale, query_proj, value_proj, cross_scale)

    def step_frame(carry, paired):
        inputs_now, upstream = paired
        output, backward = jax.vjp(frame_pair, inputs_now, params)
        grad_frame, grad_params = backward(upstream)
        return (jax.tree.map(jnp.add, carry, grad_params), (output, grad_frame))
    zeroes = jax.tree.map(jnp.zeros_like, params)
    inputs_all = jnp.moveaxis(frames_in, 1, 0)
    upstream_all = jnp.moveaxis(cotangent, 1, 0)
    totals, (outputs, grads_all) = lax.scan(step_frame, zeroes, (inputs_all, upstream_all))
    factor = (2 * FRAMES * HEIGHT * COLS) ** (-0.5)
    scaled = [grad_item * factor for grad_item in totals]
    return (jnp.moveaxis(outputs, 0, 1), jnp.moveaxis(grads_all, 0, 1), scaled[0], scaled[1], scaled[2], scaled[3], scaled[4], scaled[5], scaled[6], scaled[7], scaled[8], scaled[9], scaled[10], scaled[11])
```

```python
import functools

import jax
import jax.numpy as jnp
from jax import lax
from jax.experimental import pallas as pl
from jax.experimental.pallas import tpu as pltpu
from jax.sharding import PartitionSpec as P

epsilon = 1e-06
highest = lax.Precision.HIGHEST


def extended(value, sides, width):
    for axis, dim in sides:
        count, length = (lax.axis_size(axis), value.shape[dim])
        up = [(i, (i + 1) % count) for i in range(count - 1)]
        down = [(j, i) for i, j in up]
        last = lax.slice_in_dim(value, length - width, length, axis=dim)
        first = lax.slice_in_dim(value, 0, width, axis=dim)
        before = lax.ppermute(last, axis, up)
        after = lax.ppermute(first, axis, down)
        value = jnp.concatenate([before, value, after], axis=dim)
    return value


def from_everyone(value, axis):
    count = lax.axis_size(axis)
    return lax.all_to_all(
        jnp.broadcast_to(value[None], (count, *value.shape)), axis, 0, 0, tiled=True
    )


def taken_together(value, axis):
    return from_everyone(value, axis).sum(axis=0)


def partner(value, axis, distance):
    mask = 2**distance
    pairs = [(source, source ^ mask) for source in range(lax.axis_size(axis))]
    return lax.ppermute(value, axis, pairs)


def channel_norm(fields):
    center = fields - jnp.mean(fields, axis=-3, keepdims=True)
    spread = jnp.mean(center * center, axis=-3, keepdims=True)
    return center / jnp.sqrt(spread + epsilon)


def mixing(weight, fields):
    return jnp.einsum("oc,...chw->...ohw", weight, fields, precision=highest)


def depthwise(padded, kernel, height, breadth):
    summed = kernel[:, 0, 0][:, None, None] * padded[..., 0:height, 0:breadth]
    for offset in range(1, 9):
        row_off = offset // 3
        col_off = offset % 3
        summed = (
            summed
            + kernel[:, row_off, col_off][:, None, None]
            * padded[..., row_off : row_off + height, col_off : col_off + breadth]
        )
    return summed


def simple_gate(doubled):
    halves = doubled.shape[-3] // 2
    return doubled[..., :halves, :, :] * doubled[..., halves:, :, :]


def attend(hidden, queries, query_other, value_other, scales):
    scores = jnp.einsum(
        "...chi,...chj->...hij", queries, query_other, precision=highest
    ) * queries.shape[-3] ** (-0.5)
    weights = jnp.exp(scores)
    weights = weights / jnp.sum(weights, axis=-1, keepdims=True)
    carried = jnp.einsum("...hij,...chj->...chi", weights, value_other, precision=highest)
    return hidden + scales[:, None, None] * carried


def block_tail(
    frames,
    gating,
    pooled,
    pool_proj,
    pool_bias,
    squeeze_out,
    branch_scale,
    ffn_expand,
    ffn_shrink,
    ffn_scale,
):
    attention = jnp.einsum("oc,...c->...o", pool_proj, pooled, precision=highest) + pool_bias
    scaled = gating * attention[..., :, None, None]
    residual_one = frames + branch_scale[:, None, None] * mixing(squeeze_out, scaled)
    expanded = mixing(ffn_expand, channel_norm(residual_one))
    return residual_one + ffn_scale[:, None, None] * mixing(ffn_shrink, simple_gate(expanded))


def front_piece(frames, expand_in):
    return mixing(expand_in, channel_norm(frames))


def conv_piece(banded, conv_kernel):
    padded = jnp.pad(banded, ((0, 0), (0, 0), (0, 0), (1, 1)))
    return simple_gate(depthwise(padded, conv_kernel, banded.shape[2] - 2, banded.shape[3]))


def query_piece(hidden, query_proj):
    return mixing(query_proj, channel_norm(hidden))


def value_piece(hidden, value_proj):
    return mixing(value_proj, hidden)


def all_sum_kernel(factor, part_ref, out_ref, first, second, third, sends, recvs):
    row = lax.axis_index("row")
    lane = lax.axis_index("dp") * 2 + lax.axis_index("view")

    def in_row(step):
        return {"row": lax.rem(row + step, 16)}

    def in_lane(step):
        other = lax.rem(lane + step, 16)
        return {"dp": other // 2, "view": lax.rem(other, 2)}

    barrier = pltpu.get_barrier_semaphore()
    for step in range(1, 16):
        for device in (in_row(step), in_lane(step)):
            pl.semaphore_signal(
                barrier, inc=1, device_id=device, device_id_type=pl.DeviceIdType.MESH
            )
    pl.semaphore_wait(barrier, 30)

    def spread(phase, source, target, device):
        copies = []
        for step in range(1, 16):
            copy = pltpu.make_async_remote_copy(
                src_ref=source(step),
                dst_ref=target,
                send_sem=sends.at[phase, step - 1],
                recv_sem=recvs.at[phase, step - 1],
                device_id=device(step),
                device_id_type=pl.DeviceIdType.MESH,
            )
            copy.start()
            copies.append(copy)
        return copies

    copies = spread(0, lambda step: part_ref.at[lax.rem(row + step, 16)], first.at[row], in_row)
    first[row] = part_ref[row]
    for copy in copies:
        copy.wait()
    second[lane] = jnp.sum(first[...], axis=0)
    copies = spread(1, lambda step: second.at[lane], second.at[lane], in_lane)
    for copy in copies:
        copy.wait()
    third[row] = jnp.sum(second[...], axis=0) * factor
    copies = spread(2, lambda step: third.at[row], third.at[row], in_row)
    for copy in copies:
        copy.wait()
    out_ref[...] = third[...]


def sum_everywhere(parts, factor):
    return pl.pallas_call(
        functools.partial(all_sum_kernel, factor),
        out_shape=jax.ShapeDtypeStruct(parts.shape, jnp.float32),
        in_specs=[pl.BlockSpec(memory_space=pltpu.VMEM)],
        out_specs=pl.BlockSpec(memory_space=pltpu.VMEM),
        scratch_shapes=[
            pltpu.VMEM(parts.shape, jnp.float32),
            pltpu.VMEM(parts.shape, jnp.float32),
            pltpu.VMEM(parts.shape, jnp.float32),
            pltpu.SemaphoreType.DMA((3, 15)),
            pltpu.SemaphoreType.DMA((3, 15)),
        ],
        compiler_params=pltpu.CompilerParams(collective_id=0, has_side_effects=True),
    )(parts)


def per_device(
    frames_in,
    cotangent,
    expand_in,
    conv_kernel,
    pool_proj,
    pool_bias,
    squeeze_out,
    branch_scale,
    ffn_expand,
    ffn_shrink,
    ffn_scale,
    query_proj,
    value_proj,
    cross_scale,
):
    frames = frames_in[0]
    upstream = cotangent[0]
    own_query = query_proj[0]
    own_value = value_proj[0]
    own_scale = cross_scale[0]
    height = frames.shape[2] * lax.axis_size("row")
    breadth = frames.shape[3]
    factor = (2 * frames.shape[0] * lax.axis_size("dp") * height * breadth) ** (-0.5)
    doubled, back_front = jax.vjp(front_piece, frames, expand_in)
    banded = extended(doubled, (("row", 2),), 1)
    gating, back_conv = jax.vjp(conv_piece, banded, conv_kernel)
    pooled = taken_together(jnp.sum(gating, axis=(2, 3)), "row") / (height * breadth)
    hidden, back_tail = jax.vjp(
        block_tail,
        frames,
        gating,
        pooled,
        pool_proj,
        pool_bias,
        squeeze_out,
        branch_scale,
        ffn_expand,
        ffn_shrink,
        ffn_scale,
    )
    queries, back_query = jax.vjp(query_piece, hidden, own_query)
    hidden_other, query_weight_other, value_weight_other = partner(
        (hidden, own_query, own_value), "view", 0
    )
    query_other, back_query_other = jax.vjp(query_piece, hidden_other, query_weight_other)
    value_other, back_value_other = jax.vjp(value_piece, hidden_other, value_weight_other)
    output, back_attend = jax.vjp(attend, hidden, queries, query_other, value_other, own_scale)
    hidden_grad, query_grad, other_query_grad, other_value_grad, scale_grad = back_attend(upstream)
    other_from_query, other_query_weight = back_query_other(other_query_grad)
    other_from_value, other_value_weight = back_value_other(other_value_grad)
    hidden_back, query_weight_back, value_weight_back = partner(
        (other_from_query + other_from_value, other_query_weight, other_value_weight), "view", 0
    )
    hidden_from_query, query_weight_own = back_query(query_grad)
    hidden_total = hidden_grad + hidden_from_query + hidden_back
    query_weight_grad = query_weight_own + query_weight_back
    tail_grads = back_tail(hidden_total)
    frames_grad_tail = tail_grads[0]
    gating_grad = tail_grads[1]
    pooled_grad = taken_together(tail_grads[2], "row")
    gating_total = gating_grad + (pooled_grad / (height * breadth))[:, :, None, None]
    banded_grad, kernel_grad = back_conv(gating_total)
    border_rows = jnp.concatenate([banded_grad[:, :, :1], banded_grad[:, :, -1:]], axis=2)
    received = extended(border_rows, (("row", 2),), 1)
    doubled_grad = banded_grad[:, :, 1:-1]
    doubled_grad = doubled_grad.at[:, :, :1].add(received[:, :, :1])
    doubled_grad = doubled_grad.at[:, :, -1:].add(received[:, :, 3:])
    frames_grad_front, expand_grad = back_front(doubled_grad)
    frames_grad = frames_grad_tail + frames_grad_front
    slot_index = lax.axis_index("view")
    picks = (jnp.arange(2) == slot_index).astype(jnp.float32)

    def widened(grad_item):
        return jnp.concatenate([picks[0] * grad_item, picks[1] * grad_item], axis=1)

    kernel_cols = kernel_grad.reshape(128, 9)
    columns = [kernel_cols[:64], kernel_cols[64:]]
    columns += [tail_grads[item][:, None] for item in (4, 6, 9)]
    columns += [widened(scale_grad[:, None]), jnp.zeros((64, 41), jnp.float32)]
    packed = jnp.concatenate(
        [
            jnp.concatenate([expand_grad, tail_grads[7]], axis=1),
            jnp.concatenate([tail_grads[5], tail_grads[8]], axis=1),
            jnp.concatenate([tail_grads[3]] + columns, axis=1),
            widened(query_weight_grad),
            widened(value_weight_back),
        ],
        axis=0,
    )
    total = sum_everywhere(packed.reshape(16, 24, 128), factor).reshape(384, 128)
    mixed = total[192:256]
    per_view = total[256:384].reshape(2, 64, 2, 64)
    chosen = lax.dynamic_index_in_dim(per_view, slot_index, 2, keepdims=False)
    shared_out = [
        total[:128, :64],
        jnp.concatenate([mixed[:, 64:73], mixed[:, 73:82]], axis=0).reshape(128, 3, 3),
        mixed[:, :64],
        mixed[:, 82],
        total[128:192, :64],
        mixed[:, 83],
        total[:128, 64:],
        total[128:192, 64:],
        mixed[:, 84],
    ]
    cross = lax.dynamic_index_in_dim(mixed[:, 85:87], slot_index, 1, keepdims=False)
    owned_out = [chosen[0][None], chosen[1][None], cross[None]]
    return (
        output[None],
        frames_grad[None],
        shared_out[0],
        shared_out[1],
        shared_out[2],
        shared_out[3],
        shared_out[4],
        shared_out[5],
        shared_out[6],
        shared_out[7],
        shared_out[8],
        owned_out[0],
        owned_out[1],
        owned_out[2],
    )


def solution(mesh):
    placed = (
        P("view", "dp", None, "row", None),
        P("view", "dp", None, "row", None),
        P(),
        P(),
        P(),
        P(),
        P(),
        P(),
        P(),
        P(),
        P(),
        P("view", None, None),
        P("view", None, None),
        P("view", None),
    )
    return jax.shard_map(
        per_device,
        mesh=mesh,
        in_specs=placed,
        out_specs=(
            P("view", "dp", None, "row", None),
            P("view", "dp", None, "row", None),
            P(),
            P(),
            P(),
            P(),
            P(),
            P(),
            P(),
            P(),
            P(),
            P("view", None, None),
            P("view", None, None),
            P("view", None),
        ),
        check_vma=False,
    )
```

```python
import functools

import jax
import jax.numpy as jnp
from jax import lax
from jax.experimental import pallas as pl
from jax.experimental.pallas import tpu as pltpu
from jax.sharding import PartitionSpec as P

epsilon = 1e-06
WIDE = 512
f32 = jnp.float32
bf16 = jnp.bfloat16
MESH = pl.DeviceIdType.MESH


def halves(x):
    high = x.astype(bf16)
    return high, (x - high.astype(f32)).astype(bf16)


def left_parts(x):
    high, low = halves(x)
    return jnp.concatenate([high, low, high], axis=0)


def right_parts(x):
    high, low = halves(x)
    return jnp.concatenate([high, high, low], axis=0)


def dot_nn(a, b):
    return lax.dot_general(a, b, (((1,), (0,)), ((), ())), preferred_element_type=f32)


def dot_nt(a, b):
    return lax.dot_general(a, b, (((1,), (1,)), ((), ())), preferred_element_type=f32)


def dot_tn(a, b):
    return lax.dot_general(a, b, (((0,), (0,)), ((), ())), preferred_element_type=f32)


def over_pixels(a, b):
    a_high, a_low = halves(a)
    b_high, b_low = halves(b)
    return dot_nt(
        jnp.concatenate([a_high, a_low, a_high], axis=1),
        jnp.concatenate([b_high, b_high, b_low], axis=1),
    )


def fold(x):
    return x[:, :128] + x[:, 128:256] + x[:, 256:384] + x[:, 384:]


def normed(x):
    center = x - jnp.mean(x, axis=0, keepdims=True)
    scale = 1.0 / jnp.sqrt(jnp.mean(center * center, axis=0, keepdims=True) + epsilon)
    return center * scale, scale


def normed_back(grad, value, scale):
    return scale * (
        grad
        - jnp.mean(grad, axis=0, keepdims=True)
        - value * jnp.mean(grad * value, axis=0, keepdims=True)
    )


def block_kernel(
    sizes,
    factor,
    area,
    cols,
    x_ref,
    up_ref,
    expand_ref,
    taps_ref,
    pool_ref,
    bias_ref,
    squeeze_ref,
    branch_ref,
    ffn_up_ref,
    ffn_down_ref,
    ffn_scale_ref,
    query_ref,
    value_ref,
    cross_ref,
    out_ref,
    grad_ref,
    sum_ref,
    x_s,
    c_s,
    cp_s,
    n0_s,
    s0_s,
    d_s,
    cv_s,
    g_s,
    t_s,
    n1_s,
    s1_s,
    e_s,
    u_s,
    h_s,
    hp_s,
    dh_s,
    dhp_s,
    op_s,
    dg_s,
    dr_s,
    dcv_s,
    e_att,
    taps_s,
    fold_s,
    tap_acc,
    queryp_s,
    valuep_s,
    crossp_s,
    pool_s,
    poolg_s,
    part_s,
    first,
    second,
    third,
    expand_f,
    expand_b,
    squeeze_f,
    squeeze_b,
    up_f,
    up_b,
    down_f,
    down_b,
    sends,
    recvs,
    group_sends,
    group_recvs,
):
    rows, lanes = sizes
    row = lax.axis_index("row")
    view = lax.axis_index("view")
    lane = lax.axis_index("dp") * 2 + view
    mine = 2 * view
    theirs = 2 - mine

    def in_row(step):
        return {"row": lax.rem(row + step, rows)}

    def in_lane(step):
        other = lax.rem(lane + step, lanes)
        return {"dp": other // 2, "view": lax.rem(other, 2)}

    above = in_row(rows - 1)
    below = in_row(1)
    partner = {"view": 1 - view}

    barrier = pltpu.get_barrier_semaphore()
    for step in range(1, rows):
        pl.semaphore_signal(barrier, inc=1, device_id=in_row(step), device_id_type=MESH)
    for step in range(1, lanes):
        pl.semaphore_signal(barrier, inc=1, device_id=in_lane(step), device_id_type=MESH)

    def send(index, source, target, device):
        copy = pltpu.make_async_remote_copy(
            src_ref=source,
            dst_ref=target,
            send_sem=sends.at[index],
            recv_sem=recvs.at[index],
            device_id=device,
            device_id_type=MESH,
        )
        copy.start()
        return copy

    def spread(phase, source, target, device, count):
        copies = []
        for step in range(1, count):
            copy = pltpu.make_async_remote_copy(
                src_ref=source(step),
                dst_ref=target,
                send_sem=group_sends.at[phase, step - 1],
                recv_sem=group_recvs.at[phase, step - 1],
                device_id=device(step),
                device_id_type=MESH,
            )
            copy.start()
            copies.append(copy)
        return copies

    for h in range(4):
        x_s[h + 1, :, 384:] = jnp.zeros((64, 128), f32)
        c_s[h, :, 384:] = jnp.zeros((64, 128), f32)
        x_s[h + 1, :, :cols] = x_ref[:, h, :]
        c_s[h, :, :cols] = up_ref[:, h, :]

    pl.semaphore_wait(barrier, rows + lanes - 2)
    halo_up = send(0, x_s.at[1], x_s.at[5], above)
    halo_down = send(1, x_s.at[4], x_s.at[0], below)
    weights_sent = [
        send(2, query_ref, queryp_s, partner),
        send(3, value_ref, valuep_s, partner),
        send(4, cross_ref, crossp_s, partner),
    ]
    cotangent_sent = send(5, c_s.at[pl.ds(theirs, 2)], cp_s, partner)

    def prepare(weight, forward, backward):
        if forward is not None:
            forward[...] = left_parts(weight.T).astype(f32).T.astype(bf16)
        if backward is not None:
            backward[...] = left_parts(weight).astype(f32).T.astype(bf16)

    prepare(expand_ref[...], expand_f, expand_b)
    prepare(squeeze_ref[...], squeeze_f, squeeze_b)
    prepare(ffn_up_ref[...], up_f, up_b)
    prepare(ffn_down_ref[...], down_f, down_b)
    eye = lax.broadcasted_iota(jnp.int32, (64, 128), 0) == lax.broadcasted_iota(
        jnp.int32, (64, 128), 1
    )

    def to_column(vector):
        spread_out = jnp.broadcast_to(vector, (64, vector.shape[1]))
        return jnp.sum(
            jnp.where(eye[:, : vector.shape[1]], spread_out, 0.0), axis=1, keepdims=True
        )

    def to_row(column):
        return jnp.sum(
            jnp.where(eye, jnp.broadcast_to(column, (64, 128)), 0.0), axis=0, keepdims=True
        )

    for tap in range(9):
        taps_s[tap] = jnp.broadcast_to(taps_ref[:, tap : tap + 1], (128, 128))
    bias = to_column(bias_ref[...])
    branch = to_column(branch_ref[...])
    ffn_scale = to_column(ffn_scale_ref[...])
    cross = to_column(cross_ref[...])
    inside = lax.broadcasted_iota(jnp.int32, (1, WIDE), 1) < cols
    part_s[...] = jnp.zeros_like(part_s)
    fold_s[...] = jnp.zeros_like(fold_s)
    tap_acc[...] = jnp.zeros_like(tap_acc)

    def expand_row(h):
        value, scale = normed(x_s[h])
        d_s[h] = dot_nn(expand_f[...], right_parts(value))
        return value, scale

    @pl.loop(1, 5)
    def _(h):
        value, scale = expand_row(h)
        n0_s[h - 1] = value
        s0_s[h - 1] = scale

    halo_up.wait()
    halo_down.wait()

    @pl.when(row == 0)
    def _():
        x_s[0] = jnp.zeros((64, WIDE), f32)

    @pl.when(row == rows - 1)
    def _():
        x_s[5] = jnp.zeros((64, WIDE), f32)

    expand_row(0)
    expand_row(5)

    def tap_at(tap, start, size):
        piece = taps_s[tap, pl.ds(start, size), :]
        return jnp.concatenate([piece] * 4, axis=1)

    @pl.loop(1, 5)
    def _(h):
        for start in range(0, 128, 16):
            columns = [jnp.zeros((16, WIDE), f32)] * 3
            for i in range(3):
                value = d_s[h + i - 1, start : start + 16, :]
                for j in range(3):
                    columns[j] = columns[j] + tap_at(3 * i + j, start, 16) * value
            total = columns[1] + pltpu.roll(columns[0], 1, 1) + pltpu.roll(columns[2], WIDE - 1, 1)
            cv_s[h, start : start + 16, :] = jnp.where(inside, total, 0.0)
        gate = cv_s[h, :64, :] * cv_s[h, 64:, :]
        g_s[h - 1] = gate
        fold_s[0] += fold(gate)

    pool_s[row] = to_row(jnp.sum(fold_s[0], axis=1, keepdims=True))
    copies = spread(0, lambda step: pool_s.at[row], pool_s.at[row], in_row, rows)
    conv_up = send(6, cv_s.at[1], cv_s.at[5], above)
    conv_down = send(7, cv_s.at[4], cv_s.at[0], below)
    for copy in copies:
        copy.wait()
    pooled = jnp.sum(pool_s[...], axis=0) / area
    attention = jnp.sum(pool_ref[...] * pooled[:, :64], axis=1, keepdims=True) + bias

    def tail_row(h):
        squeezed = dot_nn(squeeze_f[...], right_parts(g_s[h] * attention))
        t_s[h] = squeezed
        residual = x_s[h + 1] + branch * squeezed
        value, scale = normed(residual)
        n1_s[h] = value
        s1_s[h] = scale
        expanded = dot_nn(up_f[...], right_parts(value))
        e_s[h] = expanded
        shrunk = dot_nn(down_f[...], right_parts(expanded[:64] * expanded[64:]))
        u_s[h] = shrunk
        h_s[h] = residual + ffn_scale * shrunk

    @pl.loop(0, 2)
    def _(k):
        tail_row(theirs + k)

    hidden_sent = send(8, h_s.at[pl.ds(theirs, 2)], hp_s, partner)

    @pl.loop(0, 2)
    def _(k):
        tail_row(mine + k)

    for copy in weights_sent:
        copy.wait()
    cotangent_sent.wait()
    hidden_sent.wait()
    crossp = to_column(crossp_s[...])

    def query_parts(weight):
        return left_parts(weight.T), left_parts(weight)

    sixteen = lax.broadcasted_iota(jnp.int32, (16, WIDE), 0)
    outside16 = lax.broadcasted_iota(jnp.int32, (16, WIDE), 1) >= cols
    ones16 = jnp.ones((16, WIDE), bf16)
    mask_left = jnp.where(
        sixteen == 0, jnp.where(outside16, -256.0, 0.0), jnp.where(sixteen == 1, 1.0, 0.0)
    ).astype(bf16)
    mask_right = jnp.where(
        sixteen == 0, 1.0, jnp.where((sixteen == 1) & outside16, -256.0, 0.0)
    ).astype(bf16)

    def attend_row(k):
        h = mine + k
        own, other = h_s[h], hp_s[k]
        own_up, other_up = c_s[h], cp_s[k]
        own_n, own_scale = normed(own)
        other_n, other_scale = normed(other)
        own_wq, own_wq_back = query_parts(query_ref[...])
        own_wv, own_wv_back = query_parts(value_ref[...])
        other_wq, other_wq_back = query_parts(queryp_s[...])
        other_wv, other_wv_back = query_parts(valuep_s[...])
        own_q = dot_tn(own_wq, right_parts(own_n))
        other_q = dot_tn(other_wq, right_parts(other_n))
        own_v = dot_tn(own_wv, right_parts(own))
        other_v = dot_tn(other_wv, right_parts(other))
        scores = dot_tn(
            jnp.concatenate([left_parts(own_q * 0.125), mask_left], axis=0),
            jnp.concatenate([right_parts(other_q), mask_right], axis=0),
        )
        weights = jnp.exp(scores)
        e_att[...] = weights
        w_high, w_low = halves(weights)

        def weighted(dot, values):
            high, low = halves(values)
            large = dot(jnp.concatenate([high, ones16, low], axis=0), w_high)
            small = dot(jnp.concatenate([high, ones16], axis=0), w_low)
            bottom = jnp.where(inside, large[64:65] + small[64:65], 1.0)
            return large[:64] + large[80:] + small[:64], 1.0 / bottom

        def through(dot, values, high_m, low_m):
            high, low = halves(values)
            large = dot(jnp.concatenate([high, low], axis=0), high_m)
            return large[:64] + large[64:] + dot(high, low_m)

        own_c, own_r = weighted(dot_nt, other_v)
        other_c, other_r = weighted(dot_nn, own_v)
        own_c = own_c * own_r
        other_c = other_c * other_r
        out_ref[h] = own + cross * own_c
        op_s[k] = other + crossp * other_c
        own_d = cross * own_up * own_r
        other_d = crossp * other_up * other_r
        fold_s[4] += fold(own_up * own_c)
        fold_s[5] += fold(other_up * other_c)
        own_delta, own_delta_low = halves(-jnp.sum(own_d * own_c, axis=0, keepdims=True))
        other_delta, other_delta_low = halves(-jnp.sum(other_d * other_c, axis=0, keepdims=True))
        left_tail = jnp.where(
            sixteen == 0,
            own_delta.astype(f32),
            jnp.where(
                sixteen == 1, own_delta_low.astype(f32), jnp.where(sixteen < 4, 1.0, 0.0)
            ),
        ).astype(bf16)
        right_tail = jnp.where(
            sixteen == 2,
            other_delta.astype(f32),
            jnp.where(
                sixteen == 3, other_delta_low.astype(f32), jnp.where(sixteen < 2, 1.0, 0.0)
            ),
        ).astype(bf16)
        change = dot_tn(
            jnp.concatenate(
                [left_parts(jnp.concatenate([own_d, own_v], axis=0)), left_tail], axis=0
            ),
            jnp.concatenate(
                [right_parts(jnp.concatenate([other_v, other_d], axis=0)), right_tail], axis=0
            ),
        )
        ds_high, ds_low = halves(e_att[...] * change * 0.125)
        other_dv = through(dot_nn, own_d, w_high, w_low)
        own_dv = through(dot_nt, other_d, w_high, w_low)
        other_dq = through(dot_nn, own_q, ds_high, ds_low)
        own_dq = through(dot_nt, other_q, ds_high, ds_low)

        def back(up, dq, dv, wq_back, wv_back, value, scale):
            dn = dot_tn(wq_back, right_parts(dq))
            return up + dot_tn(wv_back, right_parts(dv)) + normed_back(dn, value, scale)

        dhp_s[k] = back(
            other_up, other_dq, other_dv, other_wq_back, other_wv_back, other_n, other_scale
        )
        dh_s[h] = back(own_up, own_dq, own_dv, own_wq_back, own_wv_back, own_n, own_scale)
        grads = [
            over_pixels(own_dq, own_n),
            over_pixels(other_dq, other_n),
            over_pixels(own_dv, own),
            over_pixels(other_dv, other),
        ]
        for start, (first_grad, second_grad) in ((256, grads[:2]), (320, grads[2:])):
            part_s[start : start + 64, :64] += jnp.where(view == 0, first_grad, second_grad)
            part_s[start : start + 64, 64:] += jnp.where(view == 0, second_grad, first_grad)

    returned = []
    for k in range(2):
        attend_row(k)
        returned.append(send(9 + k, dhp_s.at[k], dh_s.at[mine + k], partner))
    out_sent = send(11, op_s, out_ref.at[pl.ds(mine, 2)], partner)

    def tail_back_row(h):
        up = dh_s[h]
        fold_s[1] += fold(up * u_s[h])
        du = ffn_scale * up
        expanded = e_s[h]
        gate = expanded[:64] * expanded[64:]
        dgate = dot_nn(down_b[...], right_parts(du))
        part_s[128:192, 64:] += over_pixels(du, gate)
        de = jnp.concatenate([dgate * expanded[64:], dgate * expanded[:64]], axis=0)
        part_s[:128, 64:] += over_pixels(de, n1_s[h])
        dn = dot_nn(up_b[...], right_parts(de))
        dr = up + normed_back(dn, n1_s[h], s1_s[h])
        dr_s[h] = dr
        fold_s[2] += fold(dr * t_s[h])
        dt = branch * dr
        g = g_s[h]
        dscaled = dot_nn(squeeze_b[...], right_parts(dt))
        part_s[128:192, :64] += over_pixels(dt, g * attention)
        fold_s[3] += fold(dscaled * g)
        dg_s[h + 1] = dscaled * attention

    @pl.loop(0, 2)
    def _(k):
        tail_back_row(mine + k)

    for copy in returned:
        copy.wait()

    @pl.loop(0, 2)
    def _(k):
        tail_back_row(theirs + k)

    d_attention = jnp.sum(fold_s[3], axis=1, keepdims=True)
    poolg_s[row, :, :64] = jnp.sum(pool_ref[...] * d_attention, axis=0, keepdims=True)
    poolg_s[row, :, 64:] = jnp.zeros((1, 64), f32)
    copies = spread(1, lambda step: poolg_s.at[row], poolg_s.at[row], in_row, rows)
    gate_up = send(12, dg_s.at[1], dg_s.at[5], above)
    gate_down = send(13, dg_s.at[4], dg_s.at[0], below)
    conv_up.wait()
    conv_down.wait()
    for copy in copies:
        copy.wait()
    constant = to_column(jnp.sum(poolg_s[...], axis=0) / area)
    gate_up.wait()
    gate_down.wait()

    @pl.loop(0, 6)
    def _(h):
        total = dg_s[h] + constant
        dcv_s[h, :64, :] = total * cv_s[h, 64:, :]
        dcv_s[h, 64:, :] = total * cv_s[h, :64, :]

    @pl.when(row == 0)
    def _():
        dcv_s[0] = jnp.zeros((128, WIDE), f32)

    @pl.when(row == rows - 1)
    def _():
        dcv_s[5] = jnp.zeros((128, WIDE), f32)

    @pl.loop(0, 8)
    def _(chunk):
        start = pl.multiple_of(chunk * 16, 16)
        size = 16
        for h in range(1, 5):
            center = dcv_s[h, pl.ds(start, size), :]
            moved = [pltpu.roll(center, WIDE - 1, 1), center, pltpu.roll(center, 1, 1)]
            for i in range(3):
                value = d_s[h + i - 1, pl.ds(start, size), :]
                for j in range(3):
                    tap_acc[3 * i + j, pl.ds(start, size), :] += fold(moved[j] * value)
        for h in range(1, 5):
            columns = [jnp.zeros((size, WIDE), f32)] * 3
            for i in range(3):
                value = dcv_s[h - i + 1, pl.ds(start, size), :]
                for j in range(3):
                    columns[j] = columns[j] + tap_at(3 * i + j, start, size) * value
            cv_s[h, pl.ds(start, size), :] = (
                columns[1] + pltpu.roll(columns[2], 1, 1) + pltpu.roll(columns[0], WIDE - 1, 1)
            )

    @pl.loop(0, 4)
    def _(h):
        dd = cv_s[h + 1]
        dn = dot_nn(expand_b[...], right_parts(dd))
        part_s[:128, :64] += over_pixels(dd, n0_s[h])
        grad_ref[h] = dr_s[h] + normed_back(dn, n0_s[h], s0_s[h])

    place = lax.broadcasted_iota(jnp.int32, (64, 128), 1)
    mixed = d_attention * pooled

    def columns_of(value):
        return jnp.sum(value, axis=1, keepdims=True)

    items = []
    for tap in range(9):
        items.append(columns_of(tap_acc[tap, :64, :]))
    for tap in range(9):
        items.append(columns_of(tap_acc[tap, 64:, :]))
    items += [d_attention, columns_of(fold_s[2]), columns_of(fold_s[1])]
    own_cross = columns_of(fold_s[4])
    other_cross = columns_of(fold_s[5])
    items.append(jnp.where(view == 0, own_cross, other_cross))
    items.append(jnp.where(view == 0, other_cross, own_cross))
    for index, item in enumerate(items):
        mixed = jnp.where(place == 64 + index, item, mixed)
    part_s[192:256, :] = mixed

    size = 384 // rows

    def chunk_at(index):
        return part_s.at[pl.ds(pl.multiple_of(index * size, 8), size)]

    copies = spread(
        2, lambda step: chunk_at(lax.rem(row + step, rows)), first.at[row], in_row, rows
    )
    first[row] = part_s[pl.ds(pl.multiple_of(row * size, 8), size), :]
    for copy in copies:
        copy.wait()
    second[lane] = jnp.sum(first[...], axis=0)
    copies = spread(3, lambda step: second.at[lane], second.at[lane], in_lane, lanes)
    for copy in copies:
        copy.wait()
    third[row] = jnp.sum(second[...], axis=0) * factor
    copies = spread(4, lambda step: third.at[row], third.at[row], in_row, rows)
    for copy in copies:
        copy.wait()
    sum_ref[...] = third[...]
    out_sent.wait()


def per_device(rows, lanes, *arrays):
    (
        frames_in,
        cotangent,
        expand_in,
        conv_kernel,
        pool_proj,
        pool_bias,
        squeeze_out,
        branch_scale,
        ffn_expand,
        ffn_shrink,
        ffn_scale,
        query_proj,
        value_proj,
        cross_scale,
    ) = arrays
    cols = frames_in.shape[4]
    area = 4 * rows * cols
    factor = (lanes * area) ** (-0.5)
    wide = functools.partial(jax.ShapeDtypeStruct, dtype=f32)

    def fields(*shape):
        return pltpu.VMEM(shape, f32)

    size = 384 // rows
    scratch = [
        fields(6, 64, WIDE),
        fields(4, 64, WIDE),
        fields(2, 64, WIDE),
        fields(4, 64, WIDE),
        fields(4, 1, WIDE),
        fields(6, 128, WIDE),
        fields(6, 128, WIDE),
        fields(4, 64, WIDE),
        fields(4, 64, WIDE),
        fields(4, 64, WIDE),
        fields(4, 1, WIDE),
        fields(4, 128, WIDE),
        fields(4, 64, WIDE),
        fields(4, 64, WIDE),
        fields(2, 64, WIDE),
        fields(4, 64, WIDE),
        fields(2, 64, WIDE),
        fields(2, 64, WIDE),
        fields(6, 64, WIDE),
        fields(4, 64, WIDE),
        fields(6, 128, WIDE),
        fields(WIDE, WIDE),
        fields(9, 128, 128),
        fields(6, 64, 128),
        fields(9, 128, 128),
        fields(64, 64),
        fields(64, 64),
        fields(1, 64),
        fields(rows, 1, 128),
        fields(rows, 1, 128),
        fields(384, 128),
        fields(rows, size, 128),
        fields(lanes, size, 128),
        fields(rows, size, 128),
        pltpu.VMEM((128, 192), bf16),
        pltpu.VMEM((64, 384), bf16),
        pltpu.VMEM((64, 192), bf16),
        pltpu.VMEM((64, 192), bf16),
        pltpu.VMEM((128, 192), bf16),
        pltpu.VMEM((64, 384), bf16),
        pltpu.VMEM((64, 192), bf16),
        pltpu.VMEM((64, 192), bf16),
        pltpu.SemaphoreType.DMA((14,)),
        pltpu.SemaphoreType.DMA((14,)),
        pltpu.SemaphoreType.DMA((5, 15)),
        pltpu.SemaphoreType.DMA((5, 15)),
    ]
    out, grad, total = pl.pallas_call(
        functools.partial(block_kernel, (rows, lanes), factor, area, cols),
        out_shape=(wide((4, 64, WIDE)), wide((4, 64, WIDE)), wide((rows, size, 128))),
        in_specs=[pl.BlockSpec(memory_space=pltpu.VMEM)] * 14,
        out_specs=(pl.BlockSpec(memory_space=pltpu.VMEM),) * 3,
        scratch_shapes=scratch,
        compiler_params=pltpu.CompilerParams(
            collective_id=0, has_side_effects=True, vmem_limit_bytes=56 * 2**20
        ),
    )(
        frames_in[0, 0],
        cotangent[0, 0],
        expand_in,
        conv_kernel.reshape(128, 9),
        pool_proj,
        pool_bias[None],
        squeeze_out,
        branch_scale[None],
        ffn_expand,
        ffn_shrink,
        ffn_scale[None],
        query_proj[0],
        value_proj[0],
        cross_scale,
    )

    def placed(value):
        return value[:, :, :cols].transpose(1, 0, 2)[None, None]

    total = total.reshape(384, 128)
    slot = lax.axis_index("view")
    mixed = total[192:256]
    per_view = total[256:384].reshape(2, 64, 2, 64)
    chosen = lax.dynamic_index_in_dim(per_view, slot, 2, keepdims=False)
    cross = lax.dynamic_index_in_dim(mixed[:, 85:87], slot, 1, keepdims=False)
    return (
        placed(out),
        placed(grad),
        total[:128, :64],
        jnp.concatenate([mixed[:, 64:73], mixed[:, 73:82]], axis=0).reshape(128, 3, 3),
        mixed[:, :64],
        mixed[:, 82],
        total[128:192, :64],
        mixed[:, 83],
        total[:128, 64:],
        total[128:192, 64:],
        mixed[:, 84],
        chosen[0][None],
        chosen[1][None],
        cross[None],
    )


def solution(mesh):
    field = P("view", "dp", None, "row", None)
    copied = (P(),) * 9
    owned = (P("view", None, None), P("view", None, None), P("view", None))
    return jax.shard_map(
        functools.partial(per_device, mesh.shape["row"], 2 * mesh.shape["dp"]),
        mesh=mesh,
        in_specs=(field, field) + copied + owned,
        out_specs=(field, field) + copied + owned,
        check_vma=False,
    )
```

```python
import functools

import jax
import jax.numpy as jnp
from jax import lax
from jax.experimental import pallas as pl
from jax.experimental.pallas import tpu as pltpu
from jax.sharding import PartitionSpec as P

epsilon = 1e-06
WIDE = 512
f32 = jnp.float32
bf16 = jnp.bfloat16
MESH = pl.DeviceIdType.MESH


def halves(x):
    high = x.astype(bf16)
    return high, (x - high.astype(f32)).astype(bf16)


def left_parts(x):
    high, low = halves(x)
    return jnp.concatenate([high, low, high], axis=0)


def right_parts(x):
    high, low = halves(x)
    return jnp.concatenate([high, high, low], axis=0)


def dot_nn(a, b):
    return lax.dot_general(a, b, (((1,), (0,)), ((), ())), preferred_element_type=f32)


def dot_nt(a, b):
    return lax.dot_general(a, b, (((1,), (1,)), ((), ())), preferred_element_type=f32)


def dot_tn(a, b):
    return lax.dot_general(a, b, (((0,), (0,)), ((), ())), preferred_element_type=f32)


def over_pixels(a, b):
    a_high, a_low = halves(a)
    b_high, b_low = halves(b)
    return dot_nt(
        jnp.concatenate([a_high, a_low, a_high], axis=1),
        jnp.concatenate([b_high, b_high, b_low], axis=1),
    )


def fold(x):
    return x[:, :128] + x[:, 128:256] + x[:, 256:384] + x[:, 384:]


class Link:
    def __init__(self, copy, sends=None, receives=None):
        self.copy, self.sends, self.receives = copy, sends, receives
        if sends is None:
            copy.start()
        else:
            pl.when(sends)(copy.start)

    def wait(self):
        if self.sends is None:
            self.copy.wait()
        else:
            pl.when(self.receives)(self.copy.wait_recv)
            pl.when(self.sends)(self.copy.wait_send)


def normed(x):
    center = x - jnp.mean(x, axis=0, keepdims=True)
    scale = 1.0 / jnp.sqrt(jnp.mean(center * center, axis=0, keepdims=True) + epsilon)
    return center * scale, scale


def normed_back(grad, value, scale):
    return scale * (
        grad
        - jnp.mean(grad, axis=0, keepdims=True)
        - value * jnp.mean(grad * value, axis=0, keepdims=True)
    )


def block_kernel(sizes, factor, area, cols, *refs):
    operands, results, refs = refs[:14], refs[14:18], refs[18:]
    out_ref, grad_ref, early_ref, late_ref = results
    (
        x_in, c_in, expand_w, taps_w, pool_w, bias_w, squeeze_w, branch_w,
        up_w, down_w, scale_w, query_w, value_w, cross_w,
    ) = refs[:14]
    (
        x_s, c_s, cp_s, n0_s, s0_s, d_s, cv_s, g_s, t_s, n1_s, s1_s, e_s, u_s, h_s,
        hp_s, dh_s, dhp_s, o_s, op_s, dg_s, dr_s, de_s, dcv_s, e_att, att_s, attn_s, atts_s,
        taps_s, fold_s, tap_acc, queryp_s, valuep_s, crossp_s, pool_s, poolg_s,
        early, late, early_1, early_2, early_3, late_1, late_2, late_3,
        expand_f, expand_b, squeeze_f, squeeze_b, up_f, up_b, down_f, down_b,
        query_f, query_b, value_f, value_b,
        loads, sends, recvs, group_sends, group_recvs,
    ) = refs[14:]
    rows, lanes = sizes
    row = lax.axis_index("row")
    view = lax.axis_index("view")
    lane = lax.axis_index("dp") * 2 + view
    mine = (3 * view, 1 + view)
    theirs = (3 - 3 * view, 2 - view)
    slots = (view, 1 - view)
    edge = view * (rows - 1)
    other_edge = rows - 1 - edge

    def in_row(step):
        return {"row": lax.rem(row + step, rows)}

    def in_lane(step):
        other = lax.rem(lane + step, lanes)
        return {"dp": other // 2, "view": lax.rem(other, 2)}

    above = in_row(rows - 1)
    below = in_row(1)
    mine_side = in_row((1 - view) * (rows - 1) + view)
    theirs_side = in_row(view * (rows - 1) + 1 - view)
    partner = {"view": 1 - view}

    barrier = pltpu.get_barrier_semaphore()
    for step in range(1, rows):
        pl.semaphore_signal(barrier, inc=1, device_id=in_row(step), device_id_type=MESH)
    for step in range(1, lanes):
        pl.semaphore_signal(barrier, inc=1, device_id=in_lane(step), device_id_type=MESH)

    local = [
        pltpu.make_async_copy(operands[item], refs[item], loads.at[item]) for item in range(14)
    ]
    for item in (0, 2, 3, 4, 5, 6, 7, 8, 9, 10, 11, 12, 13, 1):
        local[item].start()

    def send(index, source, target, device, *when):
        return Link(
            pltpu.make_async_remote_copy(
                src_ref=source,
                dst_ref=target,
                send_sem=sends.at[index],
                recv_sem=recvs.at[index],
                device_id=device,
                device_id_type=MESH,
            ),
            *when,
        )

    def spread(phase, source, target, device, count):
        return [
            Link(
                pltpu.make_async_remote_copy(
                    src_ref=source(step),
                    dst_ref=target,
                    send_sem=group_sends.at[phase, step - 1],
                    recv_sem=group_recvs.at[phase, step - 1],
                    device_id=device(step),
                    device_id_type=MESH,
                )
            )
            for step in range(1, count)
        ]

    def finish(links):
        for link in links:
            link.wait()

    for h in range(4):
        x_s[h + 1, :, 384:] = jnp.zeros((64, 128), f32)
    local[0].wait()
    for h in (0, 3, 1, 2):
        x_s[h + 1, :, :cols] = x_in[:, h, :]

    pl.semaphore_wait(barrier, rows + lanes - 2)
    halo_up = send(0, x_s.at[1], x_s.at[5], above, row != 0, row != rows - 1)
    halo_down = send(1, x_s.at[4], x_s.at[0], below, row != rows - 1, row != 0)

    def forward_parts(transposed):
        return left_parts(transposed).astype(f32).T.astype(bf16)

    for item in range(2, 14):
        local[item].wait()
    weights_sent = [
        send(2, query_w, queryp_s, partner),
        send(3, value_w, valuep_s, partner),
        send(4, cross_w, crossp_s, partner),
    ]
    expand_f[...] = forward_parts(expand_w[...])

    def expand_row(h):
        value, scale = normed(x_s[h])
        d_s[h] = dot_nn(expand_f[...], right_parts(value))
        return value, scale

    @pl.loop(1, 5)
    def _(h):
        value, scale = expand_row(h)
        n0_s[h - 1] = value
        s0_s[h - 1] = scale

    tap_rows = jnp.concatenate(
        [taps_w[i, j : j + 1, :] for i in range(3) for j in range(3)]
        + [jnp.zeros((7, 128), f32)],
        axis=0,
    )
    tap_columns = tap_rows.T
    for tap in range(9):
        taps_s[tap] = jnp.broadcast_to(tap_columns[:, tap : tap + 1], (128, 128))
    for h in range(4):
        c_s[h, :, 384:] = jnp.zeros((64, 128), f32)
    local[1].wait()
    for h in range(4):
        c_s[h, :, :cols] = c_in[:, h, :]

    halo_up.wait()
    halo_down.wait()

    @pl.when(row == 0)
    def _():
        x_s[0] = jnp.zeros((64, WIDE), f32)

    @pl.when(row == rows - 1)
    def _():
        x_s[5] = jnp.zeros((64, WIDE), f32)

    cotangent_sent = send(5, c_s.at[pl.ds(2 - 2 * view, 2)], cp_s, partner)
    expand_row(0)
    expand_row(5)

    inside = lax.broadcasted_iota(jnp.int32, (1, WIDE), 1) < cols
    fold_s[...] = jnp.zeros_like(fold_s)

    def tap_at(tap, start, size):
        piece = taps_s[tap, pl.ds(start, size), :]
        return jnp.concatenate([piece] * 4, axis=1)

    @pl.loop(1, 5)
    def _(h):
        for start in range(0, 128, 16):
            columns = [jnp.zeros((16, WIDE), f32)] * 3
            for i in range(3):
                value = d_s[h + i - 1, start : start + 16, :]
                for j in range(3):
                    columns[j] = columns[j] + tap_at(3 * i + j, start, 16) * value
            total = columns[1] + pltpu.roll(columns[0], 1, 1) + pltpu.roll(columns[2], WIDE - 1, 1)
            cv_s[h, start : start + 16, :] = jnp.where(inside, total, 0.0)
        gate = cv_s[h, :64, :] * cv_s[h, 64:, :]
        g_s[h - 1] = gate
        fold_s[0] += fold(gate)

    eye = lax.broadcasted_iota(jnp.int32, (64, 128), 0) == lax.broadcasted_iota(
        jnp.int32, (64, 128), 1
    )

    def to_column(vector):
        spread_out = jnp.broadcast_to(vector, (64, vector.shape[1]))
        return jnp.sum(
            jnp.where(eye[:, : vector.shape[1]], spread_out, 0.0), axis=1, keepdims=True
        )

    def to_row(column):
        return jnp.sum(
            jnp.where(eye, jnp.broadcast_to(column, (64, 128)), 0.0), axis=0, keepdims=True
        )

    pool_s[row] = to_row(jnp.sum(fold_s[0], axis=1, keepdims=True))
    links = spread(0, lambda step: pool_s.at[row], pool_s.at[row], in_row, rows)
    expand_b[...] = forward_parts(expand_w[...].T)
    up_f[...] = forward_parts(up_w[...])
    up_b[...] = forward_parts(up_w[...].T)
    for weight, forward, backward in (
        (squeeze_w, squeeze_f, squeeze_b),
        (down_w, down_f, down_b),
        (query_w, query_f.at[0], query_b.at[0]),
        (value_w, value_f.at[0], value_b.at[0]),
    ):
        forward[...] = forward_parts(weight[...].T)
        backward[...] = forward_parts(weight[...])
    bias = to_column(bias_w[...])
    branch = to_column(branch_w[...])
    ffn_scale = to_column(scale_w[...])
    cross = to_column(cross_w[...])
    tap_acc[...] = jnp.zeros_like(tap_acc)
    finish(links)

    conv_up = send(6, cv_s.at[1], cv_s.at[5], above, row != 0, row != rows - 1)
    conv_down = send(7, cv_s.at[4], cv_s.at[0], below, row != rows - 1, row != 0)
    pooled = jnp.sum(pool_s[...], axis=0) / area
    attention = jnp.sum(pool_w[...] * pooled[:, :64], axis=1, keepdims=True) + bias

    def tail_row(h):
        squeezed = dot_nn(squeeze_f[...], right_parts(g_s[h] * attention))
        t_s[h] = squeezed
        residual = x_s[h + 1] + branch * squeezed
        value, scale = normed(residual)
        n1_s[h] = value
        s1_s[h] = scale
        expanded = dot_nn(up_f[...], right_parts(value))
        e_s[h] = expanded
        shrunk = dot_nn(down_f[...], right_parts(expanded[:64] * expanded[64:]))
        u_s[h] = shrunk
        h_s[h] = residual + ffn_scale * shrunk

    hidden_sent = []
    for k in range(2):
        tail_row(theirs[k])
        hidden_sent.append(send(8 + k, h_s.at[theirs[k]], hp_s.at[k], partner))
    for k in range(2):
        tail_row(mine[k])

    finish(weights_sent)
    query_f[1] = forward_parts(queryp_s[...].T)
    query_b[1] = forward_parts(queryp_s[...])
    value_f[1] = forward_parts(valuep_s[...].T)
    value_b[1] = forward_parts(valuep_s[...])
    crossp = to_column(crossp_s[...])
    cotangent_sent.wait()

    sixteen = lax.broadcasted_iota(jnp.int32, (16, WIDE), 0)
    outside16 = lax.broadcasted_iota(jnp.int32, (16, WIDE), 1) >= cols
    ones16 = jnp.ones((16, WIDE), bf16)
    mask_left = jnp.where(
        sixteen == 0, jnp.where(outside16, -256.0, 0.0), jnp.where(sixteen == 1, 1.0, 0.0)
    ).astype(bf16)
    mask_right = jnp.where(
        sixteen == 0, 1.0, jnp.where((sixteen == 1) & outside16, -256.0, 0.0)
    ).astype(bf16)

    def attend_row(k):
        own, other = h_s[mine[k]], hp_s[k]
        own_up, other_up = c_s[mine[k]], cp_s[slots[k]]
        own_n, own_scale = normed(own)
        other_n, other_scale = normed(other)
        attn_s[k, 0] = own_n
        attn_s[k, 1] = other_n
        atts_s[k] = own_scale
        own_q = dot_nn(query_f[0], right_parts(own_n))
        other_q = dot_nn(query_f[1], right_parts(other_n))
        own_v = dot_nn(value_f[0], right_parts(own))
        other_v = dot_nn(value_f[1], right_parts(other))
        scores = dot_tn(
            jnp.concatenate([left_parts(own_q * 0.125), mask_left], axis=0),
            jnp.concatenate([right_parts(other_q), mask_right], axis=0),
        )
        weights = jnp.exp(scores)
        e_att[...] = weights
        w_high, w_low = halves(weights)

        def weighted(dot, values):
            high, low = halves(values)
            large = dot(jnp.concatenate([high, ones16, low], axis=0), w_high)
            small = dot(jnp.concatenate([high, ones16], axis=0), w_low)
            bottom = jnp.where(inside, large[64:65] + small[64:65], 1.0)
            return large[:64] + large[80:] + small[:64], 1.0 / bottom

        def through(dot, values, high_m, low_m):
            high, low = halves(values)
            large = dot(jnp.concatenate([high, low], axis=0), high_m)
            return large[:64] + large[64:] + dot(high, low_m)

        own_c, own_r = weighted(dot_nt, other_v)
        other_c, other_r = weighted(dot_nn, own_v)
        own_c = own_c * own_r
        other_c = other_c * other_r
        o_s[mine[k]] = own + cross * own_c
        op_s[k] = other + crossp * other_c
        own_d = cross * own_up * own_r
        other_d = crossp * other_up * other_r
        fold_s[4] += fold(own_up * own_c)
        fold_s[5] += fold(other_up * other_c)
        own_delta, own_delta_low = halves(-jnp.sum(own_d * own_c, axis=0, keepdims=True))
        other_delta, other_delta_low = halves(-jnp.sum(other_d * other_c, axis=0, keepdims=True))
        left_tail = jnp.where(
            sixteen == 0,
            own_delta.astype(f32),
            jnp.where(
                sixteen == 1, own_delta_low.astype(f32), jnp.where(sixteen < 4, 1.0, 0.0)
            ),
        ).astype(bf16)
        right_tail = jnp.where(
            sixteen == 2,
            other_delta.astype(f32),
            jnp.where(
                sixteen == 3, other_delta_low.astype(f32), jnp.where(sixteen < 2, 1.0, 0.0)
            ),
        ).astype(bf16)
        change = dot_tn(
            jnp.concatenate(
                [left_parts(jnp.concatenate([own_d, own_v], axis=0)), left_tail], axis=0
            ),
            jnp.concatenate(
                [right_parts(jnp.concatenate([other_v, other_d], axis=0)), right_tail], axis=0
            ),
        )
        ds_high, ds_low = halves(e_att[...] * change * 0.125)
        other_dv = through(dot_nn, own_d, w_high, w_low)
        other_dq = through(dot_nn, own_q, ds_high, ds_low)
        dn = dot_nn(query_b[1], right_parts(other_dq))
        dhp_s[k] = (
            other_up
            + dot_nn(value_b[1], right_parts(other_dv))
            + normed_back(dn, other_n, other_scale)
        )
        att_s[k, 1] = other_dq
        att_s[k, 3] = other_dv
        att_s[k, 2] = through(dot_nt, other_d, w_high, w_low)
        att_s[k, 0] = through(dot_nt, other_q, ds_high, ds_low)

    def own_back(k):
        dn = dot_nn(query_b[0], right_parts(att_s[k, 0]))
        dh_s[mine[k]] = (
            c_s[mine[k]]
            + dot_nn(value_b[0], right_parts(att_s[k, 2]))
            + normed_back(dn, attn_s[k, 0], atts_s[k])
        )

    returned = []
    for k in range(2):
        hidden_sent[k].wait()
        attend_row(k)
        returned.append(send(10 + k, dhp_s.at[k], dh_s.at[mine[k]], partner))

    def tail_back_row(h):
        up = dh_s[h]
        expanded = e_s[h]
        dgate = dot_nn(down_b[...], right_parts(ffn_scale * up))
        de = jnp.concatenate([dgate * expanded[64:], dgate * expanded[:64]], axis=0)
        de_s[h] = de
        dn = dot_nn(up_b[...], right_parts(de))
        dr = up + normed_back(dn, n1_s[h], s1_s[h])
        dr_s[h] = dr
        dscaled = dot_nn(squeeze_b[...], right_parts(branch * dr))
        fold_s[3] += fold(dscaled * g_s[h])
        dg_s[h + 1] = dscaled * attention

    own_back(0)
    tail_back_row(mine[0])
    gate_mine = send(
        12, dg_s.at[mine[0] + 1], dg_s.at[5 - 5 * view], mine_side, row != edge, row != other_edge
    )
    own_back(1)
    tail_back_row(mine[1])

    returned[0].wait()
    tail_back_row(theirs[0])
    gate_theirs = send(
        13, dg_s.at[theirs[0] + 1], dg_s.at[5 * view], theirs_side, row != other_edge, row != edge
    )
    returned[1].wait()
    tail_back_row(theirs[1])

    d_attention = jnp.sum(fold_s[3], axis=1, keepdims=True)
    poolg_s[row, :, :64] = jnp.sum(pool_w[...] * d_attention, axis=0, keepdims=True)
    poolg_s[row, :, 64:] = jnp.zeros((1, 64), f32)
    links = spread(1, lambda step: poolg_s.at[row], poolg_s.at[row], in_row, rows)
    out_sent = [send(14 + k, op_s.at[k], o_s.at[mine[k]], partner) for k in range(2)]

    query_grads = [jnp.zeros((64, 64), f32)] * 4
    for k in range(2):
        fields = (attn_s[k, 0], attn_s[k, 1], h_s[mine[k]], hp_s[k])
        for item in range(4):
            query_grads[item] = query_grads[item] + over_pixels(att_s[k, item], fields[item])
    for start, pair in ((128, query_grads[:2]), (192, query_grads[2:])):
        early[start : start + 64, :64] = jnp.where(view == 0, pair[0], pair[1])
        early[start : start + 64, 64:] = jnp.where(view == 0, pair[1], pair[0])
    early[:128, :] = jnp.zeros((128, 128), f32)

    @pl.loop(0, 4)
    def _(h):
        up = dh_s[h]
        dr = dr_s[h]
        fold_s[1] += fold(up * u_s[h])
        fold_s[2] += fold(dr * t_s[h])
        expanded = e_s[h]
        early[:64, :] += over_pixels(n1_s[h], de_s[h])
        early[64:128, :64] += over_pixels(branch * dr, g_s[h] * attention)
        early[64:128, 64:] += over_pixels(ffn_scale * up, expanded[:64] * expanded[64:])

    finish(links)

    early_size, late_size = 256 // rows, 128 // rows

    def chunk_at(index, size):
        return pl.ds(pl.multiple_of(index * size, 8), size)

    links = spread(
        2,
        lambda step: early.at[chunk_at(lax.rem(row + step, rows), early_size)],
        early_1.at[row],
        in_row,
        rows,
    )
    early_1[row] = early[chunk_at(row, early_size), :]
    constant = to_column(jnp.sum(poolg_s[...], axis=0) / area)

    def gate_back_row(h):
        total = dg_s[h] + constant
        dcv_s[h, :64, :] = total * cv_s[h, 64:, :]
        dcv_s[h, 64:, :] = total * cv_s[h, :64, :]

    pl.loop(1, 5)(gate_back_row)
    gate_mine.wait()
    gate_theirs.wait()
    conv_up.wait()
    conv_down.wait()
    for outer, limit in ((0, 0), (5, rows - 1)):

        @pl.when(row == limit)
        def _():
            dcv_s[outer] = jnp.zeros((128, WIDE), f32)

        @pl.when(row != limit)
        def _():
            gate_back_row(outer)

    @pl.loop(0, 8)
    def _(chunk):
        start = pl.multiple_of(chunk * 16, 16)
        size = 16
        for h in range(1, 5):
            center = dcv_s[h, pl.ds(start, size), :]
            moved = [pltpu.roll(center, WIDE - 1, 1), center, pltpu.roll(center, 1, 1)]
            for i in range(3):
                value = d_s[h + i - 1, pl.ds(start, size), :]
                for j in range(3):
                    tap_acc[3 * i + j, pl.ds(start, size), :] += fold(moved[j] * value)
        for h in range(1, 5):
            columns = [jnp.zeros((size, WIDE), f32)] * 3
            for i in range(3):
                value = dcv_s[h - i + 1, pl.ds(start, size), :]
                for j in range(3):
                    columns[j] = columns[j] + tap_at(3 * i + j, start, size) * value
            cv_s[h, pl.ds(start, size), :] = (
                columns[1] + pltpu.roll(columns[2], 1, 1) + pltpu.roll(columns[0], WIDE - 1, 1)
            )

    finish(links)

    early_2[lane] = jnp.sum(early_1[...], axis=0)
    early_links = spread(3, lambda step: early_2.at[lane], early_2.at[lane], in_lane, lanes)

    late[:64, :] = jnp.zeros((64, 128), f32)

    @pl.loop(0, 4)
    def _(h):
        late[:64, :] += over_pixels(n0_s[h], cv_s[h + 1])

    place = lax.broadcasted_iota(jnp.int32, (64, 128), 1)

    def columns_of(value):
        return jnp.sum(value, axis=1, keepdims=True)

    items = [columns_of(tap_acc[tap, :64, :]) for tap in range(9)]
    items += [columns_of(tap_acc[tap, 64:, :]) for tap in range(9)]
    items += [d_attention, columns_of(fold_s[2]), columns_of(fold_s[1])]
    own_cross = columns_of(fold_s[4])
    other_cross = columns_of(fold_s[5])
    items.append(jnp.where(view == 0, own_cross, other_cross))
    items.append(jnp.where(view == 0, other_cross, own_cross))
    mixed = d_attention * pooled
    for index, item in enumerate(items):
        mixed = jnp.where(place == 64 + index, item, mixed)
    late[64:, :] = mixed

    late_links = spread(
        5,
        lambda step: late.at[chunk_at(lax.rem(row + step, rows), late_size)],
        late_1.at[row],
        in_row,
        rows,
    )
    late_1[row] = late[chunk_at(row, late_size), :]

    @pl.loop(0, 4)
    def _(h):
        dn = dot_nn(expand_b[...], right_parts(cv_s[h + 1]))
        dr_s[h] = dr_s[h] + normed_back(dn, n0_s[h], s0_s[h])

    finish(early_links)
    early_3[row] = jnp.sum(early_2[...], axis=0) * factor
    early_links = spread(4, lambda step: early_3.at[row], early_3.at[row], in_row, rows)
    finish(late_links)

    late_2[lane] = jnp.sum(late_1[...], axis=0)
    late_links = spread(6, lambda step: late_2.at[lane], late_2.at[lane], in_lane, lanes)
    for h in range(4):
        grad_ref[:, h, :] = dr_s[h, :, :cols]
    finish(out_sent)
    finish(late_links)

    late_3[row] = jnp.sum(late_2[...], axis=0) * factor
    late_links = spread(7, lambda step: late_3.at[row], late_3.at[row], in_row, rows)
    for h in range(4):
        out_ref[:, h, :] = o_s[h, :, :cols]
    finish(early_links)
    early_ref[...] = early_3[...]
    finish(late_links)
    late_ref[...] = late_3[...]


def format_kernel(out_in, grad_in, early_ref, late_ref, *refs):
    (
        out_ref, grad_ref, expand_ref, taps_ref, pool_ref, bias_ref, squeeze_ref, branch_ref,
        up_ref, down_ref, scale_ref, query_ref, value_ref, cross_ref, sems,
    ) = refs
    copies = [
        pltpu.make_async_copy(out_in, out_ref, sems.at[0]),
        pltpu.make_async_copy(grad_in, grad_ref, sems.at[1]),
    ]
    for copy in copies:
        copy.start()
    view = lax.axis_index("view")
    up_ref[...] = early_ref[:64, :]
    middle = early_ref[64:128, :]
    squeeze_ref[...] = middle[:, :64]
    down_ref[...] = middle[:, 64:]
    for start, target in ((128, query_ref), (192, value_ref)):
        both = early_ref[start : start + 64, :]
        target[...] = jnp.where(view == 0, both[:, :64], both[:, 64:])
    expand_ref[...] = late_ref[:64, :]
    mixed = late_ref[64:, :]
    pool_ref[...] = mixed[:, :64]
    turned = mixed.T
    for tap in range(9):
        taps_ref[tap // 3, tap % 3 : tap % 3 + 1, :64] = turned[64 + tap : 65 + tap, :]
        taps_ref[tap // 3, tap % 3 : tap % 3 + 1, 64:] = turned[73 + tap : 74 + tap, :]
    for place, target in ((82, bias_ref), (83, branch_ref), (84, scale_ref)):
        target[...] = turned[place : place + 1, :]
    cross_ref[...] = jnp.where(view == 0, turned[85:86, :], turned[86:87, :])
    for copy in copies:
        copy.wait()


def per_device(rows, lanes, *arrays):
    cols = arrays[0].shape[4]
    area = 4 * rows * cols
    factor = (lanes * area) ** (-0.5)
    wide = functools.partial(jax.ShapeDtypeStruct, dtype=f32)

    def fields(*shape):
        return pltpu.VMEM(shape, f32)

    def parts(*shape):
        return pltpu.VMEM(shape, bf16)

    operands = [
        arrays[0][0, 0],
        arrays[1][0, 0],
        arrays[2].T,
        arrays[3].transpose(1, 2, 0),
        arrays[4],
        arrays[5][None],
        arrays[6],
        arrays[7][None],
        arrays[8].T,
        arrays[9],
        arrays[10][None],
        arrays[11][0],
        arrays[12][0],
        arrays[13],
    ]
    early_size, late_size = 256 // rows, 128 // rows
    scratch = [fields(*operand.shape) for operand in operands] + [
        fields(6, 64, WIDE),
        fields(4, 64, WIDE),
        fields(2, 64, WIDE),
        fields(4, 64, WIDE),
        fields(4, 1, WIDE),
        fields(6, 128, WIDE),
        fields(6, 128, WIDE),
        fields(4, 64, WIDE),
        fields(4, 64, WIDE),
        fields(4, 64, WIDE),
        fields(4, 1, WIDE),
        fields(4, 128, WIDE),
        fields(4, 64, WIDE),
        fields(4, 64, WIDE),
        fields(2, 64, WIDE),
        fields(4, 64, WIDE),
        fields(2, 64, WIDE),
        fields(4, 64, WIDE),
        fields(2, 64, WIDE),
        fields(6, 64, WIDE),
        fields(4, 64, WIDE),
        fields(4, 128, WIDE),
        fields(6, 128, WIDE),
        fields(WIDE, WIDE),
        fields(2, 4, 64, WIDE),
        fields(2, 2, 64, WIDE),
        fields(2, 1, WIDE),
        fields(9, 128, 128),
        fields(6, 64, 128),
        fields(9, 128, 128),
        fields(64, 64),
        fields(64, 64),
        fields(1, 64),
        fields(rows, 1, 128),
        fields(rows, 1, 128),
        fields(256, 128),
        fields(128, 128),
        fields(rows, early_size, 128),
        fields(lanes, early_size, 128),
        fields(rows, early_size, 128),
        fields(rows, late_size, 128),
        fields(lanes, late_size, 128),
        fields(rows, late_size, 128),
        parts(128, 192),
        parts(64, 384),
        parts(64, 192),
        parts(64, 192),
        parts(128, 192),
        parts(64, 384),
        parts(64, 192),
        parts(64, 192),
        parts(2, 64, 192),
        parts(2, 64, 192),
        parts(2, 64, 192),
        parts(2, 64, 192),
        pltpu.SemaphoreType.DMA((14,)),
        pltpu.SemaphoreType.DMA((16,)),
        pltpu.SemaphoreType.DMA((16,)),
        pltpu.SemaphoreType.DMA((8, 15)),
        pltpu.SemaphoreType.DMA((8, 15)),
    ]
    in_place = pl.BlockSpec(memory_space=pl.ANY)
    in_vmem = pl.BlockSpec(memory_space=pltpu.VMEM)
    out, grad, early, late = pl.pallas_call(
        functools.partial(block_kernel, (rows, lanes), factor, area, cols),
        out_shape=(
            wide((64, 4, cols)),
            wide((64, 4, cols)),
            wide((rows, early_size, 128)),
            wide((rows, late_size, 128)),
        ),
        in_specs=[in_place] * 14,
        out_specs=(in_vmem,) * 4,
        scratch_shapes=scratch,
        compiler_params=pltpu.CompilerParams(
            collective_id=0, has_side_effects=True, vmem_limit_bytes=56 * 2**20
        ),
    )(*operands)
    shapes = [operand.shape for operand in operands]
    done = pl.pallas_call(
        format_kernel,
        out_shape=[wide(shape) for shape in shapes],
        in_specs=[in_place, in_place, in_vmem, in_vmem],
        out_specs=[in_place, in_place] + [in_vmem] * 12,
        scratch_shapes=[pltpu.SemaphoreType.DMA((2,))],
    )(out, grad, early.reshape(256, 128), late.reshape(128, 128))
    return (
        done[0][None, None],
        done[1][None, None],
        done[2].T,
        done[3].transpose(2, 0, 1),
        done[4],
        done[5][0],
        done[6],
        done[7][0],
        done[8].T,
        done[9],
        done[10][0],
        done[11][None],
        done[12][None],
        done[13],
    )


def solution(mesh):
    field = P("view", "dp", None, "row", None)
    copied = (P(),) * 9
    owned = (P("view", None, None), P("view", None, None), P("view", None))
    return jax.shard_map(
        functools.partial(per_device, mesh.shape["row"], 2 * mesh.shape["dp"]),
        mesh=mesh,
        in_specs=(field, field) + copied + owned,
        out_specs=(field, field) + copied + owned,
        check_vma=False,
    )
```

```python
import functools

import jax
import jax.numpy as jnp
from jax import lax
from jax.experimental import pallas as pl
from jax.experimental.pallas import tpu as pltpu
from jax.sharding import PartitionSpec as P

epsilon = 1e-06
WIDE = 512
f32 = jnp.float32
bf16 = jnp.bfloat16
MESH = pl.DeviceIdType.MESH


def halves(x):
    high = x.astype(bf16)
    return high, (x - high.astype(f32)).astype(bf16)


def left_parts(x):
    high, low = halves(x)
    return jnp.concatenate([high, low, high], axis=0)


def right_parts(x):
    high, low = halves(x)
    return jnp.concatenate([high, high, low], axis=0)


def dot_nn(a, b):
    return lax.dot_general(a, b, (((1,), (0,)), ((), ())), preferred_element_type=f32)


def dot_nt(a, b):
    return lax.dot_general(a, b, (((1,), (1,)), ((), ())), preferred_element_type=f32)


def dot_tn(a, b):
    return lax.dot_general(a, b, (((0,), (0,)), ((), ())), preferred_element_type=f32)


def over_pixels(a, b):
    a_high, a_low = halves(a)
    b_high, b_low = halves(b)
    return dot_nt(
        jnp.concatenate([a_high, a_low, a_high], axis=1),
        jnp.concatenate([b_high, b_high, b_low], axis=1),
    )


def fold(x):
    return x[:, :128] + x[:, 128:256] + x[:, 256:384] + x[:, 384:]


class Link:
    def __init__(self, copy, sends=None, receives=None):
        self.copy, self.sends, self.receives = copy, sends, receives
        if sends is None:
            copy.start()
        else:
            pl.when(sends)(copy.start)

    def wait(self):
        if self.sends is None:
            self.copy.wait()
        else:
            pl.when(self.receives)(self.copy.wait_recv)
            pl.when(self.sends)(self.copy.wait_send)


def normed(x):
    center = x - jnp.mean(x, axis=0, keepdims=True)
    scale = 1.0 / jnp.sqrt(jnp.mean(center * center, axis=0, keepdims=True) + epsilon)
    return center * scale, scale


def normed_back(grad, value, scale):
    return scale * (
        grad
        - jnp.mean(grad, axis=0, keepdims=True)
        - value * jnp.mean(grad * value, axis=0, keepdims=True)
    )


def block_kernel(sizes, factor, area, cols, *refs):
    operands, results, refs = refs[:14], refs[14:18], refs[18:]
    out_ref, grad_ref, early_ref, late_ref = results
    (
        x_in, c_in, expand_w, taps_w, pool_w, bias_w, squeeze_w, branch_w,
        up_w, down_w, scale_w, query_w, value_w, cross_w,
    ) = refs[:14]
    (
        x_s, c_s, cp_s, n0_s, s0_s, d_s, cv_s, g_s, t_s, n1_s, s1_s, e_s, u_s, h_s,
        hp_s, dh_s, dhp_s, o_s, op_s, dg_s, dr_s, de_s, dcv_s, e_att, att_s, attn_s, atts_s,
        taps_s, fold_s, tap_acc, queryp_s, valuep_s, crossp_s, pool_s, poolg_s,
        early, late, early_1, early_2, early_3, late_1, late_2, late_3,
        expand_f, expand_b, squeeze_f, squeeze_b, up_f, up_b, down_f, down_b,
        query_f, query_b, value_f, value_b,
        loads, sends, recvs, group_sends, group_recvs,
    ) = refs[14:]
    rows, lanes = sizes
    row = lax.axis_index("row")
    view = lax.axis_index("view")
    lane = lax.axis_index("dp") * 2 + view
    mine = (3 * view, 1 + view)
    theirs = (3 - 3 * view, 2 - view)
    slots = (view, 1 - view)
    edge = view * (rows - 1)
    other_edge = rows - 1 - edge

    def in_row(step):
        return {"row": lax.rem(row + step, rows)}

    def in_lane(step):
        other = lax.rem(lane + step, lanes)
        return {"dp": other // 2, "view": lax.rem(other, 2)}

    above = in_row(rows - 1)
    below = in_row(1)
    mine_side = in_row((1 - view) * (rows - 1) + view)
    theirs_side = in_row(view * (rows - 1) + 1 - view)
    partner = {"view": 1 - view}

    barrier = pltpu.get_barrier_semaphore()
    for step in range(1, rows):
        pl.semaphore_signal(barrier, inc=1, device_id=in_row(step), device_id_type=MESH)
    for step in range(1, lanes):
        pl.semaphore_signal(barrier, inc=1, device_id=in_lane(step), device_id_type=MESH)

    local = [
        pltpu.make_async_copy(operands[item], refs[item], loads.at[item]) for item in range(14)
    ]
    for item in (0, 2, 3, 4, 5, 6, 7, 8, 9, 10, 11, 12, 13, 1):
        local[item].start()

    def send(index, source, target, device, *when):
        return Link(
            pltpu.make_async_remote_copy(
                src_ref=source,
                dst_ref=target,
                send_sem=sends.at[index],
                recv_sem=recvs.at[index],
                device_id=device,
                device_id_type=MESH,
            ),
            *when,
        )

    def spread(phase, source, target, device, count):
        return [
            Link(
                pltpu.make_async_remote_copy(
                    src_ref=source(step),
                    dst_ref=target,
                    send_sem=group_sends.at[phase, step - 1],
                    recv_sem=group_recvs.at[phase, step - 1],
                    device_id=device(step),
                    device_id_type=MESH,
                )
            )
            for step in range(1, count)
        ]

    def finish(links):
        for link in links:
            link.wait()

    for h in range(4):
        x_s[h + 1, :, 384:] = jnp.zeros((64, 128), f32)
    local[0].wait()
    for h in (0, 3, 1, 2):
        x_s[h + 1, :, :cols] = x_in[:, h, :]

    pl.semaphore_wait(barrier, rows + lanes - 2)
    halo_up = send(0, x_s.at[1], x_s.at[5], above, row != 0, row != rows - 1)
    halo_down = send(1, x_s.at[4], x_s.at[0], below, row != rows - 1, row != 0)

    def forward_parts(transposed):
        return left_parts(transposed).astype(f32).T.astype(bf16)

    for item in range(2, 14):
        local[item].wait()
    weights_sent = [
        send(2, query_w, queryp_s, partner),
        send(3, value_w, valuep_s, partner),
        send(4, cross_w, crossp_s, partner),
    ]
    expand_f[...] = forward_parts(expand_w[...])

    def expand_row(h):
        value, scale = normed(x_s[h])
        d_s[h] = dot_nn(expand_f[...], right_parts(value))
        return value, scale

    @pl.loop(1, 5)
    def _(h):
        value, scale = expand_row(h)
        n0_s[h - 1] = value
        s0_s[h - 1] = scale

    tap_rows = jnp.concatenate(
        [taps_w[i, j : j + 1, :] for i in range(3) for j in range(3)]
        + [jnp.zeros((7, 128), f32)],
        axis=0,
    )
    tap_columns = tap_rows.T
    for tap in range(9):
        taps_s[tap] = jnp.broadcast_to(tap_columns[:, tap : tap + 1], (128, 128))
    for h in range(4):
        c_s[h, :, 384:] = jnp.zeros((64, 128), f32)
    local[1].wait()
    for h in range(4):
        c_s[h, :, :cols] = c_in[:, h, :]

    halo_up.wait()
    halo_down.wait()

    @pl.when(row == 0)
    def _():
        x_s[0] = jnp.zeros((64, WIDE), f32)

    @pl.when(row == rows - 1)
    def _():
        x_s[5] = jnp.zeros((64, WIDE), f32)

    cotangent_sent = send(5, c_s.at[pl.ds(2 - 2 * view, 2)], cp_s, partner)
    expand_row(0)
    expand_row(5)

    inside = lax.broadcasted_iota(jnp.int32, (1, WIDE), 1) < cols
    fold_s[...] = jnp.zeros_like(fold_s)

    def tap_at(tap, start, size):
        piece = taps_s[tap, pl.ds(start, size), :]
        return jnp.concatenate([piece] * 4, axis=1)

    @pl.loop(1, 5)
    def _(h):
        for start in range(0, 128, 16):
            columns = [jnp.zeros((16, WIDE), f32)] * 3
            for i in range(3):
                value = d_s[h + i - 1, start : start + 16, :]
                for j in range(3):
                    columns[j] = columns[j] + tap_at(3 * i + j, start, 16) * value
            total = columns[1] + pltpu.roll(columns[0], 1, 1) + pltpu.roll(columns[2], WIDE - 1, 1)
            cv_s[h, start : start + 16, :] = jnp.where(inside, total, 0.0)
        gate = cv_s[h, :64, :] * cv_s[h, 64:, :]
        g_s[h - 1] = gate
        fold_s[0] += fold(gate)

    eye = lax.broadcasted_iota(jnp.int32, (64, 128), 0) == lax.broadcasted_iota(
        jnp.int32, (64, 128), 1
    )

    def to_column(vector):
        spread_out = jnp.broadcast_to(vector, (64, vector.shape[1]))
        return jnp.sum(
            jnp.where(eye[:, : vector.shape[1]], spread_out, 0.0), axis=1, keepdims=True
        )

    def to_row(column):
        return jnp.sum(
            jnp.where(eye, jnp.broadcast_to(column, (64, 128)), 0.0), axis=0, keepdims=True
        )

    pool_s[row] = to_row(jnp.sum(fold_s[0], axis=1, keepdims=True))
    links = spread(0, lambda step: pool_s.at[row], pool_s.at[row], in_row, rows)
    expand_b[...] = forward_parts(expand_w[...].T)
    up_f[...] = forward_parts(up_w[...])
    up_b[...] = forward_parts(up_w[...].T)
    for weight, forward, backward in (
        (squeeze_w, squeeze_f, squeeze_b),
        (down_w, down_f, down_b),
        (query_w, query_f.at[0], query_b.at[0]),
        (value_w, value_f.at[0], value_b.at[0]),
    ):
        forward[...] = forward_parts(weight[...].T)
        backward[...] = forward_parts(weight[...])
    bias = to_column(bias_w[...])
    branch = to_column(branch_w[...])
    ffn_scale = to_column(scale_w[...])
    cross = to_column(cross_w[...])
    tap_acc[...] = jnp.zeros_like(tap_acc)
    finish(links)

    conv_up = send(6, cv_s.at[1], cv_s.at[5], above, row != 0, row != rows - 1)
    conv_down = send(7, cv_s.at[4], cv_s.at[0], below, row != rows - 1, row != 0)
    pooled = jnp.sum(pool_s[...], axis=0) / area
    attention = jnp.sum(pool_w[...] * pooled[:, :64], axis=1, keepdims=True) + bias

    def tail_row(h):
        squeezed = dot_nn(squeeze_f[...], right_parts(g_s[h] * attention))
        t_s[h] = squeezed
        residual = x_s[h + 1] + branch * squeezed
        value, scale = normed(residual)
        n1_s[h] = value
        s1_s[h] = scale
        expanded = dot_nn(up_f[...], right_parts(value))
        e_s[h] = expanded
        shrunk = dot_nn(down_f[...], right_parts(expanded[:64] * expanded[64:]))
        u_s[h] = shrunk
        h_s[h] = residual + ffn_scale * shrunk

    hidden_sent = []
    for k in range(2):
        tail_row(theirs[k])
        hidden_sent.append(send(8 + k, h_s.at[theirs[k]], hp_s.at[k], partner))
    for k in range(2):
        tail_row(mine[k])

    finish(weights_sent)
    query_f[1] = forward_parts(queryp_s[...].T)
    query_b[1] = forward_parts(queryp_s[...])
    value_f[1] = forward_parts(valuep_s[...].T)
    value_b[1] = forward_parts(valuep_s[...])
    crossp = to_column(crossp_s[...])
    cotangent_sent.wait()

    sixteen = lax.broadcasted_iota(jnp.int32, (16, WIDE), 0)
    outside16 = lax.broadcasted_iota(jnp.int32, (16, WIDE), 1) >= cols
    ones16 = jnp.ones((16, WIDE), bf16)
    mask_left = jnp.where(
        sixteen == 0, jnp.where(outside16, -256.0, 0.0), jnp.where(sixteen == 1, 1.0, 0.0)
    ).astype(bf16)
    mask_right = jnp.where(
        sixteen == 0, 1.0, jnp.where((sixteen == 1) & outside16, -256.0, 0.0)
    ).astype(bf16)

    def attend_row(k):
        own, other = h_s[mine[k]], hp_s[k]
        own_up, other_up = c_s[mine[k]], cp_s[slots[k]]
        own_n, own_scale = normed(own)
        other_n, other_scale = normed(other)
        attn_s[k, 0] = own_n
        attn_s[k, 1] = other_n
        atts_s[k] = own_scale
        own_q = dot_nn(query_f[0], right_parts(own_n))
        other_q = dot_nn(query_f[1], right_parts(other_n))
        own_v = dot_nn(value_f[0], right_parts(own))
        other_v = dot_nn(value_f[1], right_parts(other))
        scores = dot_tn(
            jnp.concatenate([left_parts(own_q * 0.125), mask_left], axis=0),
            jnp.concatenate([right_parts(other_q), mask_right], axis=0),
        )
        weights = jnp.exp(scores)
        e_att[...] = weights
        w_high, w_low = halves(weights)

        def weighted(dot, values):
            high, low = halves(values)
            large = dot(jnp.concatenate([high, ones16, low], axis=0), w_high)
            small = dot(jnp.concatenate([high, ones16], axis=0), w_low)
            bottom = jnp.where(inside, large[64:65] + small[64:65], 1.0)
            return large[:64] + large[80:] + small[:64], 1.0 / bottom

        def through(dot, values, high_m, low_m):
            high, low = halves(values)
            large = dot(jnp.concatenate([high, low], axis=0), high_m)
            return large[:64] + large[64:] + dot(high, low_m)

        own_c, own_r = weighted(dot_nt, other_v)
        other_c, other_r = weighted(dot_nn, own_v)
        own_c = own_c * own_r
        other_c = other_c * other_r
        o_s[mine[k]] = own + cross * own_c
        op_s[k] = other + crossp * other_c
        if k == 0:
            out_sent.append(send(14, op_s.at[0], o_s.at[mine[0]], partner))
        own_d = cross * own_up * own_r
        other_d = crossp * other_up * other_r
        fold_s[4] += fold(own_up * own_c)
        fold_s[5] += fold(other_up * other_c)
        own_delta, own_delta_low = halves(-jnp.sum(own_d * own_c, axis=0, keepdims=True))
        other_delta, other_delta_low = halves(-jnp.sum(other_d * other_c, axis=0, keepdims=True))
        left_tail = jnp.where(
            sixteen == 0,
            own_delta.astype(f32),
            jnp.where(
                sixteen == 1, own_delta_low.astype(f32), jnp.where(sixteen < 4, 1.0, 0.0)
            ),
        ).astype(bf16)
        right_tail = jnp.where(
            sixteen == 2,
            other_delta.astype(f32),
            jnp.where(
                sixteen == 3, other_delta_low.astype(f32), jnp.where(sixteen < 2, 1.0, 0.0)
            ),
        ).astype(bf16)
        change = dot_tn(
            jnp.concatenate(
                [left_parts(jnp.concatenate([own_d, own_v], axis=0)), left_tail], axis=0
            ),
            jnp.concatenate(
                [right_parts(jnp.concatenate([other_v, other_d], axis=0)), right_tail], axis=0
            ),
        )
        ds_high, ds_low = halves(e_att[...] * change * 0.125)
        other_dv = through(dot_nn, own_d, w_high, w_low)
        other_dq = through(dot_nn, own_q, ds_high, ds_low)
        dn = dot_nn(query_b[1], right_parts(other_dq))
        dhp_s[k] = (
            other_up
            + dot_nn(value_b[1], right_parts(other_dv))
            + normed_back(dn, other_n, other_scale)
        )
        att_s[k, 1] = other_dq
        att_s[k, 3] = other_dv
        att_s[k, 2] = through(dot_nt, other_d, w_high, w_low)
        att_s[k, 0] = through(dot_nt, other_q, ds_high, ds_low)

    def own_back(k):
        dn = dot_nn(query_b[0], right_parts(att_s[k, 0]))
        dh_s[mine[k]] = (
            c_s[mine[k]]
            + dot_nn(value_b[0], right_parts(att_s[k, 2]))
            + normed_back(dn, attn_s[k, 0], atts_s[k])
        )

    returned = []
    out_sent = []
    for k in range(2):
        hidden_sent[k].wait()
        attend_row(k)
        returned.append(send(10 + k, dhp_s.at[k], dh_s.at[mine[k]], partner))

    def tail_back_row(h):
        up = dh_s[h]
        expanded = e_s[h]
        dgate = dot_nn(down_b[...], right_parts(ffn_scale * up))
        de = jnp.concatenate([dgate * expanded[64:], dgate * expanded[:64]], axis=0)
        de_s[h] = de
        dn = dot_nn(up_b[...], right_parts(de))
        dr = up + normed_back(dn, n1_s[h], s1_s[h])
        dr_s[h] = dr
        dscaled = dot_nn(squeeze_b[...], right_parts(branch * dr))
        fold_s[3] += fold(dscaled * g_s[h])
        dg_s[h + 1] = dscaled * attention

    own_back(0)
    tail_back_row(mine[0])
    gate_mine = send(
        12, dg_s.at[mine[0] + 1], dg_s.at[5 - 5 * view], mine_side, row != edge, row != other_edge
    )
    own_back(1)
    tail_back_row(mine[1])

    returned[0].wait()
    tail_back_row(theirs[0])
    gate_theirs = send(
        13, dg_s.at[theirs[0] + 1], dg_s.at[5 * view], theirs_side, row != other_edge, row != edge
    )
    returned[1].wait()
    tail_back_row(theirs[1])

    d_attention = jnp.sum(fold_s[3], axis=1, keepdims=True)
    poolg_s[row, :, :64] = jnp.sum(pool_w[...] * d_attention, axis=0, keepdims=True)
    poolg_s[row, :, 64:] = jnp.zeros((1, 64), f32)
    links = spread(1, lambda step: poolg_s.at[row], poolg_s.at[row], in_row, rows)
    out_sent.append(send(15, op_s.at[1], o_s.at[mine[1]], partner))

    query_grads = [jnp.zeros((64, 64), f32)] * 4
    for k in range(2):
        fields = (attn_s[k, 0], attn_s[k, 1], h_s[mine[k]], hp_s[k])
        for item in range(4):
            query_grads[item] = query_grads[item] + over_pixels(att_s[k, item], fields[item])
    for start, pair in ((128, query_grads[:2]), (192, query_grads[2:])):
        early[start : start + 64, :64] = jnp.where(view == 0, pair[0], pair[1])
        early[start : start + 64, 64:] = jnp.where(view == 0, pair[1], pair[0])
    early[:128, :] = jnp.zeros((128, 128), f32)

    @pl.loop(0, 4)
    def _(h):
        up = dh_s[h]
        dr = dr_s[h]
        fold_s[1] += fold(up * u_s[h])
        fold_s[2] += fold(dr * t_s[h])
        expanded = e_s[h]
        early[:64, :] += over_pixels(n1_s[h], de_s[h])
        early[64:128, :64] += over_pixels(branch * dr, g_s[h] * attention)
        early[64:128, 64:] += over_pixels(ffn_scale * up, expanded[:64] * expanded[64:])

    early_size, late_size = 256 // rows, 128 // lanes

    def chunk_at(index, size):
        return pl.ds(pl.multiple_of(index * size, 8), size)

    early_links = spread(
        2,
        lambda step: early.at[chunk_at(lax.rem(row + step, rows), early_size)],
        early_1.at[row],
        in_row,
        rows,
    )
    early_1[row] = early[chunk_at(row, early_size), :]
    finish(links)

    constant = to_column(jnp.sum(poolg_s[...], axis=0) / area)

    def gate_back_row(h):
        total = dg_s[h] + constant
        dcv_s[h, :64, :] = total * cv_s[h, 64:, :]
        dcv_s[h, 64:, :] = total * cv_s[h, :64, :]

    pl.loop(1, 5)(gate_back_row)
    gate_mine.wait()
    gate_theirs.wait()
    conv_up.wait()
    conv_down.wait()
    for outer, limit in ((0, 0), (5, rows - 1)):

        @pl.when(row == limit)
        def _():
            dcv_s[outer] = jnp.zeros((128, WIDE), f32)

        @pl.when(row != limit)
        def _():
            gate_back_row(outer)

    @pl.loop(0, 8)
    def _(chunk):
        start = pl.multiple_of(chunk * 16, 16)
        size = 16
        for h in range(1, 5):
            center = dcv_s[h, pl.ds(start, size), :]
            moved = [pltpu.roll(center, WIDE - 1, 1), center, pltpu.roll(center, 1, 1)]
            for i in range(3):
                value = d_s[h + i - 1, pl.ds(start, size), :]
                for j in range(3):
                    tap_acc[3 * i + j, pl.ds(start, size), :] += fold(moved[j] * value)
        for h in range(1, 5):
            columns = [jnp.zeros((size, WIDE), f32)] * 3
            for i in range(3):
                value = dcv_s[h - i + 1, pl.ds(start, size), :]
                for j in range(3):
                    columns[j] = columns[j] + tap_at(3 * i + j, start, size) * value
            cv_s[h, pl.ds(start, size), :] = (
                columns[1] + pltpu.roll(columns[2], 1, 1) + pltpu.roll(columns[0], WIDE - 1, 1)
            )

    finish(early_links)

    early_2[lane] = jnp.sum(early_1[...], axis=0)
    early_links = spread(3, lambda step: early_2.at[lane], early_2.at[lane], in_lane, lanes)

    late[:64, :] = jnp.zeros((64, 128), f32)

    @pl.loop(0, 4)
    def _(h):
        late[:64, :] += over_pixels(n0_s[h], cv_s[h + 1])

    place = lax.broadcasted_iota(jnp.int32, (64, 128), 1)

    def columns_of(value):
        return jnp.sum(value, axis=1, keepdims=True)

    items = [columns_of(tap_acc[tap, :64, :]) for tap in range(9)]
    items += [columns_of(tap_acc[tap, 64:, :]) for tap in range(9)]
    items += [d_attention, columns_of(fold_s[2]), columns_of(fold_s[1])]
    own_cross = columns_of(fold_s[4])
    other_cross = columns_of(fold_s[5])
    items.append(jnp.where(view == 0, own_cross, other_cross))
    items.append(jnp.where(view == 0, other_cross, own_cross))
    mixed = d_attention * pooled
    for index, item in enumerate(items):
        mixed = jnp.where(place == 64 + index, item, mixed)
    late[64:, :] = mixed

    late_links = spread(
        5,
        lambda step: late.at[chunk_at(lax.rem(lane + step, lanes), late_size)],
        late_1.at[lane],
        in_lane,
        lanes,
    )
    late_1[lane] = late[chunk_at(lane, late_size), :]

    @pl.loop(0, 4)
    def _(h):
        dn = dot_nn(expand_b[...], right_parts(cv_s[h + 1]))
        dr_s[h] = dr_s[h] + normed_back(dn, n0_s[h], s0_s[h])

    finish(early_links)
    early_3[row] = jnp.sum(early_2[...], axis=0) * factor
    early_links = spread(4, lambda step: early_3.at[row], early_3.at[row], in_row, rows)
    finish(late_links)

    late_2[row] = jnp.sum(late_1[...], axis=0)
    late_links = spread(6, lambda step: late_2.at[row], late_2.at[row], in_row, rows)
    for h in range(4):
        grad_ref[:, h, :] = dr_s[h, :, :cols]
    finish(out_sent)
    finish(late_links)

    late_3[lane] = jnp.sum(late_2[...], axis=0) * factor
    late_links = spread(7, lambda step: late_3.at[lane], late_3.at[lane], in_lane, lanes)
    for h in range(4):
        out_ref[:, h, :] = o_s[h, :, :cols]
    finish(early_links)
    early_ref[...] = early_3[...]
    finish(late_links)
    late_ref[...] = late_3[...]


def format_kernel(out_in, grad_in, early_ref, late_ref, *refs):
    (
        out_ref, grad_ref, expand_ref, taps_ref, pool_ref, bias_ref, squeeze_ref, branch_ref,
        up_ref, down_ref, scale_ref, query_ref, value_ref, cross_ref,
    ) = refs
    out_ref[...] = out_in[...]
    grad_ref[...] = grad_in[...]
    view = lax.axis_index("view")
    up_ref[...] = early_ref[:64, :]
    middle = early_ref[64:128, :]
    squeeze_ref[...] = middle[:, :64]
    down_ref[...] = middle[:, 64:]
    for start, target in ((128, query_ref), (192, value_ref)):
        both = early_ref[start : start + 64, :]
        target[...] = jnp.where(view == 0, both[:, :64], both[:, 64:])
    expand_ref[...] = late_ref[:64, :]
    mixed = late_ref[64:, :]
    pool_ref[...] = mixed[:, :64]
    turned = mixed.T
    for tap in range(9):
        taps_ref[tap // 3, tap % 3 : tap % 3 + 1, :64] = turned[64 + tap : 65 + tap, :]
        taps_ref[tap // 3, tap % 3 : tap % 3 + 1, 64:] = turned[73 + tap : 74 + tap, :]
    for place, target in ((82, bias_ref), (83, branch_ref), (84, scale_ref)):
        target[...] = turned[place : place + 1, :]
    cross_ref[...] = jnp.where(view == 0, turned[85:86, :], turned[86:87, :])


def per_device(rows, lanes, *arrays):
    cols = arrays[0].shape[4]
    area = 4 * rows * cols
    factor = (lanes * area) ** (-0.5)
    wide = functools.partial(jax.ShapeDtypeStruct, dtype=f32)

    def fields(*shape):
        return pltpu.VMEM(shape, f32)

    def parts(*shape):
        return pltpu.VMEM(shape, bf16)

    operands = [
        arrays[0][0, 0],
        arrays[1][0, 0],
        arrays[2].T,
        arrays[3].transpose(1, 2, 0),
        arrays[4],
        arrays[5][None],
        arrays[6],
        arrays[7][None],
        arrays[8].T,
        arrays[9],
        arrays[10][None],
        arrays[11][0],
        arrays[12][0],
        arrays[13],
    ]
    early_size, late_size = 256 // rows, 128 // lanes
    scratch = [fields(*operand.shape) for operand in operands] + [
        fields(6, 64, WIDE),
        fields(4, 64, WIDE),
        fields(2, 64, WIDE),
        fields(4, 64, WIDE),
        fields(4, 1, WIDE),
        fields(6, 128, WIDE),
        fields(6, 128, WIDE),
        fields(4, 64, WIDE),
        fields(4, 64, WIDE),
        fields(4, 64, WIDE),
        fields(4, 1, WIDE),
        fields(4, 128, WIDE),
        fields(4, 64, WIDE),
        fields(4, 64, WIDE),
        fields(2, 64, WIDE),
        fields(4, 64, WIDE),
        fields(2, 64, WIDE),
        fields(4, 64, WIDE),
        fields(2, 64, WIDE),
        fields(6, 64, WIDE),
        fields(4, 64, WIDE),
        fields(4, 128, WIDE),
        fields(6, 128, WIDE),
        fields(WIDE, WIDE),
        fields(2, 4, 64, WIDE),
        fields(2, 2, 64, WIDE),
        fields(2, 1, WIDE),
        fields(9, 128, 128),
        fields(6, 64, 128),
        fields(9, 128, 128),
        fields(64, 64),
        fields(64, 64),
        fields(1, 64),
        fields(rows, 1, 128),
        fields(rows, 1, 128),
        fields(256, 128),
        fields(128, 128),
        fields(rows, early_size, 128),
        fields(lanes, early_size, 128),
        fields(rows, early_size, 128),
        fields(lanes, late_size, 128),
        fields(rows, late_size, 128),
        fields(lanes, late_size, 128),
        parts(128, 192),
        parts(64, 384),
        parts(64, 192),
        parts(64, 192),
        parts(128, 192),
        parts(64, 384),
        parts(64, 192),
        parts(64, 192),
        parts(2, 64, 192),
        parts(2, 64, 192),
        parts(2, 64, 192),
        parts(2, 64, 192),
        pltpu.SemaphoreType.DMA((14,)),
        pltpu.SemaphoreType.DMA((16,)),
        pltpu.SemaphoreType.DMA((16,)),
        pltpu.SemaphoreType.DMA((8, 15)),
        pltpu.SemaphoreType.DMA((8, 15)),
    ]
    in_place = pl.BlockSpec(memory_space=pl.ANY)
    in_vmem = pl.BlockSpec(memory_space=pltpu.VMEM)
    out, grad, early, late = pl.pallas_call(
        functools.partial(block_kernel, (rows, lanes), factor, area, cols),
        out_shape=(
            wide((64, 4, cols)),
            wide((64, 4, cols)),
            wide((rows, early_size, 128)),
            wide((lanes, late_size, 128)),
        ),
        in_specs=[in_place] * 14,
        out_specs=(in_vmem,) * 4,
        scratch_shapes=scratch,
        compiler_params=pltpu.CompilerParams(
            collective_id=0, has_side_effects=True, vmem_limit_bytes=56 * 2**20
        ),
    )(*operands)
    shapes = [operand.shape for operand in operands]
    done = pl.pallas_call(
        format_kernel,
        out_shape=[wide(shape) for shape in shapes],
        in_specs=[in_vmem] * 4,
        out_specs=[in_vmem] * 14,
    )(out, grad, early.reshape(256, 128), late.reshape(128, 128))
    return (
        done[0][None, None],
        done[1][None, None],
        done[2].T,
        done[3].transpose(2, 0, 1),
        done[4],
        done[5][0],
        done[6],
        done[7][0],
        done[8].T,
        done[9],
        done[10][0],
        done[11][None],
        done[12][None],
        done[13],
    )


def solution(mesh):
    field = P("view", "dp", None, "row", None)
    copied = (P(),) * 9
    owned = (P("view", None, None), P("view", None, None), P("view", None))
    return jax.shard_map(
        functools.partial(per_device, mesh.shape["row"], 2 * mesh.shape["dp"]),
        mesh=mesh,
        in_specs=(field, field) + copied + owned,
        out_specs=(field, field) + copied + owned,
        check_vma=False,
    )
```

```python
import functools

import jax
import jax.numpy as jnp
from jax import lax
from jax.experimental import pallas as pl
from jax.experimental.pallas import tpu as pltpu
from jax.sharding import PartitionSpec as P

epsilon = 1e-06
WIDE = 512
f32 = jnp.float32
bf16 = jnp.bfloat16
MESH = pl.DeviceIdType.MESH


def halves(x):
    high = x.astype(bf16)
    return high, (x - high.astype(f32)).astype(bf16)


def left_parts(x):
    high, low = halves(x)
    return jnp.concatenate([high, low, high], axis=0)


def right_parts(x):
    high, low = halves(x)
    return jnp.concatenate([high, high, low], axis=0)


def dot_nn(a, b):
    return lax.dot_general(a, b, (((1,), (0,)), ((), ())), preferred_element_type=f32)


def dot_nt(a, b):
    return lax.dot_general(a, b, (((1,), (1,)), ((), ())), preferred_element_type=f32)


def dot_tn(a, b):
    return lax.dot_general(a, b, (((0,), (0,)), ((), ())), preferred_element_type=f32)


def over_pixels(a, b):
    a_high, a_low = halves(a)
    b_high, b_low = halves(b)
    return dot_nt(
        jnp.concatenate([a_high, a_low, a_high], axis=1),
        jnp.concatenate([b_high, b_high, b_low], axis=1),
    )


def fold(x):
    return x[:, :128] + x[:, 128:256] + x[:, 256:384] + x[:, 384:]


class Link:
    def __init__(self, copy, sends=None, receives=None):
        self.copy, self.sends, self.receives = copy, sends, receives
        if sends is None:
            copy.start()
        else:
            pl.when(sends)(copy.start)

    def wait(self):
        if self.sends is None:
            self.copy.wait()
        else:
            pl.when(self.receives)(self.copy.wait_recv)
            pl.when(self.sends)(self.copy.wait_send)


def normed(x):
    center = x - jnp.mean(x, axis=0, keepdims=True)
    scale = 1.0 / jnp.sqrt(jnp.mean(center * center, axis=0, keepdims=True) + epsilon)
    return center * scale, scale


def normed_back(grad, value, scale):
    return scale * (
        grad
        - jnp.mean(grad, axis=0, keepdims=True)
        - value * jnp.mean(grad * value, axis=0, keepdims=True)
    )


def far_first(count, ring):
    def hops(step):
        near = step % 8 if ring else step // 4
        around = 8 if ring else 4
        return min(near, around - near)

    return sorted(range(1, count), key=lambda step: -hops(step))


def block_kernel(sizes, factor, area, cols, *refs):
    operands, results, refs = refs[:14], refs[14:18], refs[18:]
    out_hbm, grad_hbm, early_ref, late_ref = results
    (
        x_in, c_in, expand_w, taps_w, pool_w, bias_w, squeeze_w, branch_w,
        up_w, down_w, scale_w, query_w, value_w, cross_w,
    ) = refs[:14]
    (
        x_s, c_s, cp_s, n0_s, s0_s, d_s, cv_s, g_s, t_s, n1_s, s1_s, e_s, u_s, h_s,
        hp_s, dh_s, dhp_s, o_s, op_s, dg_s, dr_s, de_s, dcv_s, e_att, att_s, attn_s, atts_s,
        taps_s, fold_s, tap_acc, queryp_s, valuep_s, crossp_s, pool_s, poolg_s,
        early, late, early_1, early_2, early_3, late_1, late_2, late_3,
        expand_f, expand_b, squeeze_f, squeeze_b, up_f, up_b, down_f, down_b,
        query_f, query_b, value_f, value_b,
        out_ref, grad_ref, loads, sends, recvs, group_sends, group_recvs,
    ) = refs[14:]
    rows, lanes = sizes
    row = lax.axis_index("row")
    view = lax.axis_index("view")
    lane = lax.axis_index("dp") * 2 + view
    mine = (3 * view, 1 + view)
    theirs = (3 - 3 * view, 2 - view)
    slots = (view, 1 - view)
    edge = view * (rows - 1)
    other_edge = rows - 1 - edge

    def in_row(step):
        return {"row": lax.rem(row + step, rows)}

    def in_lane(step):
        other = lax.rem(lane + step, lanes)
        return {"dp": other // 2, "view": lax.rem(other, 2)}

    above = in_row(rows - 1)
    below = in_row(1)
    mine_side = in_row((1 - view) * (rows - 1) + view)
    theirs_side = in_row(view * (rows - 1) + 1 - view)
    partner = {"view": 1 - view}

    barrier = pltpu.get_barrier_semaphore()
    for step in far_first(rows, True):
        pl.semaphore_signal(barrier, inc=1, device_id=in_row(step), device_id_type=MESH)
    for step in far_first(lanes, False):
        pl.semaphore_signal(barrier, inc=1, device_id=in_lane(step), device_id_type=MESH)

    local = [
        pltpu.make_async_copy(operands[item], refs[item], loads.at[item]) for item in range(14)
    ]
    for item in (0, 2, 3, 4, 5, 6, 7, 8, 9, 10, 11, 12, 13, 1):
        local[item].start()

    def send(index, source, target, device, *when):
        return Link(
            pltpu.make_async_remote_copy(
                src_ref=source,
                dst_ref=target,
                send_sem=sends.at[index],
                recv_sem=recvs.at[index],
                device_id=device,
                device_id_type=MESH,
            ),
            *when,
        )

    def spread(phase, source, target, device, count):
        return [
            Link(
                pltpu.make_async_remote_copy(
                    src_ref=source(step),
                    dst_ref=target,
                    send_sem=group_sends.at[phase, step - 1],
                    recv_sem=group_recvs.at[phase, step - 1],
                    device_id=device(step),
                    device_id_type=MESH,
                )
            )
            for step in far_first(count, device is in_row)
        ]

    def finish(links):
        for link in links:
            link.wait()

    for h in range(4):
        x_s[h + 1, :, 384:] = jnp.zeros((64, 128), f32)
    local[0].wait()
    for h in (0, 3, 1, 2):
        x_s[h + 1, :, :cols] = x_in[:, h, :]

    pl.semaphore_wait(barrier, rows + lanes - 2)
    halo_up = send(0, x_s.at[1], x_s.at[5], above, row != 0, row != rows - 1)
    halo_down = send(1, x_s.at[4], x_s.at[0], below, row != rows - 1, row != 0)

    def forward_parts(transposed):
        return left_parts(transposed).astype(f32).T.astype(bf16)

    for item in range(2, 14):
        local[item].wait()
    weights_sent = [
        send(2, query_w, queryp_s, partner),
        send(3, value_w, valuep_s, partner),
        send(4, cross_w, crossp_s, partner),
    ]
    expand_f[...] = forward_parts(expand_w[...])

    def expand_row(h):
        value, scale = normed(x_s[h])
        d_s[h] = dot_nn(expand_f[...], right_parts(value))
        return value, scale

    @pl.loop(1, 5)
    def _(h):
        value, scale = expand_row(h)
        n0_s[h - 1] = value
        s0_s[h - 1] = scale

    tap_rows = jnp.concatenate(
        [taps_w[i, j : j + 1, :] for i in range(3) for j in range(3)]
        + [jnp.zeros((7, 128), f32)],
        axis=0,
    )
    tap_columns = tap_rows.T
    for tap in range(9):
        taps_s[tap] = jnp.broadcast_to(tap_columns[:, tap : tap + 1], (128, 128))
    for h in range(4):
        c_s[h, :, 384:] = jnp.zeros((64, 128), f32)
    local[1].wait()
    for h in range(4):
        c_s[h, :, :cols] = c_in[:, h, :]

    cotangent_sent = send(5, c_s.at[pl.ds(2 - 2 * view, 2)], cp_s, partner)

    inside = lax.broadcasted_iota(jnp.int32, (1, WIDE), 1) < cols
    fold_s[...] = jnp.zeros_like(fold_s)

    def tap_at(tap, start, size):
        piece = taps_s[tap, pl.ds(start, size), :]
        return jnp.concatenate([piece] * 4, axis=1)

    def conv_row(h):
        for start in range(0, 128, 16):
            columns = [jnp.zeros((16, WIDE), f32)] * 3
            for i in range(3):
                value = d_s[h + i - 1, start : start + 16, :]
                for j in range(3):
                    columns[j] = columns[j] + tap_at(3 * i + j, start, 16) * value
            total = columns[1] + pltpu.roll(columns[0], 1, 1) + pltpu.roll(columns[2], WIDE - 1, 1)
            cv_s[h, start : start + 16, :] = jnp.where(inside, total, 0.0)
        gate = cv_s[h, :64, :] * cv_s[h, 64:, :]
        g_s[h - 1] = gate
        fold_s[0] += fold(gate)

    pl.loop(2, 4)(conv_row)
    halo_up.wait()
    halo_down.wait()

    @pl.when(row == 0)
    def _():
        x_s[0] = jnp.zeros((64, WIDE), f32)

    @pl.when(row == rows - 1)
    def _():
        x_s[5] = jnp.zeros((64, WIDE), f32)

    expand_row(0)
    expand_row(5)

    conv_row(1)
    conv_row(4)

    eye = lax.broadcasted_iota(jnp.int32, (64, 128), 0) == lax.broadcasted_iota(
        jnp.int32, (64, 128), 1
    )

    def to_column(vector):
        spread_out = jnp.broadcast_to(vector, (64, vector.shape[1]))
        return jnp.sum(
            jnp.where(eye[:, : vector.shape[1]], spread_out, 0.0), axis=1, keepdims=True
        )

    def to_row(column):
        return jnp.sum(
            jnp.where(eye, jnp.broadcast_to(column, (64, 128)), 0.0), axis=0, keepdims=True
        )

    pool_s[row] = to_row(jnp.sum(fold_s[0], axis=1, keepdims=True))
    links = spread(0, lambda step: pool_s.at[row], pool_s.at[row], in_row, rows)
    expand_b[...] = forward_parts(expand_w[...].T)
    up_f[...] = forward_parts(up_w[...])
    up_b[...] = forward_parts(up_w[...].T)
    for weight, forward, backward in (
        (squeeze_w, squeeze_f, squeeze_b),
        (down_w, down_f, down_b),
        (query_w, query_f.at[0], query_b.at[0]),
        (value_w, value_f.at[0], value_b.at[0]),
    ):
        forward[...] = forward_parts(weight[...].T)
        backward[...] = forward_parts(weight[...])
    bias = to_column(bias_w[...])
    branch = to_column(branch_w[...])
    ffn_scale = to_column(scale_w[...])
    cross = to_column(cross_w[...])
    tap_acc[...] = jnp.zeros_like(tap_acc)
    finish(links)

    pooled = jnp.sum(pool_s[...], axis=0) / area
    attention = jnp.sum(pool_w[...] * pooled[:, :64], axis=1, keepdims=True) + bias

    def tail_row(h):
        squeezed = dot_nn(squeeze_f[...], right_parts(g_s[h] * attention))
        t_s[h] = squeezed
        residual = x_s[h + 1] + branch * squeezed
        value, scale = normed(residual)
        n1_s[h] = value
        s1_s[h] = scale
        expanded = dot_nn(up_f[...], right_parts(value))
        e_s[h] = expanded
        shrunk = dot_nn(down_f[...], right_parts(expanded[:64] * expanded[64:]))
        u_s[h] = shrunk
        h_s[h] = residual + ffn_scale * shrunk

    hidden_sent = []
    for k in range(2):
        tail_row(theirs[k])
        hidden_sent.append(send(8 + k, h_s.at[theirs[k]], hp_s.at[k], partner))
    conv_up = send(6, cv_s.at[1], cv_s.at[5], above, row != 0, row != rows - 1)
    conv_down = send(7, cv_s.at[4], cv_s.at[0], below, row != rows - 1, row != 0)
    for k in range(2):
        tail_row(mine[k])

    finish(weights_sent)
    query_f[1] = forward_parts(queryp_s[...].T)
    query_b[1] = forward_parts(queryp_s[...])
    value_f[1] = forward_parts(valuep_s[...].T)
    value_b[1] = forward_parts(valuep_s[...])
    crossp = to_column(crossp_s[...])
    cotangent_sent.wait()

    sixteen = lax.broadcasted_iota(jnp.int32, (16, WIDE), 0)
    outside16 = lax.broadcasted_iota(jnp.int32, (16, WIDE), 1) >= cols
    ones16 = jnp.ones((16, WIDE), bf16)
    mask_left = jnp.where(
        sixteen == 0, jnp.where(outside16, -256.0, 0.0), jnp.where(sixteen == 1, 1.0, 0.0)
    ).astype(bf16)
    mask_right = jnp.where(
        sixteen == 0, 1.0, jnp.where((sixteen == 1) & outside16, -256.0, 0.0)
    ).astype(bf16)

    def attend_row(k):
        own, other = h_s[mine[k]], hp_s[k]
        own_up, other_up = c_s[mine[k]], cp_s[slots[k]]
        own_n, own_scale = normed(own)
        other_n, other_scale = normed(other)
        attn_s[k, 0] = own_n
        attn_s[k, 1] = other_n
        atts_s[k] = own_scale
        own_q = dot_nn(query_f[0], right_parts(own_n))
        other_q = dot_nn(query_f[1], right_parts(other_n))
        own_v = dot_nn(value_f[0], right_parts(own))
        other_v = dot_nn(value_f[1], right_parts(other))
        scores = dot_tn(
            jnp.concatenate([left_parts(own_q * 0.125), mask_left], axis=0),
            jnp.concatenate([right_parts(other_q), mask_right], axis=0),
        )
        weights = jnp.exp(scores)
        e_att[...] = weights
        w_high, w_low = halves(weights)

        def weighted(dot, values):
            high, low = halves(values)
            large = dot(jnp.concatenate([high, ones16, low], axis=0), w_high)
            small = dot(jnp.concatenate([high, ones16], axis=0), w_low)
            bottom = jnp.where(inside, large[64:65] + small[64:65], 1.0)
            return large[:64] + large[80:] + small[:64], 1.0 / bottom

        def through(dot, values, high_m, low_m):
            high, low = halves(values)
            large = dot(jnp.concatenate([high, low], axis=0), high_m)
            return large[:64] + large[64:] + dot(high, low_m)

        own_c, own_r = weighted(dot_nt, other_v)
        other_c, other_r = weighted(dot_nn, own_v)
        own_c = own_c * own_r
        other_c = other_c * other_r
        o_s[mine[k]] = own + cross * own_c
        op_s[k] = other + crossp * other_c
        own_d = cross * own_up * own_r
        other_d = crossp * other_up * other_r
        fold_s[4] += fold(own_up * own_c)
        fold_s[5] += fold(other_up * other_c)
        own_delta, own_delta_low = halves(-jnp.sum(own_d * own_c, axis=0, keepdims=True))
        other_delta, other_delta_low = halves(-jnp.sum(other_d * other_c, axis=0, keepdims=True))
        left_tail = jnp.where(
            sixteen == 0,
            own_delta.astype(f32),
            jnp.where(
                sixteen == 1, own_delta_low.astype(f32), jnp.where(sixteen < 4, 1.0, 0.0)
            ),
        ).astype(bf16)
        right_tail = jnp.where(
            sixteen == 2,
            other_delta.astype(f32),
            jnp.where(
                sixteen == 3, other_delta_low.astype(f32), jnp.where(sixteen < 2, 1.0, 0.0)
            ),
        ).astype(bf16)
        change = dot_tn(
            jnp.concatenate(
                [left_parts(jnp.concatenate([own_d, own_v], axis=0)), left_tail], axis=0
            ),
            jnp.concatenate(
                [right_parts(jnp.concatenate([other_v, other_d], axis=0)), right_tail], axis=0
            ),
        )
        ds_high, ds_low = halves(e_att[...] * change * 0.125)
        other_dv = through(dot_nn, own_d, w_high, w_low)
        other_dq = through(dot_nn, own_q, ds_high, ds_low)
        dn = dot_nn(query_b[1], right_parts(other_dq))
        dhp_s[k] = (
            other_up
            + dot_nn(value_b[1], right_parts(other_dv))
            + normed_back(dn, other_n, other_scale)
        )
        att_s[k, 1] = other_dq
        att_s[k, 3] = other_dv
        att_s[k, 2] = through(dot_nt, other_d, w_high, w_low)
        att_s[k, 0] = through(dot_nt, other_q, ds_high, ds_low)

    def own_back(k):
        dn = dot_nn(query_b[0], right_parts(att_s[k, 0]))
        dh_s[mine[k]] = (
            c_s[mine[k]]
            + dot_nn(value_b[0], right_parts(att_s[k, 2]))
            + normed_back(dn, attn_s[k, 0], atts_s[k])
        )

    returned = []
    for k in range(2):
        hidden_sent[k].wait()
        attend_row(k)
        returned.append(send(10 + k, dhp_s.at[k], dh_s.at[mine[k]], partner))

    def tail_back_row(h):
        up = dh_s[h]
        expanded = e_s[h]
        dgate = dot_nn(down_b[...], right_parts(ffn_scale * up))
        de = jnp.concatenate([dgate * expanded[64:], dgate * expanded[:64]], axis=0)
        de_s[h] = de
        dn = dot_nn(up_b[...], right_parts(de))
        dr = up + normed_back(dn, n1_s[h], s1_s[h])
        dr_s[h] = dr
        dscaled = dot_nn(squeeze_b[...], right_parts(branch * dr))
        fold_s[3] += fold(dscaled * g_s[h])
        dg_s[h + 1] = dscaled * attention

    own_back(0)
    tail_back_row(mine[0])
    gate_mine = send(
        12, dg_s.at[mine[0] + 1], dg_s.at[5 - 5 * view], mine_side, row != edge, row != other_edge
    )
    own_back(1)
    tail_back_row(mine[1])

    returned[0].wait()
    tail_back_row(theirs[0])
    gate_theirs = send(
        13, dg_s.at[theirs[0] + 1], dg_s.at[5 * view], theirs_side, row != other_edge, row != edge
    )
    returned[1].wait()
    tail_back_row(theirs[1])

    d_attention = jnp.sum(fold_s[3], axis=1, keepdims=True)
    poolg_s[row, :, :64] = jnp.sum(pool_w[...] * d_attention, axis=0, keepdims=True)
    poolg_s[row, :, 64:] = jnp.zeros((1, 64), f32)
    links = spread(1, lambda step: poolg_s.at[row], poolg_s.at[row], in_row, rows)
    out_sent = [send(14 + k, op_s.at[k], o_s.at[mine[k]], partner) for k in range(2)]

    query_grads = [jnp.zeros((64, 64), f32)] * 4
    for k in range(2):
        fields = (attn_s[k, 0], attn_s[k, 1], h_s[mine[k]], hp_s[k])
        for item in range(4):
            query_grads[item] = query_grads[item] + over_pixels(att_s[k, item], fields[item])
    for start, pair in ((128, query_grads[:2]), (192, query_grads[2:])):
        early[start : start + 64, :64] = jnp.where(view == 0, pair[0], pair[1])
        early[start : start + 64, 64:] = jnp.where(view == 0, pair[1], pair[0])
    early[:128, :] = jnp.zeros((128, 128), f32)

    @pl.loop(0, 4)
    def _(h):
        up = dh_s[h]
        dr = dr_s[h]
        fold_s[1] += fold(up * u_s[h])
        fold_s[2] += fold(dr * t_s[h])
        expanded = e_s[h]
        early[:64, :] += over_pixels(n1_s[h], de_s[h])
        early[64:128, :64] += over_pixels(branch * dr, g_s[h] * attention)
        early[64:128, 64:] += over_pixels(ffn_scale * up, expanded[:64] * expanded[64:])

    early_size, late_size = 256 // rows, 128 // lanes

    def chunk_at(index, size):
        return pl.ds(pl.multiple_of(index * size, 8), size)

    early_links = spread(
        2,
        lambda step: early.at[chunk_at(lax.rem(row + step, rows), early_size)],
        early_1.at[row],
        in_row,
        rows,
    )
    early_1[row] = early[chunk_at(row, early_size), :]
    finish(links)

    constant = to_column(jnp.sum(poolg_s[...], axis=0) / area)

    def gate_back_row(h):
        total = dg_s[h] + constant
        dcv_s[h, :64, :] = total * cv_s[h, 64:, :]
        dcv_s[h, 64:, :] = total * cv_s[h, :64, :]

    pl.loop(1, 5)(gate_back_row)
    gate_mine.wait()
    gate_theirs.wait()
    conv_up.wait()
    conv_down.wait()
    for outer, limit in ((0, 0), (5, rows - 1)):

        @pl.when(row == limit)
        def _():
            dcv_s[outer] = jnp.zeros((128, WIDE), f32)

        @pl.when(row != limit)
        def _():
            gate_back_row(outer)

    @pl.loop(0, 8)
    def _(chunk):
        start = pl.multiple_of(chunk * 16, 16)
        size = 16
        for h in range(1, 5):
            center = dcv_s[h, pl.ds(start, size), :]
            moved = [pltpu.roll(center, WIDE - 1, 1), center, pltpu.roll(center, 1, 1)]
            for i in range(3):
                value = d_s[h + i - 1, pl.ds(start, size), :]
                for j in range(3):
                    tap_acc[3 * i + j, pl.ds(start, size), :] += fold(moved[j] * value)
        for h in range(1, 5):
            columns = [jnp.zeros((size, WIDE), f32)] * 3
            for i in range(3):
                value = dcv_s[h - i + 1, pl.ds(start, size), :]
                for j in range(3):
                    columns[j] = columns[j] + tap_at(3 * i + j, start, size) * value
            cv_s[h, pl.ds(start, size), :] = (
                columns[1] + pltpu.roll(columns[2], 1, 1) + pltpu.roll(columns[0], WIDE - 1, 1)
            )

    late[:64, :] = jnp.zeros((64, 128), f32)

    @pl.loop(0, 4)
    def _(h):
        late[:64, :] += over_pixels(n0_s[h], cv_s[h + 1])

    place = lax.broadcasted_iota(jnp.int32, (64, 128), 1)

    def columns_of(value):
        return jnp.sum(value, axis=1, keepdims=True)

    items = [columns_of(tap_acc[tap, :64, :]) for tap in range(9)]
    items += [columns_of(tap_acc[tap, 64:, :]) for tap in range(9)]
    items += [d_attention, columns_of(fold_s[2]), columns_of(fold_s[1])]
    own_cross = columns_of(fold_s[4])
    other_cross = columns_of(fold_s[5])
    items.append(jnp.where(view == 0, own_cross, other_cross))
    items.append(jnp.where(view == 0, other_cross, own_cross))
    mixed = d_attention * pooled
    for index, item in enumerate(items):
        mixed = jnp.where(place == 64 + index, item, mixed)
    late[64:, :] = mixed

    late_links = spread(
        5,
        lambda step: late.at[chunk_at(lax.rem(lane + step, lanes), late_size)],
        late_1.at[lane],
        in_lane,
        lanes,
    )
    late_1[lane] = late[chunk_at(lane, late_size), :]
    finish(early_links)

    early_2[lane] = jnp.sum(early_1[...], axis=0)
    early_links = spread(3, lambda step: early_2.at[lane], early_2.at[lane], in_lane, lanes)

    @pl.loop(0, 4)
    def _(h):
        dn = dot_nn(expand_b[...], right_parts(cv_s[h + 1]))
        dr_s[h] = dr_s[h] + normed_back(dn, n0_s[h], s0_s[h])

    finish(early_links)
    early_3[row] = jnp.sum(early_2[...], axis=0) * factor
    early_links = spread(4, lambda step: early_3.at[row], early_3.at[row], in_row, rows)
    finish(late_links)

    late_2[row] = jnp.sum(late_1[...], axis=0)
    late_links = spread(6, lambda step: late_2.at[row], late_2.at[row], in_row, rows)
    for h in range(4):
        grad_ref[:, h, :] = dr_s[h, :, :cols]
    stored = [pltpu.make_async_copy(grad_ref, grad_hbm, loads.at[14])]
    stored[0].start()
    finish(out_sent)
    for h in range(4):
        out_ref[:, h, :] = o_s[h, :, :cols]
    stored.append(pltpu.make_async_copy(out_ref, out_hbm, loads.at[15]))
    stored[1].start()
    finish(late_links)

    late_3[lane] = jnp.sum(late_2[...], axis=0) * factor
    late_links = spread(7, lambda step: late_3.at[lane], late_3.at[lane], in_lane, lanes)
    finish(early_links)
    early_ref[...] = early_3[...]
    finish(late_links)
    late_ref[...] = late_3[...]
    for copy in stored:
        copy.wait()


def format_kernel(out_in, grad_in, early_ref, late_ref, *refs):
    (
        out_ref, grad_ref, expand_ref, taps_ref, pool_ref, bias_ref, squeeze_ref, branch_ref,
        up_ref, down_ref, scale_ref, query_ref, value_ref, cross_ref,
    ) = refs
    out_ref[...] = out_in[...]
    grad_ref[...] = grad_in[...]
    view = lax.axis_index("view")
    up_ref[...] = early_ref[:64, :]
    middle = early_ref[64:128, :]
    squeeze_ref[...] = middle[:, :64]
    down_ref[...] = middle[:, 64:]
    for start, target in ((128, query_ref), (192, value_ref)):
        both = early_ref[start : start + 64, :]
        target[...] = jnp.where(view == 0, both[:, :64], both[:, 64:])
    expand_ref[...] = late_ref[:64, :]
    mixed = late_ref[64:, :]
    pool_ref[...] = mixed[:, :64]
    turned = mixed.T
    for tap in range(9):
        taps_ref[tap // 3, tap % 3 : tap % 3 + 1, :64] = turned[64 + tap : 65 + tap, :]
        taps_ref[tap // 3, tap % 3 : tap % 3 + 1, 64:] = turned[73 + tap : 74 + tap, :]
    for place, target in ((82, bias_ref), (83, branch_ref), (84, scale_ref)):
        target[...] = turned[place : place + 1, :]
    cross_ref[...] = jnp.where(view == 0, turned[85:86, :], turned[86:87, :])


def per_device(rows, lanes, *arrays):
    cols = arrays[0].shape[4]
    area = 4 * rows * cols
    factor = (lanes * area) ** (-0.5)
    wide = functools.partial(jax.ShapeDtypeStruct, dtype=f32)

    def fields(*shape):
        return pltpu.VMEM(shape, f32)

    def parts(*shape):
        return pltpu.VMEM(shape, bf16)

    operands = [
        arrays[0][0, 0],
        arrays[1][0, 0],
        arrays[2].T,
        arrays[3].transpose(1, 2, 0),
        arrays[4],
        arrays[5][None],
        arrays[6],
        arrays[7][None],
        arrays[8].T,
        arrays[9],
        arrays[10][None],
        arrays[11][0],
        arrays[12][0],
        arrays[13],
    ]
    early_size, late_size = 256 // rows, 128 // lanes
    scratch = [fields(*operand.shape) for operand in operands] + [
        fields(6, 64, WIDE),
        fields(4, 64, WIDE),
        fields(2, 64, WIDE),
        fields(4, 64, WIDE),
        fields(4, 1, WIDE),
        fields(6, 128, WIDE),
        fields(6, 128, WIDE),
        fields(4, 64, WIDE),
        fields(4, 64, WIDE),
        fields(4, 64, WIDE),
        fields(4, 1, WIDE),
        fields(4, 128, WIDE),
        fields(4, 64, WIDE),
        fields(4, 64, WIDE),
        fields(2, 64, WIDE),
        fields(4, 64, WIDE),
        fields(2, 64, WIDE),
        fields(4, 64, WIDE),
        fields(2, 64, WIDE),
        fields(6, 64, WIDE),
        fields(4, 64, WIDE),
        fields(4, 128, WIDE),
        fields(6, 128, WIDE),
        fields(WIDE, WIDE),
        fields(2, 4, 64, WIDE),
        fields(2, 2, 64, WIDE),
        fields(2, 1, WIDE),
        fields(9, 128, 128),
        fields(6, 64, 128),
        fields(9, 128, 128),
        fields(64, 64),
        fields(64, 64),
        fields(1, 64),
        fields(rows, 1, 128),
        fields(rows, 1, 128),
        fields(256, 128),
        fields(128, 128),
        fields(rows, early_size, 128),
        fields(lanes, early_size, 128),
        fields(rows, early_size, 128),
        fields(lanes, late_size, 128),
        fields(rows, late_size, 128),
        fields(lanes, late_size, 128),
        parts(128, 192),
        parts(64, 384),
        parts(64, 192),
        parts(64, 192),
        parts(128, 192),
        parts(64, 384),
        parts(64, 192),
        parts(64, 192),
        parts(2, 64, 192),
        parts(2, 64, 192),
        parts(2, 64, 192),
        parts(2, 64, 192),
        fields(64, 4, cols),
        fields(64, 4, cols),
        pltpu.SemaphoreType.DMA((16,)),
        pltpu.SemaphoreType.DMA((16,)),
        pltpu.SemaphoreType.DMA((16,)),
        pltpu.SemaphoreType.DMA((8, 15)),
        pltpu.SemaphoreType.DMA((8, 15)),
    ]
    in_place = pl.BlockSpec(memory_space=pl.ANY)
    in_vmem = pl.BlockSpec(memory_space=pltpu.VMEM)
    out, grad, early, late = pl.pallas_call(
        functools.partial(block_kernel, (rows, lanes), factor, area, cols),
        out_shape=(
            wide((64, 4, cols)),
            wide((64, 4, cols)),
            wide((rows, early_size, 128)),
            wide((lanes, late_size, 128)),
        ),
        in_specs=[in_place] * 14,
        out_specs=(in_place, in_place, in_vmem, in_vmem),
        scratch_shapes=scratch,
        compiler_params=pltpu.CompilerParams(
            collective_id=0, has_side_effects=True, vmem_limit_bytes=56 * 2**20
        ),
    )(*operands)
    shapes = [operand.shape for operand in operands]
    done = pl.pallas_call(
        format_kernel,
        out_shape=[wide(shape) for shape in shapes],
        in_specs=[in_vmem] * 4,
        out_specs=[in_vmem] * 14,
    )(out, grad, early.reshape(256, 128), late.reshape(128, 128))
    return (
        done[0][None, None],
        done[1][None, None],
        done[2].T,
        done[3].transpose(2, 0, 1),
        done[4],
        done[5][0],
        done[6],
        done[7][0],
        done[8].T,
        done[9],
        done[10][0],
        done[11][None],
        done[12][None],
        done[13],
    )


def solution(mesh):
    field = P("view", "dp", None, "row", None)
    copied = (P(),) * 9
    owned = (P("view", None, None), P("view", None, None), P("view", None))
    return jax.shard_map(
        functools.partial(per_device, mesh.shape["row"], 2 * mesh.shape["dp"]),
        mesh=mesh,
        in_specs=(field, field) + copied + owned,
        out_specs=(field, field) + copied + owned,
        check_vma=False,
    )
```

```python
import functools

import jax
import jax.numpy as jnp
from jax import lax
from jax.experimental import pallas as pl
from jax.experimental.pallas import tpu as pltpu
from jax.sharding import PartitionSpec as P

epsilon = 1e-06
WIDE = 512
f32 = jnp.float32
bf16 = jnp.bfloat16
MESH = pl.DeviceIdType.MESH


def halves(x):
    high = x.astype(bf16)
    return high, (x - high.astype(f32)).astype(bf16)


def left_parts(x):
    high, low = halves(x)
    return jnp.concatenate([high, low, high], axis=0)


def right_parts(x):
    high, low = halves(x)
    return jnp.concatenate([high, high, low], axis=0)


def dot_nn(a, b):
    return lax.dot_general(a, b, (((1,), (0,)), ((), ())), preferred_element_type=f32)


def dot_nt(a, b):
    return lax.dot_general(a, b, (((1,), (1,)), ((), ())), preferred_element_type=f32)


def dot_tn(a, b):
    return lax.dot_general(a, b, (((0,), (0,)), ((), ())), preferred_element_type=f32)


def over_pixels(a, b):
    a_high, a_low = halves(a)
    b_high, b_low = halves(b)
    return dot_nt(
        jnp.concatenate([a_high, a_low, a_high], axis=1),
        jnp.concatenate([b_high, b_high, b_low], axis=1),
    )


def fold(x):
    return x[:, :128] + x[:, 128:256] + x[:, 256:384] + x[:, 384:]


class Link:
    def __init__(self, copy, sends=None, receives=None):
        self.copy, self.sends, self.receives = copy, sends, receives
        if sends is None:
            copy.start()
        else:
            pl.when(sends)(copy.start)

    def wait(self):
        if self.sends is None:
            self.copy.wait()
        else:
            pl.when(self.receives)(self.copy.wait_recv)
            pl.when(self.sends)(self.copy.wait_send)


def normed(x):
    center = x - jnp.mean(x, axis=0, keepdims=True)
    scale = 1.0 / jnp.sqrt(jnp.mean(center * center, axis=0, keepdims=True) + epsilon)
    return center * scale, scale


def normed_back(grad, value, scale):
    return scale * (
        grad
        - jnp.mean(grad, axis=0, keepdims=True)
        - value * jnp.mean(grad * value, axis=0, keepdims=True)
    )


def far_first(count, ring):
    def hops(step):
        near = step % 8 if ring else step // 4
        around = 8 if ring else 4
        return min(near, around - near)

    return sorted(range(1, count), key=lambda step: -hops(step))


def block_kernel(sizes, factor, area, cols, *refs):
    operands, results, refs = refs[:14], refs[14:18], refs[18:]
    out_hbm, grad_hbm, early_ref, late_ref = results
    (
        x_in, c_in, expand_w, taps_w, pool_w, bias_w, squeeze_w, branch_w,
        up_w, down_w, scale_w, query_w, value_w, cross_w,
    ) = refs[:14]
    (
        x_s, c_s, cp_s, n0_s, s0_s, d_s, cv_s, g_s, t_s, n1_s, s1_s, e_s, u_s, h_s,
        hp_s, dh_s, dhp_s, o_s, op_s, dg_s, dr_s, de_s, dcv_s, e_att, att_s, attn_s, atts_s,
        taps_s, fold_s, tap_acc, y_s, w_s, queryp_s, valuep_s, crossp_s, pool_s, poolg_s,
        early, late, early_1, early_2, early_3, late_1, late_2, late_3,
        expand_f, expand_b, squeeze_f, squeeze_b, up_f, up_b, down_f, down_b,
        query_f, query_b, value_f, value_b,
        out_ref, grad_ref, loads, sends, recvs, group_sends, group_recvs,
    ) = refs[14:]
    rows, lanes = sizes
    row = lax.axis_index("row")
    view = lax.axis_index("view")
    lane = lax.axis_index("dp") * 2 + view
    mine = (3 * view, 1 + view)
    theirs = (3 - 3 * view, 2 - view)
    slots = (view, 1 - view)
    edge = view * (rows - 1)
    other_edge = rows - 1 - edge

    def in_row(step):
        return {"row": lax.rem(row + step, rows)}

    def in_lane(step):
        other = lax.rem(lane + step, lanes)
        return {"dp": other // 2, "view": lax.rem(other, 2)}

    above = in_row(rows - 1)
    below = in_row(1)
    mine_side = in_row((1 - view) * (rows - 1) + view)
    theirs_side = in_row(view * (rows - 1) + 1 - view)
    partner = {"view": 1 - view}

    barrier = pltpu.get_barrier_semaphore()
    for step in far_first(rows, True):
        pl.semaphore_signal(barrier, inc=1, device_id=in_row(step), device_id_type=MESH)
    for step in far_first(lanes, False):
        pl.semaphore_signal(barrier, inc=1, device_id=in_lane(step), device_id_type=MESH)

    local = [
        pltpu.make_async_copy(operands[item], refs[item], loads.at[item]) for item in range(14)
    ]
    for item in (0, 2, 3, 4, 5, 6, 7, 8, 9, 10, 11, 12, 13, 1):
        local[item].start()

    def send(index, source, target, device, *when):
        return Link(
            pltpu.make_async_remote_copy(
                src_ref=source,
                dst_ref=target,
                send_sem=sends.at[index],
                recv_sem=recvs.at[index],
                device_id=device,
                device_id_type=MESH,
            ),
            *when,
        )

    def spread(phase, source, target, device, count):
        return [
            Link(
                pltpu.make_async_remote_copy(
                    src_ref=source(step),
                    dst_ref=target,
                    send_sem=group_sends.at[phase, step - 1],
                    recv_sem=group_recvs.at[phase, step - 1],
                    device_id=device(step),
                    device_id_type=MESH,
                )
            )
            for step in far_first(count, device is in_row)
        ]

    def finish(links):
        for link in links:
            link.wait()

    for h in range(4):
        x_s[h + 1, :, 384:] = jnp.zeros((64, 128), f32)
    local[0].wait()
    for h in (0, 3, 1, 2):
        x_s[h + 1, :, :cols] = x_in[:, h, :]

    pl.semaphore_wait(barrier, rows + lanes - 2)
    halo_up = send(0, x_s.at[1], x_s.at[5], above, row != 0, row != rows - 1)
    halo_down = send(1, x_s.at[4], x_s.at[0], below, row != rows - 1, row != 0)

    def forward_parts(transposed):
        return left_parts(transposed).astype(f32).T.astype(bf16)

    for item in range(2, 14):
        local[item].wait()
    weights_sent = [
        send(2, query_w, queryp_s, partner),
        send(3, value_w, valuep_s, partner),
        send(4, cross_w, crossp_s, partner),
    ]
    expand_f[...] = forward_parts(expand_w[...])

    def expand_row(h):
        value, scale = normed(x_s[h])
        d_s[h] = dot_nn(expand_f[...], right_parts(value))
        return value, scale

    @pl.loop(1, 5)
    def _(h):
        value, scale = expand_row(h)
        n0_s[h] = value
        s0_s[h - 1] = scale

    tap_rows = jnp.concatenate(
        [taps_w[i, j : j + 1, :] for i in range(3) for j in range(3)]
        + [jnp.zeros((7, 128), f32)],
        axis=0,
    )
    tap_columns = tap_rows.T
    for tap in range(9):
        taps_s[tap] = jnp.broadcast_to(tap_columns[:, tap : tap + 1], (128, 128))
    for h in range(4):
        c_s[h, :, 384:] = jnp.zeros((64, 128), f32)
    local[1].wait()
    for h in range(4):
        c_s[h, :, :cols] = c_in[:, h, :]

    cotangent_sent = send(5, c_s.at[pl.ds(2 - 2 * view, 2)], cp_s, partner)

    inside = lax.broadcasted_iota(jnp.int32, (1, WIDE), 1) < cols
    fold_s[...] = jnp.zeros_like(fold_s)

    def tap_at(tap, start, size):
        piece = taps_s[tap, pl.ds(start, size), :]
        return jnp.concatenate([piece] * 4, axis=1)

    def conv_row(h):
        for start in range(0, 128, 16):
            columns = [jnp.zeros((16, WIDE), f32)] * 3
            for i in range(3):
                value = d_s[h + i - 1, start : start + 16, :]
                for j in range(3):
                    columns[j] = columns[j] + tap_at(3 * i + j, start, 16) * value
            total = columns[1] + pltpu.roll(columns[0], 1, 1) + pltpu.roll(columns[2], WIDE - 1, 1)
            cv_s[h, start : start + 16, :] = jnp.where(inside, total, 0.0)
        gate = cv_s[h, :64, :] * cv_s[h, 64:, :]
        g_s[h - 1] = gate
        fold_s[0] += fold(gate)

    pl.loop(2, 4)(conv_row)
    halo_up.wait()
    halo_down.wait()

    @pl.when(row == 0)
    def _():
        x_s[0] = jnp.zeros((64, WIDE), f32)

    @pl.when(row == rows - 1)
    def _():
        x_s[5] = jnp.zeros((64, WIDE), f32)

    for h in (0, 5):
        value, _ = expand_row(h)
        n0_s[h] = value

    conv_row(1)
    conv_row(4)

    eye = lax.broadcasted_iota(jnp.int32, (64, 128), 0) == lax.broadcasted_iota(
        jnp.int32, (64, 128), 1
    )

    def to_column(vector):
        spread_out = jnp.broadcast_to(vector, (64, vector.shape[1]))
        return jnp.sum(
            jnp.where(eye[:, : vector.shape[1]], spread_out, 0.0), axis=1, keepdims=True
        )

    def to_row(column):
        return jnp.sum(
            jnp.where(eye, jnp.broadcast_to(column, (64, 128)), 0.0), axis=0, keepdims=True
        )

    pool_s[row] = to_row(jnp.sum(fold_s[0], axis=1, keepdims=True))
    links = spread(0, lambda step: pool_s.at[row], pool_s.at[row], in_row, rows)
    expand_b[...] = forward_parts(expand_w[...].T)
    up_f[...] = forward_parts(up_w[...])
    up_b[...] = forward_parts(up_w[...].T)
    for weight, forward, backward in (
        (squeeze_w, squeeze_f, squeeze_b),
        (down_w, down_f, down_b),
        (query_w, query_f.at[0], query_b.at[0]),
        (value_w, value_f.at[0], value_b.at[0]),
    ):
        forward[...] = forward_parts(weight[...].T)
        backward[...] = forward_parts(weight[...])
    bias = to_column(bias_w[...])
    branch = to_column(branch_w[...])
    ffn_scale = to_column(scale_w[...])
    cross = to_column(cross_w[...])
    tap_acc[...] = jnp.zeros_like(tap_acc)
    w_s[...] = jnp.zeros_like(w_s)

    def conv_back(part):
        @pl.loop(0, 8)
        def _(chunk):
            size = 16
            start = pl.multiple_of(chunk * size, size)
            for h in range(1, 5):
                center = dcv_s[h, pl.ds(start, size), :]
                moved = [pltpu.roll(center, WIDE - 1, 1), center, pltpu.roll(center, 1, 1)]
                for i in range(3):
                    value = d_s[h + i - 1, pl.ds(start, size), :]
                    for j in range(3):
                        tap_acc[part, 3 * i + j, pl.ds(start, size), :] += fold(moved[j] * value)
            for h in range(6):
                columns = [jnp.zeros((size, WIDE), f32)] * 3
                for i in range(3):
                    if 1 <= h - i + 1 <= 4:
                        value = dcv_s[h - i + 1, pl.ds(start, size), :]
                        for j in range(3):
                            columns[j] = columns[j] + tap_at(3 * i + j, start, size) * value
                y_s[part, h, pl.ds(start, size), :] = (
                    columns[1]
                    + pltpu.roll(columns[2], 1, 1)
                    + pltpu.roll(columns[0], WIDE - 1, 1)
                )

    def expand_products(part):
        @pl.loop(0, 6)
        def _(h):
            w_s[part] += over_pixels(n0_s[h], y_s[part, h])

    @pl.loop(1, 5)
    def _(h):
        dcv_s[h, :64, :] = cv_s[h, 64:, :]
        dcv_s[h, 64:, :] = cv_s[h, :64, :]

    conv_back(0)
    finish(links)

    pooled = jnp.sum(pool_s[...], axis=0) / area
    attention = jnp.sum(pool_w[...] * pooled[:, :64], axis=1, keepdims=True) + bias

    def tail_row(h):
        squeezed = dot_nn(squeeze_f[...], right_parts(g_s[h] * attention))
        t_s[h] = squeezed
        residual = x_s[h + 1] + branch * squeezed
        value, scale = normed(residual)
        n1_s[h] = value
        s1_s[h] = scale
        expanded = dot_nn(up_f[...], right_parts(value))
        e_s[h] = expanded
        shrunk = dot_nn(down_f[...], right_parts(expanded[:64] * expanded[64:]))
        u_s[h] = shrunk
        h_s[h] = residual + ffn_scale * shrunk

    hidden_sent = []
    for k in range(2):
        tail_row(theirs[k])
        hidden_sent.append(send(8 + k, h_s.at[theirs[k]], hp_s.at[k], partner))
    conv_up = send(6, cv_s.at[1], cv_s.at[5], above, row != 0, row != rows - 1)
    conv_down = send(7, cv_s.at[4], cv_s.at[0], below, row != rows - 1, row != 0)
    for k in range(2):
        tail_row(mine[k])
    expand_products(0)

    finish(weights_sent)
    query_f[1] = forward_parts(queryp_s[...].T)
    query_b[1] = forward_parts(queryp_s[...])
    value_f[1] = forward_parts(valuep_s[...].T)
    value_b[1] = forward_parts(valuep_s[...])
    crossp = to_column(crossp_s[...])
    cotangent_sent.wait()

    sixteen = lax.broadcasted_iota(jnp.int32, (16, WIDE), 0)
    outside16 = lax.broadcasted_iota(jnp.int32, (16, WIDE), 1) >= cols
    ones16 = jnp.ones((16, WIDE), bf16)
    mask_left = jnp.where(
        sixteen == 0, jnp.where(outside16, -256.0, 0.0), jnp.where(sixteen == 1, 1.0, 0.0)
    ).astype(bf16)
    mask_right = jnp.where(
        sixteen == 0, 1.0, jnp.where((sixteen == 1) & outside16, -256.0, 0.0)
    ).astype(bf16)

    def attend_row(k):
        own, other = h_s[mine[k]], hp_s[k]
        own_up, other_up = c_s[mine[k]], cp_s[slots[k]]
        own_n, own_scale = normed(own)
        other_n, other_scale = normed(other)
        attn_s[k, 0] = own_n
        attn_s[k, 1] = other_n
        atts_s[k] = own_scale
        own_q = dot_nn(query_f[0], right_parts(own_n))
        other_q = dot_nn(query_f[1], right_parts(other_n))
        own_v = dot_nn(value_f[0], right_parts(own))
        other_v = dot_nn(value_f[1], right_parts(other))
        scores = dot_tn(
            jnp.concatenate([left_parts(own_q * 0.125), mask_left], axis=0),
            jnp.concatenate([right_parts(other_q), mask_right], axis=0),
        )
        weights = jnp.exp(scores)
        e_att[...] = weights
        w_high, w_low = halves(weights)

        def weighted(dot, values):
            high, low = halves(values)
            large = dot(jnp.concatenate([high, ones16, low], axis=0), w_high)
            small = dot(jnp.concatenate([high, ones16], axis=0), w_low)
            bottom = jnp.where(inside, large[64:65] + small[64:65], 1.0)
            return large[:64] + large[80:] + small[:64], 1.0 / bottom

        def through(dot, values, high_m, low_m):
            high, low = halves(values)
            large = dot(jnp.concatenate([high, low], axis=0), high_m)
            return large[:64] + large[64:] + dot(high, low_m)

        own_c, own_r = weighted(dot_nt, other_v)
        other_c, other_r = weighted(dot_nn, own_v)
        own_c = own_c * own_r
        other_c = other_c * other_r
        o_s[mine[k]] = own + cross * own_c
        op_s[k] = other + crossp * other_c
        own_d = cross * own_up * own_r
        other_d = crossp * other_up * other_r
        fold_s[4] += fold(own_up * own_c)
        fold_s[5] += fold(other_up * other_c)
        own_delta, own_delta_low = halves(-jnp.sum(own_d * own_c, axis=0, keepdims=True))
        other_delta, other_delta_low = halves(-jnp.sum(other_d * other_c, axis=0, keepdims=True))
        left_tail = jnp.where(
            sixteen == 0,
            own_delta.astype(f32),
            jnp.where(
                sixteen == 1, own_delta_low.astype(f32), jnp.where(sixteen < 4, 1.0, 0.0)
            ),
        ).astype(bf16)
        right_tail = jnp.where(
            sixteen == 2,
            other_delta.astype(f32),
            jnp.where(
                sixteen == 3, other_delta_low.astype(f32), jnp.where(sixteen < 2, 1.0, 0.0)
            ),
        ).astype(bf16)
        change = dot_tn(
            jnp.concatenate(
                [left_parts(jnp.concatenate([own_d, own_v], axis=0)), left_tail], axis=0
            ),
            jnp.concatenate(
                [right_parts(jnp.concatenate([other_v, other_d], axis=0)), right_tail], axis=0
            ),
        )
        ds_high, ds_low = halves(e_att[...] * change * 0.125)
        other_dv = through(dot_nn, own_d, w_high, w_low)
        other_dq = through(dot_nn, own_q, ds_high, ds_low)
        dn = dot_nn(query_b[1], right_parts(other_dq))
        dhp_s[k] = (
            other_up
            + dot_nn(value_b[1], right_parts(other_dv))
            + normed_back(dn, other_n, other_scale)
        )
        att_s[k, 1] = other_dq
        att_s[k, 3] = other_dv
        att_s[k, 2] = through(dot_nt, other_d, w_high, w_low)
        att_s[k, 0] = through(dot_nt, other_q, ds_high, ds_low)

    def own_back(k):
        dn = dot_nn(query_b[0], right_parts(att_s[k, 0]))
        dh_s[mine[k]] = (
            c_s[mine[k]]
            + dot_nn(value_b[0], right_parts(att_s[k, 2]))
            + normed_back(dn, attn_s[k, 0], atts_s[k])
        )

    returned = []
    for k in range(2):
        hidden_sent[k].wait()
        attend_row(k)
        returned.append(send(10 + k, dhp_s.at[k], dh_s.at[mine[k]], partner))

    def tail_back_row(h):
        up = dh_s[h]
        expanded = e_s[h]
        dgate = dot_nn(down_b[...], right_parts(ffn_scale * up))
        de = jnp.concatenate([dgate * expanded[64:], dgate * expanded[:64]], axis=0)
        de_s[h] = de
        dn = dot_nn(up_b[...], right_parts(de))
        dr = up + normed_back(dn, n1_s[h], s1_s[h])
        dr_s[h] = dr
        dscaled = dot_nn(squeeze_b[...], right_parts(branch * dr))
        fold_s[3] += fold(dscaled * g_s[h])
        dg_s[h + 1] = dscaled * attention

    own_back(0)
    tail_back_row(mine[0])
    gate_mine = send(
        12, dg_s.at[mine[0] + 1], dg_s.at[5 - 5 * view], mine_side, row != edge, row != other_edge
    )
    own_back(1)
    tail_back_row(mine[1])

    query_grads = [jnp.zeros((64, 64), f32)] * 4
    for k in range(2):
        fields = (attn_s[k, 0], attn_s[k, 1], h_s[mine[k]], hp_s[k])
        for item in range(4):
            query_grads[item] = query_grads[item] + over_pixels(att_s[k, item], fields[item])
    for start, pair in ((128, query_grads[:2]), (192, query_grads[2:])):
        early[start : start + 64, :64] = jnp.where(view == 0, pair[0], pair[1])
        early[start : start + 64, 64:] = jnp.where(view == 0, pair[1], pair[0])

    returned[0].wait()
    tail_back_row(theirs[0])
    gate_theirs = send(
        13, dg_s.at[theirs[0] + 1], dg_s.at[5 * view], theirs_side, row != other_edge, row != edge
    )
    returned[1].wait()
    tail_back_row(theirs[1])

    d_attention = jnp.sum(fold_s[3], axis=1, keepdims=True)
    poolg = jnp.sum(pool_w[...] * d_attention, axis=0, keepdims=True)
    poolg_s[row, :, :64] = poolg
    poolg_s[row, :, 64:] = poolg
    links = spread(1, lambda step: poolg_s.at[row], poolg_s.at[row], in_row, rows)
    out_sent = [send(14 + k, op_s.at[k], o_s.at[mine[k]], partner) for k in range(2)]

    early[:128, :] = jnp.zeros((128, 128), f32)

    @pl.loop(0, 4)
    def _(h):
        up = dh_s[h]
        dr = dr_s[h]
        fold_s[1] += fold(up * u_s[h])
        fold_s[2] += fold(dr * t_s[h])
        expanded = e_s[h]
        early[:64, :] += over_pixels(n1_s[h], de_s[h])
        early[64:128, :64] += over_pixels(branch * dr, g_s[h] * attention)
        early[64:128, 64:] += over_pixels(ffn_scale * up, expanded[:64] * expanded[64:])

    early_size, late_size = 256 // rows, 128 // lanes

    def chunk_at(index, size):
        return pl.ds(pl.multiple_of(index * size, 8), size)

    early_links = spread(
        2,
        lambda step: early.at[chunk_at(lax.rem(row + step, rows), early_size)],
        early_1.at[row],
        in_row,
        rows,
    )
    early_1[row] = early[chunk_at(row, early_size), :]

    @pl.loop(1, 5)
    def _(h):
        dcv_s[h, :64, :] = dg_s[h] * cv_s[h, 64:, :]
        dcv_s[h, 64:, :] = dg_s[h] * cv_s[h, :64, :]

    conv_back(1)
    expand_products(1)
    finish(links)

    constants = jnp.sum(poolg_s[...], axis=0) / area
    constant = to_column(constants)
    late[:64, :] = w_s[1] + w_s[0] * constants

    place = lax.broadcasted_iota(jnp.int32, (64, 128), 1)

    def columns_of(value):
        return jnp.sum(value, axis=1, keepdims=True)

    items = [
        columns_of(tap_acc[1, tap, start : start + 64, :])
        + constant * columns_of(tap_acc[0, tap, start : start + 64, :])
        for start in (0, 64)
        for tap in range(9)
    ]
    items += [d_attention, columns_of(fold_s[2]), columns_of(fold_s[1])]
    own_cross = columns_of(fold_s[4])
    other_cross = columns_of(fold_s[5])
    items.append(jnp.where(view == 0, own_cross, other_cross))
    items.append(jnp.where(view == 0, other_cross, own_cross))
    mixed = d_attention * pooled
    for index, item in enumerate(items):
        mixed = jnp.where(place == 64 + index, item, mixed)
    late[64:, :] = mixed

    late_links = spread(
        5,
        lambda step: late.at[chunk_at(lax.rem(lane + step, lanes), late_size)],
        late_1.at[lane],
        in_lane,
        lanes,
    )
    late_1[lane] = late[chunk_at(lane, late_size), :]
    finish(early_links)

    early_2[lane] = jnp.sum(early_1[...], axis=0)
    early_links = spread(3, lambda step: early_2.at[lane], early_2.at[lane], in_lane, lanes)

    gate_mine.wait()
    gate_theirs.wait()
    conv_up.wait()
    conv_down.wait()
    constant_both = jnp.concatenate([constant, constant], axis=0)

    @pl.loop(1, 5)
    def _(h):
        y_s[1, h] += constant_both * y_s[0, h]

    for outer, limit, target, i in ((0, 0, 1, 2), (5, rows - 1, 4, 0)):

        @pl.when(row != limit)
        def _():
            total = dg_s[outer] + constant
            dcv_s[outer, :64, :] = total * cv_s[outer, 64:, :]
            dcv_s[outer, 64:, :] = total * cv_s[outer, :64, :]
            for start in range(0, 128, 16):
                value = dcv_s[outer, start : start + 16, :]
                columns = [tap_at(3 * i + j, start, 16) * value for j in range(3)]
                y_s[1, target, start : start + 16, :] += (
                    columns[1]
                    + pltpu.roll(columns[2], 1, 1)
                    + pltpu.roll(columns[0], WIDE - 1, 1)
                )

    @pl.loop(0, 4)
    def _(h):
        dn = dot_nn(expand_b[...], right_parts(y_s[1, h + 1]))
        dr_s[h] = dr_s[h] + normed_back(dn, n0_s[h + 1], s0_s[h])

    finish(early_links)
    early_3[row] = jnp.sum(early_2[...], axis=0) * factor
    early_links = spread(4, lambda step: early_3.at[row], early_3.at[row], in_row, rows)
    finish(late_links)

    late_2[row] = jnp.sum(late_1[...], axis=0)
    late_links = spread(6, lambda step: late_2.at[row], late_2.at[row], in_row, rows)
    for h in range(4):
        grad_ref[:, h, :] = dr_s[h, :, :cols]
    stored = [pltpu.make_async_copy(grad_ref, grad_hbm, loads.at[14])]
    stored[0].start()
    finish(out_sent)
    for h in range(4):
        out_ref[:, h, :] = o_s[h, :, :cols]
    stored.append(pltpu.make_async_copy(out_ref, out_hbm, loads.at[15]))
    stored[1].start()
    finish(late_links)

    late_3[lane] = jnp.sum(late_2[...], axis=0) * factor
    late_links = spread(7, lambda step: late_3.at[lane], late_3.at[lane], in_lane, lanes)
    finish(early_links)
    early_ref[...] = early_3[...]
    finish(late_links)
    late_ref[...] = late_3[...]
    for copy in stored:
        copy.wait()


def format_kernel(out_in, grad_in, early_ref, late_ref, *refs):
    (
        out_ref, grad_ref, expand_ref, taps_ref, pool_ref, bias_ref, squeeze_ref, branch_ref,
        up_ref, down_ref, scale_ref, query_ref, value_ref, cross_ref,
    ) = refs
    out_ref[...] = out_in[...]
    grad_ref[...] = grad_in[...]
    view = lax.axis_index("view")
    up_ref[...] = early_ref[:64, :]
    middle = early_ref[64:128, :]
    squeeze_ref[...] = middle[:, :64]
    down_ref[...] = middle[:, 64:]
    for start, target in ((128, query_ref), (192, value_ref)):
        both = early_ref[start : start + 64, :]
        target[...] = jnp.where(view == 0, both[:, :64], both[:, 64:])
    expand_ref[...] = late_ref[:64, :]
    mixed = late_ref[64:, :]
    pool_ref[...] = mixed[:, :64]
    turned = mixed.T
    for tap in range(9):
        taps_ref[tap // 3, tap % 3 : tap % 3 + 1, :64] = turned[64 + tap : 65 + tap, :]
        taps_ref[tap // 3, tap % 3 : tap % 3 + 1, 64:] = turned[73 + tap : 74 + tap, :]
    for place, target in ((82, bias_ref), (83, branch_ref), (84, scale_ref)):
        target[...] = turned[place : place + 1, :]
    cross_ref[...] = jnp.where(view == 0, turned[85:86, :], turned[86:87, :])


def per_device(rows, lanes, *arrays):
    cols = arrays[0].shape[4]
    area = 4 * rows * cols
    factor = (lanes * area) ** (-0.5)
    wide = functools.partial(jax.ShapeDtypeStruct, dtype=f32)

    def fields(*shape):
        return pltpu.VMEM(shape, f32)

    def parts(*shape):
        return pltpu.VMEM(shape, bf16)

    operands = [
        arrays[0][0, 0],
        arrays[1][0, 0],
        arrays[2].T,
        arrays[3].transpose(1, 2, 0),
        arrays[4],
        arrays[5][None],
        arrays[6],
        arrays[7][None],
        arrays[8].T,
        arrays[9],
        arrays[10][None],
        arrays[11][0],
        arrays[12][0],
        arrays[13],
    ]
    early_size, late_size = 256 // rows, 128 // lanes
    scratch = [fields(*operand.shape) for operand in operands] + [
        fields(6, 64, WIDE),
        fields(4, 64, WIDE),
        fields(2, 64, WIDE),
        fields(6, 64, WIDE),
        fields(4, 1, WIDE),
        fields(6, 128, WIDE),
        fields(6, 128, WIDE),
        fields(4, 64, WIDE),
        fields(4, 64, WIDE),
        fields(4, 64, WIDE),
        fields(4, 1, WIDE),
        fields(4, 128, WIDE),
        fields(4, 64, WIDE),
        fields(4, 64, WIDE),
        fields(2, 64, WIDE),
        fields(4, 64, WIDE),
        fields(2, 64, WIDE),
        fields(4, 64, WIDE),
        fields(2, 64, WIDE),
        fields(6, 64, WIDE),
        fields(4, 64, WIDE),
        fields(4, 128, WIDE),
        fields(6, 128, WIDE),
        fields(WIDE, WIDE),
        fields(2, 4, 64, WIDE),
        fields(2, 2, 64, WIDE),
        fields(2, 1, WIDE),
        fields(9, 128, 128),
        fields(6, 64, 128),
        fields(2, 9, 128, 128),
        fields(2, 6, 128, WIDE),
        fields(2, 64, 128),
        fields(64, 64),
        fields(64, 64),
        fields(1, 64),
        fields(rows, 1, 128),
        fields(rows, 1, 128),
        fields(256, 128),
        fields(128, 128),
        fields(rows, early_size, 128),
        fields(lanes, early_size, 128),
        fields(rows, early_size, 128),
        fields(lanes, late_size, 128),
        fields(rows, late_size, 128),
        fields(lanes, late_size, 128),
        parts(128, 192),
        parts(64, 384),
        parts(64, 192),
        parts(64, 192),
        parts(128, 192),
        parts(64, 384),
        parts(64, 192),
        parts(64, 192),
        parts(2, 64, 192),
        parts(2, 64, 192),
        parts(2, 64, 192),
        parts(2, 64, 192),
        fields(64, 4, cols),
        fields(64, 4, cols),
        pltpu.SemaphoreType.DMA((16,)),
        pltpu.SemaphoreType.DMA((16,)),
        pltpu.SemaphoreType.DMA((16,)),
        pltpu.SemaphoreType.DMA((8, 15)),
        pltpu.SemaphoreType.DMA((8, 15)),
    ]
    in_place = pl.BlockSpec(memory_space=pl.ANY)
    in_vmem = pl.BlockSpec(memory_space=pltpu.VMEM)
    out, grad, early, late = pl.pallas_call(
        functools.partial(block_kernel, (rows, lanes), factor, area, cols),
        out_shape=(
            wide((64, 4, cols)),
            wide((64, 4, cols)),
            wide((rows, early_size, 128)),
            wide((lanes, late_size, 128)),
        ),
        in_specs=[in_place] * 14,
        out_specs=(in_place, in_place, in_vmem, in_vmem),
        scratch_shapes=scratch,
        compiler_params=pltpu.CompilerParams(
            collective_id=0, has_side_effects=True, vmem_limit_bytes=56 * 2**20
        ),
    )(*operands)
    shapes = [operand.shape for operand in operands]
    done = pl.pallas_call(
        format_kernel,
        out_shape=[wide(shape) for shape in shapes],
        in_specs=[in_vmem] * 4,
        out_specs=[in_vmem] * 14,
    )(out, grad, early.reshape(256, 128), late.reshape(128, 128))
    return (
        done[0][None, None],
        done[1][None, None],
        done[2].T,
        done[3].transpose(2, 0, 1),
        done[4],
        done[5][0],
        done[6],
        done[7][0],
        done[8].T,
        done[9],
        done[10][0],
        done[11][None],
        done[12][None],
        done[13],
    )


def solution(mesh):
    field = P("view", "dp", None, "row", None)
    copied = (P(),) * 9
    owned = (P("view", None, None), P("view", None, None), P("view", None))
    return jax.shard_map(
        functools.partial(per_device, mesh.shape["row"], 2 * mesh.shape["dp"]),
        mesh=mesh,
        in_specs=(field, field) + copied + owned,
        out_specs=(field, field) + copied + owned,
        check_vma=False,
    )
```

```python
import functools

import jax
import jax.numpy as jnp
from jax import lax
from jax.experimental import pallas as pl
from jax.experimental.pallas import tpu as pltpu
from jax.sharding import PartitionSpec as P

epsilon = 1e-06
WIDE = 512
f32 = jnp.float32
bf16 = jnp.bfloat16
MESH = pl.DeviceIdType.MESH


def halves(x):
    high = x.astype(bf16)
    return high, (x - high.astype(f32)).astype(bf16)


def left_parts(x):
    high, low = halves(x)
    return jnp.concatenate([high, low, high], axis=0)


def right_parts(x):
    high, low = halves(x)
    return jnp.concatenate([high, high, low], axis=0)


def dot_nn(a, b):
    return lax.dot_general(a, b, (((1,), (0,)), ((), ())), preferred_element_type=f32)


def dot_nt(a, b):
    return lax.dot_general(a, b, (((1,), (1,)), ((), ())), preferred_element_type=f32)


def dot_tn(a, b):
    return lax.dot_general(a, b, (((0,), (0,)), ((), ())), preferred_element_type=f32)


def over_pixels(a, b):
    a_high, a_low = halves(a)
    b_high, b_low = halves(b)
    return dot_nt(
        jnp.concatenate([a_high, a_low, a_high], axis=1),
        jnp.concatenate([b_high, b_high, b_low], axis=1),
    )


def fold(x):
    return x[:, :128] + x[:, 128:256] + x[:, 256:384] + x[:, 384:]


class Link:
    def __init__(self, copy, sends=None, receives=None):
        self.copy, self.sends, self.receives = copy, sends, receives
        if sends is None:
            copy.start()
        else:
            pl.when(sends)(copy.start)

    def wait(self):
        if self.sends is None:
            self.copy.wait()
        else:
            pl.when(self.receives)(self.copy.wait_recv)
            pl.when(self.sends)(self.copy.wait_send)


def normed(x):
    center = x - jnp.mean(x, axis=0, keepdims=True)
    scale = 1.0 / jnp.sqrt(jnp.mean(center * center, axis=0, keepdims=True) + epsilon)
    return center * scale, scale


def normed_back(grad, value, scale):
    return scale * (
        grad
        - jnp.mean(grad, axis=0, keepdims=True)
        - value * jnp.mean(grad * value, axis=0, keepdims=True)
    )


def far_first(count, ring):
    def hops(step):
        near = step % 8 if ring else step // 4
        around = 8 if ring else 4
        return min(near, around - near)

    return sorted(range(1, count), key=lambda step: -hops(step))


def block_kernel(sizes, factor, area, cols, *refs):
    operands, results, refs = refs[:14], refs[14:18], refs[18:]
    out_hbm, grad_hbm, early_ref, late_ref = results
    (
        x_in, c_in, expand_w, taps_w, pool_w, bias_w, squeeze_w, branch_w,
        up_w, down_w, scale_w, query_w, value_w, cross_w,
    ) = refs[:14]
    (
        x_s, c_s, cp_s, n0_s, s0_s, d_s, cv_s, g_s, t_s, n1_s, s1_s, e_s, u_s, h_s,
        hp_s, dh_s, dhp_s, o_s, op_s, dg_s, dr_s, de_s, dcv_s, e_att, att_s, attn_s, atts_s, own_s,
        taps_s, fold_s, tap_acc, y_s, w_s, queryp_s, valuep_s, crossp_s, pool_s, poolg_s,
        early, late, early_1, early_2, early_3, late_1, late_2, late_3,
        expand_f, expand_b, squeeze_f, squeeze_b, up_f, up_b, down_f, down_b,
        query_f, query_b, value_f, value_b,
        out_ref, grad_ref, loads, sends, recvs, group_sends, group_recvs,
    ) = refs[14:]
    rows, lanes = sizes
    row = lax.axis_index("row")
    view = lax.axis_index("view")
    lane = lax.axis_index("dp") * 2 + view
    mine = (3 * view, 1 + view)
    theirs = (3 - 3 * view, 2 - view)
    slots = (view, 1 - view)
    edge = view * (rows - 1)
    other_edge = rows - 1 - edge

    def in_row(step):
        return {"row": lax.rem(row + step, rows)}

    def in_lane(step):
        other = lax.rem(lane + step, lanes)
        return {"dp": other // 2, "view": lax.rem(other, 2)}

    above = in_row(rows - 1)
    below = in_row(1)
    mine_side = in_row((1 - view) * (rows - 1) + view)
    theirs_side = in_row(view * (rows - 1) + 1 - view)
    partner = {"view": 1 - view}

    barrier = pltpu.get_barrier_semaphore()
    for step in far_first(rows, True):
        pl.semaphore_signal(barrier, inc=1, device_id=in_row(step), device_id_type=MESH)
    for step in far_first(lanes, False):
        pl.semaphore_signal(barrier, inc=1, device_id=in_lane(step), device_id_type=MESH)

    local = [
        pltpu.make_async_copy(operands[item], refs[item], loads.at[item]) for item in range(14)
    ]
    for item in (0, 2, 3, 4, 5, 6, 7, 8, 9, 10, 11, 12, 13, 1):
        local[item].start()

    def send(index, source, target, device, *when):
        return Link(
            pltpu.make_async_remote_copy(
                src_ref=source,
                dst_ref=target,
                send_sem=sends.at[index],
                recv_sem=recvs.at[index],
                device_id=device,
                device_id_type=MESH,
            ),
            *when,
        )

    def spread(phase, source, target, device, count):
        return [
            Link(
                pltpu.make_async_remote_copy(
                    src_ref=source(step),
                    dst_ref=target,
                    send_sem=group_sends.at[phase, step - 1],
                    recv_sem=group_recvs.at[phase, step - 1],
                    device_id=device(step),
                    device_id_type=MESH,
                )
            )
            for step in far_first(count, device is in_row)
        ]

    def finish(links):
        for link in links:
            link.wait()

    for h in range(4):
        x_s[h + 1, :, 384:] = jnp.zeros((64, 128), f32)
    local[0].wait()
    for h in (0, 3, 1, 2):
        x_s[h + 1, :, :cols] = x_in[:, h, :]

    pl.semaphore_wait(barrier, rows + lanes - 2)
    halo_up = send(0, x_s.at[1], x_s.at[5], above, row != 0, row != rows - 1)
    halo_down = send(1, x_s.at[4], x_s.at[0], below, row != rows - 1, row != 0)

    def forward_parts(transposed):
        return left_parts(transposed).astype(f32).T.astype(bf16)

    for item in range(2, 14):
        local[item].wait()
    weights_sent = [
        send(2, query_w, queryp_s, partner),
        send(3, value_w, valuep_s, partner),
        send(4, cross_w, crossp_s, partner),
    ]
    expand_f[...] = forward_parts(expand_w[...])

    def expand_row(h):
        value, scale = normed(x_s[h])
        d_s[h] = dot_nn(expand_f[...], right_parts(value))
        return value, scale

    @pl.loop(1, 5)
    def _(h):
        value, scale = expand_row(h)
        n0_s[h] = value
        s0_s[h - 1] = scale

    tap_rows = jnp.concatenate(
        [taps_w[i, j : j + 1, :] for i in range(3) for j in range(3)]
        + [jnp.zeros((7, 128), f32)],
        axis=0,
    )
    tap_columns = tap_rows.T
    for tap in range(9):
        taps_s[tap] = jnp.broadcast_to(tap_columns[:, tap : tap + 1], (128, 128))
    for h in range(4):
        c_s[h, :, 384:] = jnp.zeros((64, 128), f32)
    local[1].wait()
    for h in range(4):
        c_s[h, :, :cols] = c_in[:, h, :]

    cotangent_sent = send(5, c_s.at[pl.ds(2 - 2 * view, 2)], cp_s, partner)

    inside = lax.broadcasted_iota(jnp.int32, (1, WIDE), 1) < cols
    fold_s[...] = jnp.zeros_like(fold_s)

    def tap_at(tap, start, size):
        piece = taps_s[tap, pl.ds(start, size), :]
        return jnp.concatenate([piece] * 4, axis=1)

    def conv_row(h):
        for start in range(0, 128, 16):
            columns = [jnp.zeros((16, WIDE), f32)] * 3
            for i in range(3):
                value = d_s[h + i - 1, start : start + 16, :]
                for j in range(3):
                    columns[j] = columns[j] + tap_at(3 * i + j, start, 16) * value
            total = columns[1] + pltpu.roll(columns[0], 1, 1) + pltpu.roll(columns[2], WIDE - 1, 1)
            cv_s[h, start : start + 16, :] = jnp.where(inside, total, 0.0)
        gate = cv_s[h, :64, :] * cv_s[h, 64:, :]
        g_s[h - 1] = gate
        fold_s[0] += fold(gate)

    pl.loop(2, 4)(conv_row)
    halo_up.wait()
    halo_down.wait()

    @pl.when(row == 0)
    def _():
        x_s[0] = jnp.zeros((64, WIDE), f32)

    @pl.when(row == rows - 1)
    def _():
        x_s[5] = jnp.zeros((64, WIDE), f32)

    for h in (0, 5):
        value, _ = expand_row(h)
        n0_s[h] = value

    conv_row(1)
    conv_row(4)

    eye = lax.broadcasted_iota(jnp.int32, (64, 128), 0) == lax.broadcasted_iota(
        jnp.int32, (64, 128), 1
    )

    def to_column(vector):
        spread_out = jnp.broadcast_to(vector, (64, vector.shape[1]))
        return jnp.sum(
            jnp.where(eye[:, : vector.shape[1]], spread_out, 0.0), axis=1, keepdims=True
        )

    def to_row(column):
        return jnp.sum(
            jnp.where(eye, jnp.broadcast_to(column, (64, 128)), 0.0), axis=0, keepdims=True
        )

    pool_s[row] = to_row(jnp.sum(fold_s[0], axis=1, keepdims=True))
    links = spread(0, lambda step: pool_s.at[row], pool_s.at[row], in_row, rows)
    expand_b[...] = forward_parts(expand_w[...].T)
    up_f[...] = forward_parts(up_w[...])
    up_b[...] = forward_parts(up_w[...].T)
    for weight, forward, backward in (
        (squeeze_w, squeeze_f, squeeze_b),
        (down_w, down_f, down_b),
        (query_w, query_f.at[0], query_b.at[0]),
        (value_w, value_f.at[0], value_b.at[0]),
    ):
        forward[...] = forward_parts(weight[...].T)
        backward[...] = forward_parts(weight[...])
    bias = to_column(bias_w[...])
    branch = to_column(branch_w[...])
    ffn_scale = to_column(scale_w[...])
    cross = to_column(cross_w[...])
    tap_acc[...] = jnp.zeros_like(tap_acc)
    w_s[...] = jnp.zeros_like(w_s)

    def conv_back(part):
        @pl.loop(0, 8)
        def _(chunk):
            size = 16
            start = pl.multiple_of(chunk * size, size)
            for h in range(1, 5):
                center = dcv_s[h, pl.ds(start, size), :]
                moved = [pltpu.roll(center, WIDE - 1, 1), center, pltpu.roll(center, 1, 1)]
                for i in range(3):
                    value = d_s[h + i - 1, pl.ds(start, size), :]
                    for j in range(3):
                        tap_acc[part, 3 * i + j, pl.ds(start, size), :] += fold(moved[j] * value)
            for h in range(6):
                columns = [jnp.zeros((size, WIDE), f32)] * 3
                for i in range(3):
                    if 1 <= h - i + 1 <= 4:
                        value = dcv_s[h - i + 1, pl.ds(start, size), :]
                        for j in range(3):
                            columns[j] = columns[j] + tap_at(3 * i + j, start, size) * value
                y_s[part, h, pl.ds(start, size), :] = (
                    columns[1]
                    + pltpu.roll(columns[2], 1, 1)
                    + pltpu.roll(columns[0], WIDE - 1, 1)
                )

    def expand_products(part):
        @pl.loop(0, 6)
        def _(h):
            w_s[part] += over_pixels(n0_s[h], y_s[part, h])

    @pl.loop(1, 5)
    def _(h):
        dcv_s[h, :64, :] = cv_s[h, 64:, :]
        dcv_s[h, 64:, :] = cv_s[h, :64, :]

    conv_back(0)
    finish(links)

    pooled = jnp.sum(pool_s[...], axis=0) / area
    attention = jnp.sum(pool_w[...] * pooled[:, :64], axis=1, keepdims=True) + bias

    def tail_row(h):
        squeezed = dot_nn(squeeze_f[...], right_parts(g_s[h] * attention))
        t_s[h] = squeezed
        residual = x_s[h + 1] + branch * squeezed
        value, scale = normed(residual)
        n1_s[h] = value
        s1_s[h] = scale
        expanded = dot_nn(up_f[...], right_parts(value))
        e_s[h] = expanded
        shrunk = dot_nn(down_f[...], right_parts(expanded[:64] * expanded[64:]))
        u_s[h] = shrunk
        h_s[h] = residual + ffn_scale * shrunk

    hidden_sent = []
    for k in range(2):
        tail_row(theirs[k])
        hidden_sent.append(send(8 + k, h_s.at[theirs[k]], hp_s.at[k], partner))
    conv_up = send(6, cv_s.at[1], cv_s.at[5], above, row != 0, row != rows - 1)
    conv_down = send(7, cv_s.at[4], cv_s.at[0], below, row != rows - 1, row != 0)
    for k in range(2):
        tail_row(mine[k])
    expand_products(0)

    finish(weights_sent)
    query_f[1] = forward_parts(queryp_s[...].T)
    query_b[1] = forward_parts(queryp_s[...])
    value_f[1] = forward_parts(valuep_s[...].T)
    value_b[1] = forward_parts(valuep_s[...])
    crossp = to_column(crossp_s[...])
    cotangent_sent.wait()

    sixteen = lax.broadcasted_iota(jnp.int32, (16, WIDE), 0)
    outside16 = lax.broadcasted_iota(jnp.int32, (16, WIDE), 1) >= cols
    ones16 = jnp.ones((16, WIDE), bf16)
    mask_left = jnp.where(
        sixteen == 0, jnp.where(outside16, -256.0, 0.0), jnp.where(sixteen == 1, 1.0, 0.0)
    ).astype(bf16)
    mask_right = jnp.where(
        sixteen == 0, 1.0, jnp.where((sixteen == 1) & outside16, -256.0, 0.0)
    ).astype(bf16)

    def own_parts(k):
        own = h_s[mine[k]]
        own_n, own_scale = normed(own)
        attn_s[k, 0] = own_n
        atts_s[k] = own_scale
        own_s[k, 0] = dot_nn(query_f[0], right_parts(own_n))
        own_s[k, 1] = dot_nn(value_f[0], right_parts(own))

    def attend_row(k):
        own, other = h_s[mine[k]], hp_s[k]
        own_up, other_up = c_s[mine[k]], cp_s[slots[k]]
        other_n, other_scale = normed(other)
        attn_s[k, 1] = other_n
        own_q, own_v = own_s[k, 0], own_s[k, 1]
        other_q = dot_nn(query_f[1], right_parts(other_n))
        other_v = dot_nn(value_f[1], right_parts(other))
        scores = dot_tn(
            jnp.concatenate([left_parts(own_q * 0.125), mask_left], axis=0),
            jnp.concatenate([right_parts(other_q), mask_right], axis=0),
        )
        weights = jnp.exp(scores)
        e_att[...] = weights
        w_high, w_low = halves(weights)

        def weighted(dot, values):
            high, low = halves(values)
            large = dot(jnp.concatenate([high, ones16, low], axis=0), w_high)
            small = dot(jnp.concatenate([high, ones16], axis=0), w_low)
            bottom = jnp.where(inside, large[64:65] + small[64:65], 1.0)
            return large[:64] + large[80:] + small[:64], 1.0 / bottom

        def through(dot, values, high_m, low_m):
            high, low = halves(values)
            large = dot(jnp.concatenate([high, low], axis=0), high_m)
            return large[:64] + large[64:] + dot(high, low_m)

        own_c, own_r = weighted(dot_nt, other_v)
        other_c, other_r = weighted(dot_nn, own_v)
        own_c = own_c * own_r
        other_c = other_c * other_r
        own_d = cross * own_up * own_r
        other_d = crossp * other_up * other_r
        own_delta, own_delta_low = halves(-jnp.sum(own_d * own_c, axis=0, keepdims=True))
        other_delta, other_delta_low = halves(-jnp.sum(other_d * other_c, axis=0, keepdims=True))
        left_tail = jnp.where(
            sixteen == 0,
            own_delta.astype(f32),
            jnp.where(
                sixteen == 1, own_delta_low.astype(f32), jnp.where(sixteen < 4, 1.0, 0.0)
            ),
        ).astype(bf16)
        right_tail = jnp.where(
            sixteen == 2,
            other_delta.astype(f32),
            jnp.where(
                sixteen == 3, other_delta_low.astype(f32), jnp.where(sixteen < 2, 1.0, 0.0)
            ),
        ).astype(bf16)
        change = dot_tn(
            jnp.concatenate(
                [left_parts(jnp.concatenate([own_d, own_v], axis=0)), left_tail], axis=0
            ),
            jnp.concatenate(
                [right_parts(jnp.concatenate([other_v, other_d], axis=0)), right_tail], axis=0
            ),
        )
        ds_high, ds_low = halves(e_att[...] * change * 0.125)
        other_dv = through(dot_nn, own_d, w_high, w_low)
        other_dq = through(dot_nn, own_q, ds_high, ds_low)
        dn = dot_nn(query_b[1], right_parts(other_dq))
        dhp_s[k] = (
            other_up
            + dot_nn(value_b[1], right_parts(other_dv))
            + normed_back(dn, other_n, other_scale)
        )
        returned.append(send(10 + k, dhp_s.at[k], dh_s.at[mine[k]], partner))
        o_s[mine[k]] = own + cross * own_c
        op_s[k] = other + crossp * other_c
        fold_s[4] += fold(own_up * own_c)
        fold_s[5] += fold(other_up * other_c)
        att_s[k, 1] = other_dq
        att_s[k, 3] = other_dv
        att_s[k, 2] = through(dot_nt, other_d, w_high, w_low)
        att_s[k, 0] = through(dot_nt, other_q, ds_high, ds_low)

    def own_back(k):
        dn = dot_nn(query_b[0], right_parts(att_s[k, 0]))
        dh_s[mine[k]] = (
            c_s[mine[k]]
            + dot_nn(value_b[0], right_parts(att_s[k, 2]))
            + normed_back(dn, attn_s[k, 0], atts_s[k])
        )

    returned = []
    for k in range(2):
        own_parts(k)
    for k in range(2):
        hidden_sent[k].wait()
        attend_row(k)

    def tail_back_row(h):
        up = dh_s[h]
        expanded = e_s[h]
        dgate = dot_nn(down_b[...], right_parts(ffn_scale * up))
        de = jnp.concatenate([dgate * expanded[64:], dgate * expanded[:64]], axis=0)
        de_s[h] = de
        dn = dot_nn(up_b[...], right_parts(de))
        dr = up + normed_back(dn, n1_s[h], s1_s[h])
        dr_s[h] = dr
        dscaled = dot_nn(squeeze_b[...], right_parts(branch * dr))
        fold_s[3] += fold(dscaled * g_s[h])
        dg_s[h + 1] = dscaled * attention

    own_back(0)
    tail_back_row(mine[0])
    gate_mine = send(
        12, dg_s.at[mine[0] + 1], dg_s.at[5 - 5 * view], mine_side, row != edge, row != other_edge
    )
    own_back(1)
    tail_back_row(mine[1])

    query_grads = [jnp.zeros((64, 64), f32)] * 4
    for k in range(2):
        fields = (attn_s[k, 0], attn_s[k, 1], h_s[mine[k]], hp_s[k])
        for item in range(4):
            query_grads[item] = query_grads[item] + over_pixels(att_s[k, item], fields[item])
    for start, pair in ((128, query_grads[:2]), (192, query_grads[2:])):
        early[start : start + 64, :64] = jnp.where(view == 0, pair[0], pair[1])
        early[start : start + 64, 64:] = jnp.where(view == 0, pair[1], pair[0])

    returned[0].wait()
    tail_back_row(theirs[0])
    gate_theirs = send(
        13, dg_s.at[theirs[0] + 1], dg_s.at[5 * view], theirs_side, row != other_edge, row != edge
    )
    returned[1].wait()
    tail_back_row(theirs[1])

    d_attention = jnp.sum(fold_s[3], axis=1, keepdims=True)
    poolg = jnp.sum(pool_w[...] * d_attention, axis=0, keepdims=True)
    poolg_s[row, :, :64] = poolg
    poolg_s[row, :, 64:] = poolg
    links = spread(1, lambda step: poolg_s.at[row], poolg_s.at[row], in_row, rows)
    out_sent = [send(14 + k, op_s.at[k], o_s.at[mine[k]], partner) for k in range(2)]

    early[:128, :] = jnp.zeros((128, 128), f32)

    @pl.loop(0, 4)
    def _(h):
        up = dh_s[h]
        dr = dr_s[h]
        fold_s[1] += fold(up * u_s[h])
        fold_s[2] += fold(dr * t_s[h])
        expanded = e_s[h]
        early[:64, :] += over_pixels(n1_s[h], de_s[h])
        early[64:128, :64] += over_pixels(branch * dr, g_s[h] * attention)
        early[64:128, 64:] += over_pixels(ffn_scale * up, expanded[:64] * expanded[64:])

    early_size, late_size = 256 // lanes, 128 // lanes

    def chunk_at(index, size):
        return pl.ds(pl.multiple_of(index * size, 8), size)

    early_links = spread(
        2,
        lambda step: early.at[chunk_at(lax.rem(lane + step, lanes), early_size)],
        early_1.at[lane],
        in_lane,
        lanes,
    )
    early_1[lane] = early[chunk_at(lane, early_size), :]

    @pl.loop(1, 5)
    def _(h):
        dcv_s[h, :64, :] = dg_s[h] * cv_s[h, 64:, :]
        dcv_s[h, 64:, :] = dg_s[h] * cv_s[h, :64, :]

    conv_back(1)
    expand_products(1)
    finish(links)

    constants = jnp.sum(poolg_s[...], axis=0) / area
    constant = to_column(constants)
    late[:64, :] = w_s[1] + w_s[0] * constants

    place = lax.broadcasted_iota(jnp.int32, (64, 128), 1)

    def columns_of(value):
        return jnp.sum(value, axis=1, keepdims=True)

    items = [
        columns_of(tap_acc[1, tap, start : start + 64, :])
        + constant * columns_of(tap_acc[0, tap, start : start + 64, :])
        for start in (0, 64)
        for tap in range(9)
    ]
    items += [d_attention, columns_of(fold_s[2]), columns_of(fold_s[1])]
    own_cross = columns_of(fold_s[4])
    other_cross = columns_of(fold_s[5])
    items.append(jnp.where(view == 0, own_cross, other_cross))
    items.append(jnp.where(view == 0, other_cross, own_cross))
    mixed = d_attention * pooled
    for index, item in enumerate(items):
        mixed = jnp.where(place == 64 + index, item, mixed)
    late[64:, :] = mixed

    constant_both = jnp.concatenate([constant, constant], axis=0)
    late_links = spread(
        5,
        lambda step: late.at[chunk_at(lax.rem(lane + step, lanes), late_size)],
        late_1.at[lane],
        in_lane,
        lanes,
    )
    late_1[lane] = late[chunk_at(lane, late_size), :]

    @pl.loop(1, 5)
    def _(h):
        y_s[1, h] += constant_both * y_s[0, h]

    finish(late_links)

    late_2[row] = jnp.sum(late_1[...], axis=0)
    late_links = spread(6, lambda step: late_2.at[row], late_2.at[row], in_row, rows)
    finish(early_links)
    early_2[row] = jnp.sum(early_1[...], axis=0)
    early_links = spread(3, lambda step: early_2.at[row], early_2.at[row], in_row, rows)

    gate_mine.wait()
    gate_theirs.wait()
    conv_up.wait()
    conv_down.wait()
    for outer, limit, target, i in ((0, 0, 1, 2), (5, rows - 1, 4, 0)):

        @pl.when(row != limit)
        def _():
            total = dg_s[outer] + constant
            dcv_s[outer, :64, :] = total * cv_s[outer, 64:, :]
            dcv_s[outer, 64:, :] = total * cv_s[outer, :64, :]
            for start in range(0, 128, 16):
                value = dcv_s[outer, start : start + 16, :]
                columns = [tap_at(3 * i + j, start, 16) * value for j in range(3)]
                y_s[1, target, start : start + 16, :] += (
                    columns[1]
                    + pltpu.roll(columns[2], 1, 1)
                    + pltpu.roll(columns[0], WIDE - 1, 1)
                )

    @pl.loop(0, 4)
    def _(h):
        dn = dot_nn(expand_b[...], right_parts(y_s[1, h + 1]))
        dr_s[h] = dr_s[h] + normed_back(dn, n0_s[h + 1], s0_s[h])

    for h in range(4):
        grad_ref[:, h, :] = dr_s[h, :, :cols]
    stored = [pltpu.make_async_copy(grad_ref, grad_hbm, loads.at[14])]
    stored[0].start()
    finish(late_links)

    late_3[lane] = jnp.sum(late_2[...], axis=0) * factor
    late_links = spread(7, lambda step: late_3.at[lane], late_3.at[lane], in_lane, lanes)
    finish(early_links)
    early_3[lane] = jnp.sum(early_2[...], axis=0) * factor
    early_links = spread(4, lambda step: early_3.at[lane], early_3.at[lane], in_lane, lanes)
    finish(out_sent)
    for h in range(4):
        out_ref[:, h, :] = o_s[h, :, :cols]
    stored.append(pltpu.make_async_copy(out_ref, out_hbm, loads.at[15]))
    stored[1].start()
    finish(early_links)
    early_ref[...] = early_3[...]
    finish(late_links)
    late_ref[...] = late_3[...]
    for copy in stored:
        copy.wait()


def format_kernel(out_in, grad_in, early_ref, late_ref, *refs):
    (
        out_ref, grad_ref, expand_ref, taps_ref, pool_ref, bias_ref, squeeze_ref, branch_ref,
        up_ref, down_ref, scale_ref, query_ref, value_ref, cross_ref,
    ) = refs
    out_ref[...] = out_in[...]
    grad_ref[...] = grad_in[...]
    view = lax.axis_index("view")
    up_ref[...] = early_ref[:64, :]
    middle = early_ref[64:128, :]
    squeeze_ref[...] = middle[:, :64]
    down_ref[...] = middle[:, 64:]
    for start, target in ((128, query_ref), (192, value_ref)):
        both = early_ref[start : start + 64, :]
        target[...] = jnp.where(view == 0, both[:, :64], both[:, 64:])
    expand_ref[...] = late_ref[:64, :]
    mixed = late_ref[64:, :]
    pool_ref[...] = mixed[:, :64]
    turned = mixed.T
    for tap in range(9):
        taps_ref[tap // 3, tap % 3 : tap % 3 + 1, :64] = turned[64 + tap : 65 + tap, :]
        taps_ref[tap // 3, tap % 3 : tap % 3 + 1, 64:] = turned[73 + tap : 74 + tap, :]
    for place, target in ((82, bias_ref), (83, branch_ref), (84, scale_ref)):
        target[...] = turned[place : place + 1, :]
    cross_ref[...] = jnp.where(view == 0, turned[85:86, :], turned[86:87, :])


def per_device(rows, lanes, *arrays):
    cols = arrays[0].shape[4]
    area = 4 * rows * cols
    factor = (lanes * area) ** (-0.5)
    wide = functools.partial(jax.ShapeDtypeStruct, dtype=f32)

    def fields(*shape):
        return pltpu.VMEM(shape, f32)

    def parts(*shape):
        return pltpu.VMEM(shape, bf16)

    operands = [
        arrays[0][0, 0],
        arrays[1][0, 0],
        arrays[2].T,
        arrays[3].transpose(1, 2, 0),
        arrays[4],
        arrays[5][None],
        arrays[6],
        arrays[7][None],
        arrays[8].T,
        arrays[9],
        arrays[10][None],
        arrays[11][0],
        arrays[12][0],
        arrays[13],
    ]
    early_size, late_size = 256 // lanes, 128 // lanes
    scratch = [fields(*operand.shape) for operand in operands] + [
        fields(6, 64, WIDE),
        fields(4, 64, WIDE),
        fields(2, 64, WIDE),
        fields(6, 64, WIDE),
        fields(4, 1, WIDE),
        fields(6, 128, WIDE),
        fields(6, 128, WIDE),
        fields(4, 64, WIDE),
        fields(4, 64, WIDE),
        fields(4, 64, WIDE),
        fields(4, 1, WIDE),
        fields(4, 128, WIDE),
        fields(4, 64, WIDE),
        fields(4, 64, WIDE),
        fields(2, 64, WIDE),
        fields(4, 64, WIDE),
        fields(2, 64, WIDE),
        fields(4, 64, WIDE),
        fields(2, 64, WIDE),
        fields(6, 64, WIDE),
        fields(4, 64, WIDE),
        fields(4, 128, WIDE),
        fields(6, 128, WIDE),
        fields(WIDE, WIDE),
        fields(2, 4, 64, WIDE),
        fields(2, 2, 64, WIDE),
        fields(2, 1, WIDE),
        fields(2, 2, 64, WIDE),
        fields(9, 128, 128),
        fields(6, 64, 128),
        fields(2, 9, 128, 128),
        fields(2, 6, 128, WIDE),
        fields(2, 64, 128),
        fields(64, 64),
        fields(64, 64),
        fields(1, 64),
        fields(rows, 1, 128),
        fields(rows, 1, 128),
        fields(256, 128),
        fields(128, 128),
        fields(lanes, early_size, 128),
        fields(rows, early_size, 128),
        fields(lanes, early_size, 128),
        fields(lanes, late_size, 128),
        fields(rows, late_size, 128),
        fields(lanes, late_size, 128),
        parts(128, 192),
        parts(64, 384),
        parts(64, 192),
        parts(64, 192),
        parts(128, 192),
        parts(64, 384),
        parts(64, 192),
        parts(64, 192),
        parts(2, 64, 192),
        parts(2, 64, 192),
        parts(2, 64, 192),
        parts(2, 64, 192),
        fields(64, 4, cols),
        fields(64, 4, cols),
        pltpu.SemaphoreType.DMA((16,)),
        pltpu.SemaphoreType.DMA((16,)),
        pltpu.SemaphoreType.DMA((16,)),
        pltpu.SemaphoreType.DMA((8, 15)),
        pltpu.SemaphoreType.DMA((8, 15)),
    ]
    in_place = pl.BlockSpec(memory_space=pl.ANY)
    in_vmem = pl.BlockSpec(memory_space=pltpu.VMEM)
    out, grad, early, late = pl.pallas_call(
        functools.partial(block_kernel, (rows, lanes), factor, area, cols),
        out_shape=(
            wide((64, 4, cols)),
            wide((64, 4, cols)),
            wide((lanes, early_size, 128)),
            wide((lanes, late_size, 128)),
        ),
        in_specs=[in_place] * 14,
        out_specs=(in_place, in_place, in_vmem, in_vmem),
        scratch_shapes=scratch,
        compiler_params=pltpu.CompilerParams(
            collective_id=0, has_side_effects=True, vmem_limit_bytes=56 * 2**20
        ),
    )(*operands)
    shapes = [operand.shape for operand in operands]
    done = pl.pallas_call(
        format_kernel,
        out_shape=[wide(shape) for shape in shapes],
        in_specs=[in_vmem] * 4,
        out_specs=[in_vmem] * 14,
    )(out, grad, early.reshape(256, 128), late.reshape(128, 128))
    return (
        done[0][None, None],
        done[1][None, None],
        done[2].T,
        done[3].transpose(2, 0, 1),
        done[4],
        done[5][0],
        done[6],
        done[7][0],
        done[8].T,
        done[9],
        done[10][0],
        done[11][None],
        done[12][None],
        done[13],
    )


def solution(mesh):
    field = P("view", "dp", None, "row", None)
    copied = (P(),) * 9
    owned = (P("view", None, None), P("view", None, None), P("view", None))
    return jax.shard_map(
        functools.partial(per_device, mesh.shape["row"], 2 * mesh.shape["dp"]),
        mesh=mesh,
        in_specs=(field, field) + copied + owned,
        out_specs=(field, field) + copied + owned,
        check_vma=False,
    )
```

```python
import functools

import jax
import jax.numpy as jnp
from jax import lax
from jax.experimental import pallas as pl
from jax.experimental.pallas import tpu as pltpu
from jax.sharding import PartitionSpec as P

epsilon = 1e-06
WIDE = 512
f32 = jnp.float32
bf16 = jnp.bfloat16
MESH = pl.DeviceIdType.MESH


def halves(x):
    high = x.astype(bf16)
    return high, (x - high.astype(f32)).astype(bf16)


def left_parts(x):
    high, low = halves(x)
    return jnp.concatenate([high, low, high], axis=0)


def right_parts(x):
    high, low = halves(x)
    return jnp.concatenate([high, high, low], axis=0)


def dot_nn(a, b):
    return lax.dot_general(a, b, (((1,), (0,)), ((), ())), preferred_element_type=f32)


def dot_nt(a, b):
    return lax.dot_general(a, b, (((1,), (1,)), ((), ())), preferred_element_type=f32)


def dot_tn(a, b):
    return lax.dot_general(a, b, (((0,), (0,)), ((), ())), preferred_element_type=f32)


def over_pixels(a, b):
    a_high, a_low = halves(a)
    b_high, b_low = halves(b)
    return dot_nt(
        jnp.concatenate([a_high, a_low, a_high], axis=1),
        jnp.concatenate([b_high, b_high, b_low], axis=1),
    )


def fold(x):
    return x[:, :128] + x[:, 128:256] + x[:, 256:384] + x[:, 384:]


class Link:
    def __init__(self, copy, sends=None, receives=None):
        self.copy, self.sends, self.receives = copy, sends, receives
        if sends is None:
            copy.start()
        else:
            pl.when(sends)(copy.start)

    def wait(self):
        if self.sends is None:
            self.copy.wait()
        else:
            pl.when(self.receives)(self.copy.wait_recv)
            pl.when(self.sends)(self.copy.wait_send)


def normed(x):
    center = x - jnp.mean(x, axis=0, keepdims=True)
    scale = 1.0 / jnp.sqrt(jnp.mean(center * center, axis=0, keepdims=True) + epsilon)
    return center * scale, scale


def normed_back(grad, value, scale):
    return scale * (
        grad
        - jnp.mean(grad, axis=0, keepdims=True)
        - value * jnp.mean(grad * value, axis=0, keepdims=True)
    )


def far_first(count, ring):
    def hops(step):
        near = step % 8 if ring else step // 4
        around = 8 if ring else 4
        return min(near, around - near)

    return sorted(range(1, count), key=lambda step: -hops(step))


def block_kernel(sizes, factor, area, cols, *refs):
    operands, results, refs = refs[:14], refs[14:18], refs[18:]
    out_hbm, grad_hbm, early_ref, late_ref = results
    (
        x_in, c_in, expand_w, taps_w, pool_w, bias_w, squeeze_w, branch_w,
        up_w, down_w, scale_w, query_w, value_w, cross_w,
    ) = refs[:14]
    (
        x_s, c_s, cp_s, n0_s, s0_s, d_s, cv_s, g_s, t_s, n1_s, s1_s, e_s, u_s, h_s,
        hp_s, dh_s, dhp_s, o_s, op_s, dg_s, dr_s, de_s, dcv_s, e_att, att_s, attn_s, atts_s, own_s,
        taps_s, fold_s, tap_acc, y_s, w_s, queryp_s, valuep_s, crossp_s, pool_s, poolg_s,
        early, late, early_1, early_2, early_3, late_1, late_2, late_3,
        expand_f, expand_b, squeeze_f, squeeze_b, up_f, up_b, down_f, down_b,
        query_f, query_b, value_f, value_b,
        out_ref, grad_ref, loads, sends, recvs, group_sends, group_recvs,
    ) = refs[14:]
    rows, lanes = sizes
    row = lax.axis_index("row")
    view = lax.axis_index("view")
    lane = lax.axis_index("dp") * 2 + view
    mine = (3 * view, 1 + view)
    theirs = (3 - 3 * view, 2 - view)
    slots = (view, 1 - view)
    edge = view * (rows - 1)
    other_edge = rows - 1 - edge

    def in_row(step):
        return {"row": lax.rem(row + step, rows)}

    def in_lane(step):
        other = lax.rem(lane + step, lanes)
        return {"dp": other // 2, "view": lax.rem(other, 2)}

    above = in_row(rows - 1)
    below = in_row(1)
    mine_side = in_row((1 - view) * (rows - 1) + view)
    theirs_side = in_row(view * (rows - 1) + 1 - view)
    partner = {"view": 1 - view}

    barrier = pltpu.get_barrier_semaphore()
    for step in far_first(rows, True):
        pl.semaphore_signal(barrier, inc=1, device_id=in_row(step), device_id_type=MESH)
    for step in far_first(lanes, False):
        pl.semaphore_signal(barrier, inc=1, device_id=in_lane(step), device_id_type=MESH)

    local = [
        pltpu.make_async_copy(operands[item], refs[item], loads.at[item]) for item in range(14)
    ]
    for item in (0, 2, 3, 4, 5, 6, 7, 8, 9, 10, 11, 12, 13, 1):
        local[item].start()

    def send(index, source, target, device, *when):
        return Link(
            pltpu.make_async_remote_copy(
                src_ref=source,
                dst_ref=target,
                send_sem=sends.at[index],
                recv_sem=recvs.at[index],
                device_id=device,
                device_id_type=MESH,
            ),
            *when,
        )

    def spread(phase, source, target, device, count):
        return [
            Link(
                pltpu.make_async_remote_copy(
                    src_ref=source(step),
                    dst_ref=target,
                    send_sem=group_sends.at[phase, step - 1],
                    recv_sem=group_recvs.at[phase, step - 1],
                    device_id=device(step),
                    device_id_type=MESH,
                )
            )
            for step in far_first(count, device is in_row)
        ]

    def finish(links):
        for link in links:
            link.wait()

    for h in range(4):
        x_s[h + 1, :, 384:] = jnp.zeros((64, 128), f32)
    local[0].wait()
    for h in (0, 3, 1, 2):
        x_s[h + 1, :, :cols] = x_in[:, h, :]

    pl.semaphore_wait(barrier, rows + lanes - 2)
    halo_up = send(0, x_s.at[1], x_s.at[5], above, row != 0, row != rows - 1)
    halo_down = send(1, x_s.at[4], x_s.at[0], below, row != rows - 1, row != 0)

    def forward_parts(transposed):
        return left_parts(transposed).astype(f32).T.astype(bf16)

    for item in range(2, 14):
        local[item].wait()
    weights_sent = [
        send(2, query_w, queryp_s, partner),
        send(3, value_w, valuep_s, partner),
        send(4, cross_w, crossp_s, partner),
    ]
    expand_f[...] = forward_parts(expand_w[...])

    def expand_row(h):
        value, scale = normed(x_s[h])
        d_s[h] = dot_nn(expand_f[...], right_parts(value))
        return value, scale

    @pl.loop(1, 5)
    def _(h):
        value, scale = expand_row(h)
        n0_s[h] = value
        s0_s[h - 1] = scale

    tap_rows = jnp.concatenate(
        [taps_w[i, j : j + 1, :] for i in range(3) for j in range(3)]
        + [jnp.zeros((7, 128), f32)],
        axis=0,
    )
    tap_columns = tap_rows.T
    for tap in range(9):
        taps_s[tap] = jnp.broadcast_to(tap_columns[:, tap : tap + 1], (128, 128))
    for h in range(4):
        c_s[h, :, 384:] = jnp.zeros((64, 128), f32)
    local[1].wait()
    for h in range(4):
        c_s[h, :, :cols] = c_in[:, h, :]

    cotangent_sent = send(5, c_s.at[pl.ds(2 - 2 * view, 2)], cp_s, partner)

    inside = lax.broadcasted_iota(jnp.int32, (1, WIDE), 1) < cols
    fold_s[...] = jnp.zeros_like(fold_s)

    def tap_at(tap, start, size):
        piece = taps_s[tap, pl.ds(start, size), :]
        return jnp.concatenate([piece] * 4, axis=1)

    def conv_row(h):
        for start in range(0, 128, 16):
            columns = [jnp.zeros((16, WIDE), f32)] * 3
            for i in range(3):
                value = d_s[h + i - 1, start : start + 16, :]
                for j in range(3):
                    columns[j] = columns[j] + tap_at(3 * i + j, start, 16) * value
            total = columns[1] + pltpu.roll(columns[0], 1, 1) + pltpu.roll(columns[2], WIDE - 1, 1)
            cv_s[h, start : start + 16, :] = jnp.where(inside, total, 0.0)
        gate = cv_s[h, :64, :] * cv_s[h, 64:, :]
        g_s[h - 1] = gate
        fold_s[0] += fold(gate)

    pl.loop(2, 4)(conv_row)
    halo_up.wait()
    halo_down.wait()

    @pl.when(row == 0)
    def _():
        x_s[0] = jnp.zeros((64, WIDE), f32)

    @pl.when(row == rows - 1)
    def _():
        x_s[5] = jnp.zeros((64, WIDE), f32)

    for h in (0, 5):
        value, _ = expand_row(h)
        n0_s[h] = value

    conv_row(1)
    conv_row(4)

    eye = lax.broadcasted_iota(jnp.int32, (64, 128), 0) == lax.broadcasted_iota(
        jnp.int32, (64, 128), 1
    )

    def to_column(vector):
        spread_out = jnp.broadcast_to(vector, (64, vector.shape[1]))
        return jnp.sum(
            jnp.where(eye[:, : vector.shape[1]], spread_out, 0.0), axis=1, keepdims=True
        )

    def to_row(column):
        return jnp.sum(
            jnp.where(eye, jnp.broadcast_to(column, (64, 128)), 0.0), axis=0, keepdims=True
        )

    pool_s[row] = to_row(jnp.sum(fold_s[0], axis=1, keepdims=True))
    links = spread(0, lambda step: pool_s.at[row], pool_s.at[row], in_row, rows)
    expand_b[...] = forward_parts(expand_w[...].T)
    up_f[...] = forward_parts(up_w[...])
    up_b[...] = forward_parts(up_w[...].T)
    for weight, forward, backward in (
        (squeeze_w, squeeze_f, squeeze_b),
        (down_w, down_f, down_b),
        (query_w, query_f.at[0], query_b.at[0]),
        (value_w, value_f.at[0], value_b.at[0]),
    ):
        forward[...] = forward_parts(weight[...].T)
        backward[...] = forward_parts(weight[...])
    bias = to_column(bias_w[...])
    branch = to_column(branch_w[...])
    ffn_scale = to_column(scale_w[...])
    cross = to_column(cross_w[...])
    tap_acc[...] = jnp.zeros_like(tap_acc)
    w_s[...] = jnp.zeros_like(w_s)

    def conv_back(part):
        @pl.loop(0, 8)
        def _(chunk):
            size = 16
            start = pl.multiple_of(chunk * size, size)
            for h in range(1, 5):
                center = dcv_s[h, pl.ds(start, size), :]
                moved = [pltpu.roll(center, WIDE - 1, 1), center, pltpu.roll(center, 1, 1)]
                for i in range(3):
                    value = d_s[h + i - 1, pl.ds(start, size), :]
                    for j in range(3):
                        tap_acc[part, 3 * i + j, pl.ds(start, size), :] += fold(moved[j] * value)
            for h in range(6):
                columns = [jnp.zeros((size, WIDE), f32)] * 3
                for i in range(3):
                    if 1 <= h - i + 1 <= 4:
                        value = dcv_s[h - i + 1, pl.ds(start, size), :]
                        for j in range(3):
                            columns[j] = columns[j] + tap_at(3 * i + j, start, size) * value
                y_s[part, h, pl.ds(start, size), :] = (
                    columns[1]
                    + pltpu.roll(columns[2], 1, 1)
                    + pltpu.roll(columns[0], WIDE - 1, 1)
                )

    def expand_products(part):
        @pl.loop(0, 6)
        def _(h):
            w_s[part] += over_pixels(n0_s[h], y_s[part, h])

    @pl.loop(1, 5)
    def _(h):
        dcv_s[h, :64, :] = cv_s[h, 64:, :]
        dcv_s[h, 64:, :] = cv_s[h, :64, :]

    conv_back(0)
    finish(links)

    pooled = jnp.sum(pool_s[...], axis=0) / area
    attention = jnp.sum(pool_w[...] * pooled[:, :64], axis=1, keepdims=True) + bias

    def tail_row(h):
        squeezed = dot_nn(squeeze_f[...], right_parts(g_s[h] * attention))
        t_s[h] = squeezed
        residual = x_s[h + 1] + branch * squeezed
        value, scale = normed(residual)
        n1_s[h] = value
        s1_s[h] = scale
        expanded = dot_nn(up_f[...], right_parts(value))
        e_s[h] = expanded
        shrunk = dot_nn(down_f[...], right_parts(expanded[:64] * expanded[64:]))
        u_s[h] = shrunk
        h_s[h] = residual + ffn_scale * shrunk

    hidden_sent = []
    for k in range(2):
        tail_row(theirs[k])
        hidden_sent.append(send(8 + k, h_s.at[theirs[k]], hp_s.at[k], partner))
    conv_up = send(6, cv_s.at[1], cv_s.at[5], above, row != 0, row != rows - 1)
    conv_down = send(7, cv_s.at[4], cv_s.at[0], below, row != rows - 1, row != 0)
    for k in range(2):
        tail_row(mine[k])
    expand_products(0)

    finish(weights_sent)
    query_f[1] = forward_parts(queryp_s[...].T)
    query_b[1] = forward_parts(queryp_s[...])
    value_f[1] = forward_parts(valuep_s[...].T)
    value_b[1] = forward_parts(valuep_s[...])
    crossp = to_column(crossp_s[...])
    cotangent_sent.wait()

    sixteen = lax.broadcasted_iota(jnp.int32, (16, WIDE), 0)
    outside16 = lax.broadcasted_iota(jnp.int32, (16, WIDE), 1) >= cols
    ones16 = jnp.ones((16, WIDE), bf16)
    mask_left = jnp.where(
        sixteen == 0, jnp.where(outside16, -256.0, 0.0), jnp.where(sixteen == 1, 1.0, 0.0)
    ).astype(bf16)
    mask_right = jnp.where(
        sixteen == 0, 1.0, jnp.where((sixteen == 1) & outside16, -256.0, 0.0)
    ).astype(bf16)

    def own_parts(k):
        own = h_s[mine[k]]
        own_n, own_scale = normed(own)
        attn_s[k, 0] = own_n
        atts_s[k] = own_scale
        own_s[k, 0] = dot_nn(query_f[0], right_parts(own_n))
        own_s[k, 1] = dot_nn(value_f[0], right_parts(own))

    def attend_row(k):
        own, other = h_s[mine[k]], hp_s[k]
        own_up, other_up = c_s[mine[k]], cp_s[slots[k]]
        other_n, other_scale = normed(other)
        attn_s[k, 1] = other_n
        own_q, own_v = own_s[k, 0], own_s[k, 1]
        other_q = dot_nn(query_f[1], right_parts(other_n))
        other_v = dot_nn(value_f[1], right_parts(other))
        scores = dot_tn(
            jnp.concatenate([left_parts(own_q * 0.125), mask_left], axis=0),
            jnp.concatenate([right_parts(other_q), mask_right], axis=0),
        )
        weights = jnp.exp(scores)
        e_att[...] = weights
        w_high, w_low = halves(weights)

        def weighted(dot, values):
            high, low = halves(values)
            large = dot(jnp.concatenate([high, ones16, low], axis=0), w_high)
            small = dot(jnp.concatenate([high, ones16], axis=0), w_low)
            bottom = jnp.where(inside, large[64:65] + small[64:65], 1.0)
            return large[:64] + large[80:] + small[:64], 1.0 / bottom

        def through(dot, values, high_m, low_m):
            high, low = halves(values)
            large = dot(jnp.concatenate([high, low], axis=0), high_m)
            return large[:64] + large[64:] + dot(high, low_m)

        own_c, own_r = weighted(dot_nt, other_v)
        other_c, other_r = weighted(dot_nn, own_v)
        own_c = own_c * own_r
        other_c = other_c * other_r
        own_d = cross * own_up * own_r
        other_d = crossp * other_up * other_r
        own_delta, own_delta_low = halves(-jnp.sum(own_d * own_c, axis=0, keepdims=True))
        other_delta, other_delta_low = halves(-jnp.sum(other_d * other_c, axis=0, keepdims=True))
        left_tail = jnp.where(
            sixteen == 0,
            own_delta.astype(f32),
            jnp.where(
                sixteen == 1, own_delta_low.astype(f32), jnp.where(sixteen < 4, 1.0, 0.0)
            ),
        ).astype(bf16)
        right_tail = jnp.where(
            sixteen == 2,
            other_delta.astype(f32),
            jnp.where(
                sixteen == 3, other_delta_low.astype(f32), jnp.where(sixteen < 2, 1.0, 0.0)
            ),
        ).astype(bf16)
        change = dot_tn(
            jnp.concatenate(
                [left_parts(jnp.concatenate([own_d, own_v], axis=0)), left_tail], axis=0
            ),
            jnp.concatenate(
                [right_parts(jnp.concatenate([other_v, other_d], axis=0)), right_tail], axis=0
            ),
        )
        ds_high, ds_low = halves(e_att[...] * change * 0.125)
        other_dv = through(dot_nn, own_d, w_high, w_low)
        other_dq = through(dot_nn, own_q, ds_high, ds_low)
        dn = dot_nn(query_b[1], right_parts(other_dq))
        dhp_s[k] = (
            other_up
            + dot_nn(value_b[1], right_parts(other_dv))
            + normed_back(dn, other_n, other_scale)
        )
        returned.append(send(10 + k, dhp_s.at[k], dh_s.at[mine[k]], partner))
        o_s[mine[k]] = own + cross * own_c
        op_s[k] = other + crossp * other_c
        fold_s[4] += fold(own_up * own_c)
        fold_s[5] += fold(other_up * other_c)
        att_s[k, 1] = other_dq
        att_s[k, 3] = other_dv
        att_s[k, 2] = through(dot_nt, other_d, w_high, w_low)
        att_s[k, 0] = through(dot_nt, other_q, ds_high, ds_low)

    def own_back(k):
        dn = dot_nn(query_b[0], right_parts(att_s[k, 0]))
        dh_s[mine[k]] = (
            c_s[mine[k]]
            + dot_nn(value_b[0], right_parts(att_s[k, 2]))
            + normed_back(dn, attn_s[k, 0], atts_s[k])
        )

    returned = []
    for k in range(2):
        own_parts(k)
    for k in range(2):
        hidden_sent[k].wait()
        attend_row(k)

    def tail_back_row(h):
        up = dh_s[h]
        expanded = e_s[h]
        dgate = dot_nn(down_b[...], right_parts(ffn_scale * up))
        de = jnp.concatenate([dgate * expanded[64:], dgate * expanded[:64]], axis=0)
        de_s[h] = de
        dn = dot_nn(up_b[...], right_parts(de))
        dr = up + normed_back(dn, n1_s[h], s1_s[h])
        dr_s[h] = dr
        dscaled = dot_nn(squeeze_b[...], right_parts(branch * dr))
        fold_s[3] += fold(dscaled * g_s[h])
        dg_s[h + 1] = dscaled * attention

    own_back(0)
    tail_back_row(mine[0])
    gate_mine = send(
        12, dg_s.at[mine[0] + 1], dg_s.at[5 - 5 * view], mine_side, row != edge, row != other_edge
    )
    own_back(1)
    tail_back_row(mine[1])

    query_grads = [jnp.zeros((64, 64), f32)] * 4
    for k in range(2):
        fields = (attn_s[k, 0], attn_s[k, 1], h_s[mine[k]], hp_s[k])
        for item in range(4):
            query_grads[item] = query_grads[item] + over_pixels(att_s[k, item], fields[item])
    for start, pair in ((128, query_grads[:2]), (192, query_grads[2:])):
        early[start : start + 64, :64] = jnp.where(view == 0, pair[0], pair[1])
        early[start : start + 64, 64:] = jnp.where(view == 0, pair[1], pair[0])

    returned[0].wait()
    tail_back_row(theirs[0])
    gate_theirs = send(
        13, dg_s.at[theirs[0] + 1], dg_s.at[5 * view], theirs_side, row != other_edge, row != edge
    )
    returned[1].wait()
    tail_back_row(theirs[1])

    d_attention = jnp.sum(fold_s[3], axis=1, keepdims=True)
    poolg = jnp.sum(pool_w[...] * d_attention, axis=0, keepdims=True)
    poolg_s[row, :, :64] = poolg
    poolg_s[row, :, 64:] = poolg
    links = spread(1, lambda step: poolg_s.at[row], poolg_s.at[row], in_row, rows)

    early[:128, :] = jnp.zeros((128, 128), f32)

    @pl.loop(0, 4)
    def _(h):
        up = dh_s[h]
        dr = dr_s[h]
        fold_s[1] += fold(up * u_s[h])
        fold_s[2] += fold(dr * t_s[h])
        expanded = e_s[h]
        early[:64, :] += over_pixels(n1_s[h], de_s[h])
        early[64:128, :64] += over_pixels(branch * dr, g_s[h] * attention)
        early[64:128, 64:] += over_pixels(ffn_scale * up, expanded[:64] * expanded[64:])

    early_size, late_size = 256 // lanes, 128 // lanes

    def chunk_at(index, size):
        return pl.ds(pl.multiple_of(index * size, 8), size)

    early_links = spread(
        2,
        lambda step: early.at[chunk_at(lax.rem(lane + step, lanes), early_size)],
        early_1.at[lane],
        in_lane,
        lanes,
    )
    early_1[lane] = early[chunk_at(lane, early_size), :]

    @pl.loop(1, 5)
    def _(h):
        dcv_s[h, :64, :] = dg_s[h] * cv_s[h, 64:, :]
        dcv_s[h, 64:, :] = dg_s[h] * cv_s[h, :64, :]

    conv_back(1)
    expand_products(1)
    finish(links)

    constants = jnp.sum(poolg_s[...], axis=0) / area
    constant = to_column(constants)
    late[:64, :] = w_s[1] + w_s[0] * constants

    place = lax.broadcasted_iota(jnp.int32, (64, 128), 1)

    def columns_of(value):
        return jnp.sum(value, axis=1, keepdims=True)

    items = [
        columns_of(tap_acc[1, tap, start : start + 64, :])
        + constant * columns_of(tap_acc[0, tap, start : start + 64, :])
        for start in (0, 64)
        for tap in range(9)
    ]
    items += [d_attention, columns_of(fold_s[2]), columns_of(fold_s[1])]
    own_cross = columns_of(fold_s[4])
    other_cross = columns_of(fold_s[5])
    items.append(jnp.where(view == 0, own_cross, other_cross))
    items.append(jnp.where(view == 0, other_cross, own_cross))
    mixed = d_attention * pooled
    for index, item in enumerate(items):
        mixed = jnp.where(place == 64 + index, item, mixed)
    late[64:, :] = mixed

    constant_both = jnp.concatenate([constant, constant], axis=0)
    late_links = spread(
        5,
        lambda step: late.at[chunk_at(lax.rem(lane + step, lanes), late_size)],
        late_1.at[lane],
        in_lane,
        lanes,
    )
    out_sent = [send(14 + k, op_s.at[k], o_s.at[mine[k]], partner) for k in range(2)]
    late_1[lane] = late[chunk_at(lane, late_size), :]

    @pl.loop(1, 5)
    def _(h):
        y_s[1, h] += constant_both * y_s[0, h]

    finish(late_links)

    late_2[row] = jnp.sum(late_1[...], axis=0)
    late_links = spread(6, lambda step: late_2.at[row], late_2.at[row], in_row, rows)
    finish(early_links)
    early_2[row] = jnp.sum(early_1[...], axis=0)
    early_links = spread(3, lambda step: early_2.at[row], early_2.at[row], in_row, rows)

    gate_mine.wait()
    gate_theirs.wait()
    conv_up.wait()
    conv_down.wait()
    for outer, limit, target, i in ((0, 0, 1, 2), (5, rows - 1, 4, 0)):

        @pl.when(row != limit)
        def _():
            total = dg_s[outer] + constant
            dcv_s[outer, :64, :] = total * cv_s[outer, 64:, :]
            dcv_s[outer, 64:, :] = total * cv_s[outer, :64, :]
            for start in range(0, 128, 16):
                value = dcv_s[outer, start : start + 16, :]
                columns = [tap_at(3 * i + j, start, 16) * value for j in range(3)]
                y_s[1, target, start : start + 16, :] += (
                    columns[1]
                    + pltpu.roll(columns[2], 1, 1)
                    + pltpu.roll(columns[0], WIDE - 1, 1)
                )

    @pl.loop(0, 4)
    def _(h):
        dn = dot_nn(expand_b[...], right_parts(y_s[1, h + 1]))
        dr_s[h] = dr_s[h] + normed_back(dn, n0_s[h + 1], s0_s[h])

    for h in range(4):
        grad_ref[:, h, :] = dr_s[h, :, :cols]
    stored = [pltpu.make_async_copy(grad_ref, grad_hbm, loads.at[14])]
    stored[0].start()
    finish(late_links)

    late_3[lane] = jnp.sum(late_2[...], axis=0) * factor
    late_links = spread(7, lambda step: late_3.at[lane], late_3.at[lane], in_lane, lanes)
    finish(early_links)
    early_3[lane] = jnp.sum(early_2[...], axis=0) * factor
    early_links = spread(4, lambda step: early_3.at[lane], early_3.at[lane], in_lane, lanes)
    finish(out_sent)
    for h in range(4):
        out_ref[:, h, :] = o_s[h, :, :cols]
    stored.append(pltpu.make_async_copy(out_ref, out_hbm, loads.at[15]))
    stored[1].start()
    finish(early_links)
    early_ref[...] = early_3[...]
    finish(late_links)
    late_ref[...] = late_3[...]
    for copy in stored:
        copy.wait()


def format_kernel(out_in, grad_in, early_ref, late_ref, *refs):
    (
        out_ref, grad_ref, expand_ref, taps_ref, pool_ref, bias_ref, squeeze_ref, branch_ref,
        up_ref, down_ref, scale_ref, query_ref, value_ref, cross_ref,
    ) = refs
    out_ref[...] = out_in[...]
    grad_ref[...] = grad_in[...]
    view = lax.axis_index("view")
    up_ref[...] = early_ref[:64, :]
    middle = early_ref[64:128, :]
    squeeze_ref[...] = middle[:, :64]
    down_ref[...] = middle[:, 64:]
    for start, target in ((128, query_ref), (192, value_ref)):
        both = early_ref[start : start + 64, :]
        target[...] = jnp.where(view == 0, both[:, :64], both[:, 64:])
    expand_ref[...] = late_ref[:64, :]
    mixed = late_ref[64:, :]
    pool_ref[...] = mixed[:, :64]
    turned = mixed.T
    for tap in range(9):
        taps_ref[tap // 3, tap % 3 : tap % 3 + 1, :64] = turned[64 + tap : 65 + tap, :]
        taps_ref[tap // 3, tap % 3 : tap % 3 + 1, 64:] = turned[73 + tap : 74 + tap, :]
    for place, target in ((82, bias_ref), (83, branch_ref), (84, scale_ref)):
        target[...] = turned[place : place + 1, :]
    cross_ref[...] = jnp.where(view == 0, turned[85:86, :], turned[86:87, :])


def per_device(rows, lanes, *arrays):
    cols = arrays[0].shape[4]
    area = 4 * rows * cols
    factor = (lanes * area) ** (-0.5)
    wide = functools.partial(jax.ShapeDtypeStruct, dtype=f32)

    def fields(*shape):
        return pltpu.VMEM(shape, f32)

    def parts(*shape):
        return pltpu.VMEM(shape, bf16)

    operands = [
        arrays[0][0, 0],
        arrays[1][0, 0],
        arrays[2].T,
        arrays[3].transpose(1, 2, 0),
        arrays[4],
        arrays[5][None],
        arrays[6],
        arrays[7][None],
        arrays[8].T,
        arrays[9],
        arrays[10][None],
        arrays[11][0],
        arrays[12][0],
        arrays[13],
    ]
    early_size, late_size = 256 // lanes, 128 // lanes
    scratch = [fields(*operand.shape) for operand in operands] + [
        fields(6, 64, WIDE),
        fields(4, 64, WIDE),
        fields(2, 64, WIDE),
        fields(6, 64, WIDE),
        fields(4, 1, WIDE),
        fields(6, 128, WIDE),
        fields(6, 128, WIDE),
        fields(4, 64, WIDE),
        fields(4, 64, WIDE),
        fields(4, 64, WIDE),
        fields(4, 1, WIDE),
        fields(4, 128, WIDE),
        fields(4, 64, WIDE),
        fields(4, 64, WIDE),
        fields(2, 64, WIDE),
        fields(4, 64, WIDE),
        fields(2, 64, WIDE),
        fields(4, 64, WIDE),
        fields(2, 64, WIDE),
        fields(6, 64, WIDE),
        fields(4, 64, WIDE),
        fields(4, 128, WIDE),
        fields(6, 128, WIDE),
        fields(WIDE, WIDE),
        fields(2, 4, 64, WIDE),
        fields(2, 2, 64, WIDE),
        fields(2, 1, WIDE),
        fields(2, 2, 64, WIDE),
        fields(9, 128, 128),
        fields(6, 64, 128),
        fields(2, 9, 128, 128),
        fields(2, 6, 128, WIDE),
        fields(2, 64, 128),
        fields(64, 64),
        fields(64, 64),
        fields(1, 64),
        fields(rows, 1, 128),
        fields(rows, 1, 128),
        fields(256, 128),
        fields(128, 128),
        fields(lanes, early_size, 128),
        fields(rows, early_size, 128),
        fields(lanes, early_size, 128),
        fields(lanes, late_size, 128),
        fields(rows, late_size, 128),
        fields(lanes, late_size, 128),
        parts(128, 192),
        parts(64, 384),
        parts(64, 192),
        parts(64, 192),
        parts(128, 192),
        parts(64, 384),
        parts(64, 192),
        parts(64, 192),
        parts(2, 64, 192),
        parts(2, 64, 192),
        parts(2, 64, 192),
        parts(2, 64, 192),
        fields(64, 4, cols),
        fields(64, 4, cols),
        pltpu.SemaphoreType.DMA((16,)),
        pltpu.SemaphoreType.DMA((16,)),
        pltpu.SemaphoreType.DMA((16,)),
        pltpu.SemaphoreType.DMA((8, 15)),
        pltpu.SemaphoreType.DMA((8, 15)),
    ]
    in_place = pl.BlockSpec(memory_space=pl.ANY)
    in_vmem = pl.BlockSpec(memory_space=pltpu.VMEM)
    out, grad, early, late = pl.pallas_call(
        functools.partial(block_kernel, (rows, lanes), factor, area, cols),
        out_shape=(
            wide((64, 4, cols)),
            wide((64, 4, cols)),
            wide((lanes, early_size, 128)),
            wide((lanes, late_size, 128)),
        ),
        in_specs=[in_place] * 14,
        out_specs=(in_place, in_place, in_vmem, in_vmem),
        scratch_shapes=scratch,
        compiler_params=pltpu.CompilerParams(
            collective_id=0, has_side_effects=True, vmem_limit_bytes=56 * 2**20
        ),
    )(*operands)
    shapes = [operand.shape for operand in operands]
    done = pl.pallas_call(
        format_kernel,
        out_shape=[wide(shape) for shape in shapes],
        in_specs=[in_vmem] * 4,
        out_specs=[in_vmem] * 14,
    )(out, grad, early.reshape(256, 128), late.reshape(128, 128))
    return (
        done[0][None, None],
        done[1][None, None],
        done[2].T,
        done[3].transpose(2, 0, 1),
        done[4],
        done[5][0],
        done[6],
        done[7][0],
        done[8].T,
        done[9],
        done[10][0],
        done[11][None],
        done[12][None],
        done[13],
    )


def solution(mesh):
    field = P("view", "dp", None, "row", None)
    copied = (P(),) * 9
    owned = (P("view", None, None), P("view", None, None), P("view", None))
    return jax.shard_map(
        functools.partial(per_device, mesh.shape["row"], 2 * mesh.shape["dp"]),
        mesh=mesh,
        in_specs=(field, field) + copied + owned,
        out_specs=(field, field) + copied + owned,
        check_vma=False,
    )
```
